128 devices in a mesh: blk: 32 (over x, z_hi, y), sub: 4 (over z_lo, core).
Axes of the slice: x: 4, y: 4, z: 4 (z_hi: 2, z_lo: 2; z = z_hi * 2 + z_lo), core: 2. Of those that a mesh axis runs over, the one named last changes fastest.
Arguments:
- fluid_temp: float32 [1024, 128, 512], P('blk', 'sub'), may hold values from -6 to 6
- velocity: float32 [3, 1024, 128, 512], P(None, 'blk', 'sub'), may hold values from -6 to 6
- eddy_diff: float32 [1024, 128, 512], P('blk', 'sub'), may hold values from 0.05 to 0.5
- wall_prev: float32 [131072], P(('blk', 'sub')), may hold values from -6 to 6
- row_count: int32 [128], P(('blk', 'sub')), may hold values from 256 to 1024, as said below
- owner_table: int32 [128, 128], P(('blk', 'sub')), may hold values from 0 to 4, as said below
- landing_cell: int32 [128, 1536], P(('blk', 'sub')), may hold values from 0 to 1023
- solid_temp: float32 [1024, 128, 256], P('blk', 'sub'), may hold values from -6 to 6
- conductivity: float32 [1024, 128, 256], P('blk', 'sub'), may hold values from 0.2 to 5
- sink: float32 [1024, 128, 256], P('blk', 'sub'), may hold values from 0.2 to 2
- heat_source: float32 [1024, 128, 256], P('blk', 'sub'), may hold values from -6 to 6
Outputs:
- fluid_new: float32 [1024, 128, 512], P('blk', 'sub')
- solid_new: float32 [1024, 128, 256], P('blk', 'sub')
- wall_new: float32 [131072], P(('blk', 'sub'))
The draws below stay inside these ranges and needn't reach their ends.
Inputs may be any that keep to these rules, and one draw needn't show every extreme that they name: `row_count`: live rows of a fluid block; some block has all 1024 live in every draw. `owner_table`: no group points outside the grid of blocks; at least half of a block's groups are 0; at most 16 groups of a block have any one direction from 1 to 4, and some solid block receives exactly that many from every neighbour it has.
All inputs are finite; a program needn't handle non-finite values.
Results may differ from the reference program's by a relative error of at most 0.0003.
Values sent between devices are 32-bit elements; how exact they have to be, the bound alone decides.
A program may use at most 128 MiB of HBM per device.

```python
import math
import jax
import jax.numpy as jnp
from jax import lax

FX = 32
FY = 32
FZ = 512
SX = 32
SY = 32
SZ = 256
CAP = 8
FLUID_SWEEPS = 2
SWEEPS = 8
OWNERS = 128
ROWS = 1024
GROUPS = 128
NEAR_GROUPS = 16
NEAR_ROWS = 128
INCOMING = 1536
TOTAL_ROWS = 131072
SURF = 1024
NX = 1024
NY = 128
NSX = 1024
NSY = 128
N_BLK = 32
N_SUB = 4


def draw_row_count(key, part):
    first_key = jax.random.fold_in(key, 11)
    second_key = jax.random.fold_in(key, 23)
    counts = jax.random.randint(first_key, (OWNERS,), ROWS // 4, ROWS + 1)
    fullest = jax.random.randint(second_key, (), 0, OWNERS)
    return jnp.where(jnp.arange(OWNERS) == fullest, ROWS, counts).astype(jnp.int32)


def draw_owner_table(key, part):
    count_key = jax.random.fold_in(key, 31)
    pick_key = jax.random.fold_in(key, 37)
    shuffle_key = jax.random.fold_in(key, 41)
    owner_ids = jnp.arange(OWNERS, dtype=jnp.int32)
    blk_of = owner_ids // N_SUB
    sub_of = owner_ids % N_SUB
    blk_total = OWNERS // N_SUB
    valid_dir = jnp.stack([blk_of + 1 < blk_total, blk_of > 0, sub_of + 1 < N_SUB, sub_of > 0], axis=1)
    offsets = jnp.array([N_SUB, -N_SUB, 1, -1], dtype=jnp.int32)
    target = owner_ids[:, None] + offsets[None, :]
    chosen = jax.random.randint(pick_key, (), 0, OWNERS)
    counts = jax.random.randint(count_key, (OWNERS, 4), 0, NEAR_GROUPS + 1)
    counts = jnp.where(target == chosen, NEAR_GROUPS, counts) * valid_dir.astype(jnp.int32)
    upper_end = jnp.cumsum(counts, axis=1)
    lower_end = upper_end - counts
    positions = jnp.arange(GROUPS, dtype=jnp.int32)
    inside = (positions[None, None, :] >= lower_end[:, :, None]) & (positions[None, None, :] < upper_end[:, :, None])
    dir_codes = jnp.sum(inside.astype(jnp.int32) * jnp.arange(1, 5, dtype=jnp.int32)[None, :, None], axis=1)
    owner_keys = jax.random.split(shuffle_key, OWNERS)
    orders = jax.vmap(lambda sub_key: jax.random.permutation(sub_key, GROUPS))(owner_keys)
    return jnp.take_along_axis(dir_codes, orders, axis=1).astype(jnp.int32)


def draw_landing_cell(key, part):
    row_index = jnp.arange(ROWS, dtype=jnp.int32)
    base_x = row_index // FY * SX // FX
    base_y = row_index % FY * SY // FY
    jitter_x = jax.random.randint(jax.random.fold_in(key, 51), (OWNERS, ROWS), -1, 2)
    jitter_y = jax.random.randint(jax.random.fold_in(key, 53), (OWNERS, ROWS), -1, 2)
    self_x = jnp.clip(base_x[None, :] + jitter_x, 0, SX - 1)
    self_y = jnp.clip(base_y[None, :] + jitter_y, 0, SY - 1)
    pieces = [self_x * SY + self_y]
    for band_no in range(4):
        depth = jax.random.randint(jax.random.fold_in(key, 61 + band_no), (OWNERS, NEAR_ROWS), 0, 2)
        along_x = jax.random.randint(jax.random.fold_in(key, 71 + band_no), (OWNERS, NEAR_ROWS), 0, SX)
        along_y = jax.random.randint(jax.random.fold_in(key, 81 + band_no), (OWNERS, NEAR_ROWS), 0, SY)
        if band_no == 0:
            pieces.append(depth * SY + along_y)
        elif band_no == 1:
            pieces.append((SX - 1 - depth) * SY + along_y)
        elif band_no == 2:
            pieces.append(along_x * SY + depth)
        else:
            pieces.append(along_x * SY + SY - 1 - depth)
    cells = jnp.concatenate(pieces, axis=1)
    cells = cells.at[0, ROWS].set(0).at[0, INCOMING - 1].set(SURF - 1)
    return cells.astype(jnp.int32)


def block_levels(key, dims, cuts, least, top_value):
    loudness = 1.0
    for position, blocks in cuts:
        steps = jax.random.uniform(jax.random.fold_in(jax.random.fold_in(key, 6), position), (blocks,), jnp.float32, least / len(cuts), top_value / len(cuts))
        loudness = loudness * jnp.repeat(jnp.exp(steps), dims[position] // blocks).reshape((-1,) + (1,) * (len(dims) - 1 - position))
    return loudness


def normal_values(stream_key, dims, width, limit, cuts=(), kind=jnp.bfloat16):
    values = width * jax.random.normal(stream_key, dims, jnp.float32)
    if cuts:
        values = values * block_levels(stream_key, dims, cuts, -0.22, 0.18)
    return jnp.clip(values, -limit, limit).astype(kind)


def setup_inputs(seed: int = 0) -> dict:
    keys = jax.random.split(jax.random.key(seed), 12)
    fluid_temp = normal_values(keys[0], (NX, NY, FZ), 1.0, 6.0, ((0, 32), (1, 4)), jnp.float32)
    velocity = normal_values(keys[1], (3, NX, NY, FZ), 1.0, 6.0, ((1, 32), (2, 4)), jnp.float32)
    eddy_diff = jnp.clip(jnp.exp(math.log(0.5) - 2.3025851 * jax.random.uniform(keys[2], (NX, NY, FZ), jnp.float32) ** block_levels(keys[2], (NX, NY, FZ), ((0, 32), (1, 4)), -0.2, 0.2)), 0.05, 0.5)
    wall_prev = normal_values(keys[3], (TOTAL_ROWS,), 1.0, 6.0, ((0, 128),), jnp.float32)
    row_count = draw_row_count(jax.random.fold_in(keys[11], 71), 0)
    owner_table = draw_owner_table(jax.random.fold_in(keys[11], 71), 0)
    landing_cell = draw_landing_cell(jax.random.fold_in(keys[11], 71), 0)
    solid_temp = normal_values(keys[7], (NSX, NSY, SZ), 1.0, 6.0, ((0, 32), (1, 4)), jnp.float32)
    conductivity = jnp.clip(jnp.exp(math.log(5.0) - 3.218876 * jax.random.uniform(keys[8], (NSX, NSY, SZ), jnp.float32) ** block_levels(keys[8], (NSX, NSY, SZ), ((0, 32), (1, 4)), -0.2, 0.2)), 0.2, 5.0)
    sink = jnp.clip(jnp.exp(math.log(2.0) - 2.3025851 * jax.random.uniform(keys[9], (NSX, NSY, SZ), jnp.float32) ** block_levels(keys[9], (NSX, NSY, SZ), ((0, 32), (1, 4)), -0.2, 0.2)), 0.2, 2.0)
    heat_source = normal_values(keys[10], (NSX, NSY, SZ), 1.0, 6.0, ((0, 32), (1, 4)), jnp.float32)
    return dict(fluid_temp=fluid_temp, velocity=velocity, eddy_diff=eddy_diff, wall_prev=wall_prev, row_count=row_count, owner_table=owner_table, landing_cell=landing_cell, solid_temp=solid_temp, conductivity=conductivity, sink=sink, heat_source=heat_source)


RELAX_FACTOR = 0.8
EIG_LOW = 0.02
EIG_HIGH = 2.0


def face_slice(values_in, axis_no, start):
    slicer = [slice(1, -1)] * 3
    slicer[axis_no] = slice(start, values_in.shape[axis_no] - 1 + start)
    return values_in[tuple(slicer)]


def fluid_update(temp_pad, velo_pad, alpha_pad):
    center_val = temp_pad[1:-1, 1:-1, 1:-1]
    residue = jnp.zeros_like(center_val)
    weight = jnp.zeros_like(center_val)
    for axis_no in range(3):
        lower_val = face_slice(temp_pad, axis_no, 0)
        upper_val = face_slice(temp_pad, axis_no, 1)
        face_speed = 0.5 * (face_slice(velo_pad[axis_no], axis_no, 0) + face_slice(velo_pad[axis_no], axis_no, 1))
        face_diff = 0.5 * (face_slice(alpha_pad, axis_no, 0) + face_slice(alpha_pad, axis_no, 1))
        face_flux = jnp.maximum(face_speed, 0.0) * lower_val + jnp.minimum(face_speed, 0.0) * upper_val - face_diff * (upper_val - lower_val)
        count_faces = face_flux.shape[axis_no]
        residue = residue - (lax.slice_in_dim(face_flux, 1, count_faces, axis=axis_no) - lax.slice_in_dim(face_flux, 0, count_faces - 1, axis=axis_no))
        face_weight = face_diff + 0.5 * jnp.abs(face_speed)
        weight = weight + lax.slice_in_dim(face_weight, 1, count_faces, axis=axis_no) + lax.slice_in_dim(face_weight, 0, count_faces - 1, axis=axis_no)
    return center_val + RELAX_FACTOR * residue / weight


def wall_pad(temp_rim, wall_temp, live_plane):
    wall_cell = temp_rim[1:-1, 1:-1, 0]
    ghost_val = jnp.pad(wall_cell + live_plane * 2.0 * (wall_temp - wall_cell), 1)
    return jnp.concatenate([ghost_val[:, :, None], temp_rim, jnp.zeros_like(ghost_val)[:, :, None]], axis=2)


def edge_pad(values_in):
    return jnp.pad(values_in, ((0, 0), (0, 0), (1, 1)), mode="edge")


def flow_pad(flow_rim):
    normal_speed = flow_rim[2]
    normal_pad = jnp.concatenate([-normal_speed[:, :, :1], normal_speed, normal_speed[:, :, -1:]], axis=2)
    velo_pad = jnp.stack([edge_pad(flow_rim[0]), edge_pad(flow_rim[1]), normal_pad])
    return velo_pad, edge_pad(flow_rim[3])


def conduct(state_pad, cond_pad, diag_extra, rhs_field):
    center_val = state_pad[1:-1, 1:-1]
    center_cond = cond_pad[1:-1, 1:-1]
    state_z = jnp.pad(center_val, ((0, 0), (0, 0), (1, 1)))
    cond_z = jnp.pad(center_cond, ((0, 0), (0, 0), (1, 1)))
    neighbours = [(state_pad[2:, 1:-1], cond_pad[2:, 1:-1]), (state_pad[:-2, 1:-1], cond_pad[:-2, 1:-1]),
                  (state_pad[1:-1, 2:], cond_pad[1:-1, 2:]), (state_pad[1:-1, :-2], cond_pad[1:-1, :-2]),
                  (state_z[:, :, 2:], cond_z[:, :, 2:]), (state_z[:, :, :-2], cond_z[:, :, :-2])]
    applied = diag_extra * center_val
    diag_sum = diag_extra
    for near_val, near_cond in neighbours:
        summed = center_cond + near_cond
        conduct_face = 2.0 * center_cond * near_cond / jnp.where(summed > 0.0, summed, 1.0)
        applied = applied + conduct_face * (center_val - near_val)
        diag_sum = diag_sum + conduct_face
    return (rhs_field - applied) / jnp.where(diag_sum > 0.0, diag_sum, 1.0)


def cheby_coefficients(count_sweeps):
    center_eig = 0.5 * (EIG_HIGH + EIG_LOW)
    half_width = 0.5 * (EIG_HIGH - EIG_LOW)
    ratio_eig = center_eig / half_width
    damping = 1.0 / ratio_eig
    coefficients = [(0.0, 1.0 / center_eig)]
    for sweep_no in range(1, count_sweeps):
        damping_new = 1.0 / (2.0 * ratio_eig - damping)
        coefficients.append((damping_new * damping, 2.0 * damping_new / half_width))
        damping = damping_new
    return coefficients


def pick_groups_all(group_dirs, dir_code):
    matched = group_dirs == dir_code
    group_rank = jnp.cumsum(matched.astype(jnp.int32), axis=1) - 1
    slot_ids = jnp.arange(NEAR_GROUPS, dtype=jnp.int32)
    return (matched[:, :, None] & (group_rank[:, :, None] == slot_ids[None, None, :])).astype(jnp.float32)


def reference(fluid_temp, velocity, eddy_diff, wall_prev, row_count, owner_table, landing_cell, solid_temp, conductivity, sink, heat_source):
    owner_total = N_BLK * N_SUB
    row_total = FX * FY
    live_rows = (jnp.arange(row_total, dtype=jnp.int32)[None, :] < row_count[:, None]).astype(jnp.float32)

    def to_plane(values_in):
        return values_in.reshape(N_BLK, N_SUB, FX, FY).transpose(0, 2, 1, 3).reshape(N_BLK * FX, N_SUB * FY)

    def from_plane(field):
        return field.reshape(N_BLK, FX, N_SUB, FY).transpose(0, 2, 1, 3).reshape(owner_total, row_total)

    wall_temp = to_plane(wall_prev.reshape(owner_total, row_total))
    live_plane = to_plane(live_rows)
    flow_stack = jnp.concatenate([velocity, eddy_diff[None]], axis=0)
    velo_pad, alpha_pad = flow_pad(jnp.pad(flow_stack, ((0, 0), (1, 1), (1, 1), (0, 0))))
    fluid_now = fluid_temp
    for sweep_no in range(FLUID_SWEEPS):
        fluid_now = fluid_update(wall_pad(jnp.pad(fluid_now, ((1, 1), (1, 1), (0, 0))), wall_temp, live_plane), velo_pad, alpha_pad)
    gas_temp = from_plane(fluid_now[:, :, 0])
    film_coeff = 2.0 * from_plane(eddy_diff[:, :, 0]) * live_rows
    dir_rows = jnp.repeat(owner_table, CAP, axis=1)
    self_mask = (dir_rows == 0).astype(jnp.float32)
    row_pair = jnp.stack([film_coeff, gas_temp], axis=1).reshape(owner_total, 2, GROUPS, CAP)
    owner_ids = jnp.arange(owner_total, dtype=jnp.int32)
    blk_of = owner_ids // N_SUB
    sub_of = owner_ids % N_SUB
    offsets = (N_SUB, -N_SUB, 1, -1)
    target_ok = (blk_of + 1 < N_BLK, blk_of > 0, sub_of + 1 < N_SUB, sub_of > 0)
    source_ok = (blk_of > 0, blk_of + 1 < N_BLK, sub_of > 0, sub_of + 1 < N_SUB)
    selections = []
    arrived = []
    for dir_index in range(4):
        selection = pick_groups_all(owner_table, dir_index + 1)
        selections.append(selection)
        outbound = jnp.einsum("ocgk,ogs->ocsk", row_pair, selection, precision=lax.Precision.HIGHEST).reshape(owner_total, 2, NEAR_ROWS)
        source = jnp.clip(owner_ids - offsets[dir_index], 0, owner_total - 1).astype(jnp.int32)
        arrived.append(jnp.where(source_ok[dir_index][:, None, None], outbound[source], 0.0))
    film_in = jnp.concatenate([film_coeff * self_mask] + [piece[:, 0] for piece in arrived], axis=1)
    gas_in = jnp.concatenate([gas_temp] + [piece[:, 1] for piece in arrived], axis=1)
    segment = (owner_ids[:, None] * SURF + landing_cell).reshape(-1).astype(jnp.int32)
    film_sum = jax.ops.segment_sum(film_in.reshape(-1), segment, num_segments=owner_total * SURF)
    film_gas = jax.ops.segment_sum((film_in * gas_in).reshape(-1), segment, num_segments=owner_total * SURF)

    def to_solid(values_in):
        return values_in.reshape(N_BLK, N_SUB, SX, SY).transpose(0, 2, 1, 3).reshape(N_BLK * SX, N_SUB * SY)

    surface_mask = (jnp.arange(SZ, dtype=jnp.int32) == 0).astype(jnp.float32)
    diag_extra = sink + to_solid(film_sum)[:, :, None] * surface_mask
    rhs_field = heat_source + to_solid(film_gas)[:, :, None] * surface_mask
    cond_pad = jnp.pad(conductivity, ((1, 1), (1, 1), (0, 0)))
    solid_now = solid_temp
    update = jnp.zeros_like(solid_temp)
    for decay, gain_term in cheby_coefficients(SWEEPS):
        scaled_res = conduct(jnp.pad(solid_now, ((1, 1), (1, 1), (0, 0))), cond_pad, diag_extra, rhs_field)
        update = decay * update + gain_term * scaled_res
        solid_now = solid_now + update
    surface = solid_now[:, :, 0].reshape(N_BLK, SX, N_SUB, SY).transpose(0, 2, 1, 3).reshape(owner_total, SURF)
    slot_values = surface[owner_ids[:, None], landing_cell]
    wall_sum = self_mask * slot_values[:, :row_total]
    for dir_index in range(4):
        band_start = row_total + dir_index * NEAR_ROWS
        band = slot_values[:, band_start:band_start + NEAR_ROWS]
        target = jnp.clip(owner_ids + offsets[dir_index], 0, owner_total - 1).astype(jnp.int32)
        returned = jnp.where(target_ok[dir_index][:, None], band[target], 0.0)
        spread = jnp.einsum("osk,ogs->ogk", returned.reshape(owner_total, NEAR_GROUPS, CAP), selections[dir_index], precision=lax.Precision.HIGHEST)
        wall_sum = wall_sum + spread.reshape(owner_total, row_total)
    wall_new = (wall_sum * live_rows).reshape(-1)
    return fluid_now, solid_now, wall_new
```

```python
import functools

import jax
import jax.numpy as jnp
from jax import lax
from jax.experimental import pallas as pl
from jax.experimental.pallas import tpu as pltpu
from jax.sharding import PartitionSpec as P

MESH = pl.DeviceIdType.MESH
SWEEPS = 8
HALO = 8
DEEP = 16
EIG_LOW = 0.02
EIG_HIGH = 2.0
HIGHEST = lax.Precision.HIGHEST
DIRS = ((1, 0), (-1, 0), (0, 1), (0, -1), (1, 1), (1, -1), (-1, 1), (-1, -1))


def cheby_coefficients(count_sweeps):
    center_eig = 0.5 * (EIG_HIGH + EIG_LOW)
    half_width = 0.5 * (EIG_HIGH - EIG_LOW)
    ratio_eig = center_eig / half_width
    damping = 1.0 / ratio_eig
    coefficients = [(0.0, 1.0 / center_eig)]
    for _ in range(1, count_sweeps):
        damping_new = 1.0 / (2.0 * ratio_eig - damping)
        coefficients.append((damping_new * damping, 2.0 * damping_new / half_width))
        damping = damping_new
    return coefficients


def iota(shape, dim):
    return lax.broadcasted_iota(jnp.int32, shape, dim)


def shift_rows(v, low, high):
    n = v.shape[0]
    row = iota(v.shape, 0)
    below = jnp.where(row == 0, low, pltpu.roll(v, 1, axis=0))
    above = jnp.where(row == n - 1, high, pltpu.roll(v, n - 1, axis=0))
    return below, above


def roll_lanes(v):
    n = v.shape[1]
    return pltpu.roll(v, 1, axis=1), pltpu.roll(v, n - 1, axis=1)


def face(u, un, a, an):
    total_u, total_a = u + un, a + an
    return total_a + jnp.maximum(total_u, 0.0), total_a - jnp.minimum(total_u, 0.0)


def conductance(k, kn):
    total = k + kn
    return 2.0 * k * kn / jnp.where(total > 0.0, total, 1.0)


def kernel(
    n_blk, n_sub,
    count_ref, t_hbm, vel_hbm, a_hbm, x_hbm, k_hbm, e_hbm, q_hbm, wall_ref, owner_ref, land_ref,
    t_out, x_out, wedge_out, wall_out,
    t0, t1, t2, ux, uy, uz, al, cf, sf,
    hxf, hyf, ysf, hxt, hyt, yst,
    xa, xb, kc, ec, qc, cs, pc, hxs, hys, yss, hxk, hyk, ysk,
    nb, fb, wk, wcf, wxa, wxb, wp, wd,
    rows_s, rows_r, wall_s, wall_r, hot_x, hot_y, slots,
    load_sem, send_sem, recv_sem,
):
    b, s = lax.axis_index("blk"), lax.axis_index("sub")
    nx, ny, nz = t0.shape
    nsz = xa.shape[2]
    coefficients = cheby_coefficients(SWEEPS)

    def inside(db, ds):
        ok = None
        for delta, at, count in ((db, b, n_blk), (ds, s, n_sub)):
            if delta:
                this = (at < count - 1) if delta > 0 else (at > 0)
                ok = this if ok is None else ok & this
        return ok

    counter = [0]
    pending = []

    class Message:
        def __init__(self, src, dst, d):
            db, ds = DIRS[d]
            self.n = counter[0]
            counter[0] += 1
            self.make = lambda: pltpu.make_async_remote_copy(
                src_ref=src, dst_ref=dst, send_sem=send_sem.at[self.n], recv_sem=recv_sem.at[self.n],
                device_id=(b + db, s + ds), device_id_type=MESH)
            self.goes, self.comes = inside(db, ds), inside(-db, -ds)

        def start(self):
            @pl.when(self.goes)
            def _():
                self.make().start()
            pending.append(self)

        def sent(self):
            @pl.when(self.goes)
            def _():
                self.make().wait_send()
            pending.remove(self)

        def arrived(self):
            @pl.when(self.comes)
            def _():
                self.make().wait_recv()

    loads = {}
    for n, (name, src, dst) in enumerate((
        ("k", k_hbm, kc), ("x", x_hbm, xa), ("e", e_hbm, ec), ("q", q_hbm, qc),
        ("a", a_hbm, al), ("uy", vel_hbm.at[1], uy), ("t", t_hbm, t0), ("ux", vel_hbm.at[0], ux), ("uz", vel_hbm.at[2], uz),
    )):
        loads[name] = pltpu.make_async_copy(src, dst, load_sem.at[n])
        loads[name].start()

    barrier = pltpu.get_barrier_semaphore()
    for db, ds in DIRS:
        @pl.when(inside(db, ds))
        def _(db=db, ds=ds):
            pl.semaphore_signal(barrier, inc=1, device_id=(b + db, s + ds), device_id_type=MESH)

    for d in range(2):
        @pl.when(jnp.logical_not(inside(-DIRS[d][0], 0)))
        def _(d=d):
            for ref in (hxf.at[d], hxt.at[d], hxk.at[d]):
                ref[...] = jnp.zeros(ref.shape, jnp.float32)
            for n in range(SWEEPS - 1):
                hxs[n, d] = jnp.zeros(hxs.shape[2:], jnp.float32)

        @pl.when(jnp.logical_not(inside(0, -DIRS[2 + d][1])))
        def _(d=d):
            for ref in (hyf.at[d], hyt.at[d], hyk.at[d]):
                ref[...] = jnp.zeros(ref.shape, jnp.float32)
            for n in range(SWEEPS - 1):
                hys[n, d] = jnp.zeros(hys.shape[2:], jnp.float32)
    for d in range(4):
        @pl.when(jnp.logical_not(inside(-DIRS[d][0], -DIRS[d][1])))
        def _(d=d):
            rows_r[d] = jnp.zeros(rows_r.shape[1:], jnp.float32)
            wall_r[d] = jnp.zeros(wall_r.shape[1:], jnp.float32)

    def near_slot(d):
        db, ds = DIRS[d]
        column = {1: 0, 0: 1, -1: 2}[ds]
        if db == 0:
            return column, slice(HALO, HALO + nx), slice(HALO, HALO + nx)
        if db > 0:
            return column, slice(nx, HALO + nx), slice(0, HALO)
        return column, slice(HALO, 2 * HALO), slice(HALO + nx, 2 * HALO + nx)

    for d in range(8):
        @pl.when(jnp.logical_not(inside(-DIRS[d][0], -DIRS[d][1])))
        def _(d=d):
            column, _, rows = near_slot(d)
            height = rows.stop - rows.start
            nb[column, :, rows, :] = jnp.zeros((DEEP, height, 128), jnp.float32)
            fb[column, rows, :] = jnp.zeros((height, 128), jnp.float32)

    near = (b > 0).astype(jnp.int32) + (b < n_blk - 1).astype(jnp.int32)
    side = (s > 0).astype(jnp.int32) + (s < n_sub - 1).astype(jnp.int32)
    pl.semaphore_wait(barrier, near + side + near * side)

    edge = (nx - 1, 0)
    solid_x = [[Message(k_hbm.at[edge[d]], hxk.at[d, 0], d), Message(x_hbm.at[edge[d]], hxk.at[d, 1], d)] for d in range(2)]
    for pair in solid_x:
        for m in pair:
            m.start()
    fluid_x = [[Message(a_hbm.at[edge[d]], hxf.at[d, 0], d), Message(vel_hbm.at[0, edge[d]], hxf.at[d, 1], d),
                Message(t_hbm.at[edge[d]], hxf.at[d, 2], d)] for d in range(2)]
    for trio in fluid_x:
        for m in trio:
            m.start()

    def pack(refs, dst):
        def body(x, _):
            for f, ref in enumerate(refs):
                dst[0, f, pl.ds(x, 1), :] = ref[x, ny - 1:ny, :]
                dst[1, f, pl.ds(x, 1), :] = ref[x, 0:1, :]
            return 0
        lax.fori_loop(0, nx, body, 0)

    loads["k"].wait()
    loads["x"].wait()
    pack((kc, xa), ysk)
    solid_y = [Message(ysk.at[d], hyk.at[d], 2 + d) for d in range(2)]
    for m in solid_y:
        m.start()
    loads["a"].wait()
    loads["uy"].wait()
    loads["t"].wait()
    pack((al, uy, t0), ysf)
    fluid_y = [Message(ysf.at[d], hyf.at[d], 2 + d) for d in range(2)]
    for m in fluid_y:
        m.start()

    loads["e"].wait()
    loads["q"].wait()

    def turn(x, _):
        tile = jnp.concatenate([ref[x, :, 0:128] for ref in (xa, kc, ec, qc)], axis=0)
        nb[1, :, pl.ds(HALO + x, 1), :] = jnp.transpose(tile)[0:DEEP].reshape(DEEP, 1, 128)
        return 0

    lax.fori_loop(0, nx, turn, 0)
    near_msgs = []
    for d in range(8):
        column, out_rows, rows = near_slot(d)
        near_msgs.append(Message(nb.at[1, :, out_rows, :], nb.at[column, :, rows, :], d))
        near_msgs[-1].start()

    lane_s = iota((ny, nsz), 1)

    def solid_coef(x, km, kp):
        k = kc[x]
        ym, yp = shift_rows(k, hyk[0, 0, pl.ds(x, 1), :], hyk[1, 0, pl.ds(x, 1), :])
        zm, zp = roll_lanes(k)
        zm, zp = jnp.where(lane_s == 0, 0.0, zm), jnp.where(lane_s == nsz - 1, 0.0, zp)
        g = [conductance(k, kn) for kn in (km, kp, ym, yp, zm, zp)]
        inverse = 1.0 / (((g[0] + g[1]) + (g[2] + g[3])) + ((g[4] + g[5]) + ec[x]))
        for n in range(6):
            cs[n, x] = g[n] * inverse
        cs[6, x] = qc[x] * inverse

    def solid_plane(n, src, dst, x, xm, xp, low, high):
        decay, gain = coefficients[n]
        v = src[x]
        ym, yp = shift_rows(v, low, high)
        zm, zp = roll_lanes(v)
        r = (cs[6, x] - v) + cs[0, x] * xm + cs[1, x] * xp + cs[2, x] * ym + cs[3, x] * yp + cs[4, x] * zm + cs[5, x] * zp
        p = gain * r if n == 0 else decay * pc[x] + gain * r
        if n < SWEEPS - 1:
            pc[x] = p
        new = v + p
        dst[x] = new
        if n < SWEEPS - 1:
            yss[n, 0, pl.ds(x, 1), :] = new[ny - 1:ny, :]
            yss[n, 1, pl.ds(x, 1), :] = new[0:1, :]

    solid_msgs = {}

    def solid_sweep(n):
        src, dst = (xa, xb) if n % 2 == 0 else (xb, xa)
        if n == 0:
            low, high = hyk.at[0, 1], hyk.at[1, 1]
            xlow, xhigh = hxk.at[0, 1], hxk.at[1, 1]
        else:
            low, high = hys.at[n - 1, 0], hys.at[n - 1, 1]
            xlow, xhigh = hxs.at[n - 1, 0], hxs.at[n - 1, 1]
            for m in solid_msgs[n - 1]:
                m.arrived()
        if n >= 2:
            for m in solid_msgs[n - 2][:2]:
                m.sent()

        def plane(x, xm, xp):
            solid_plane(n, src, dst, x, xm, xp, low[pl.ds(x, 1), :], high[pl.ds(x, 1), :])

        plane(0, xlow[...], src[1])
        plane(nx - 1, src[nx - 2], xhigh[...])
        if n < SWEEPS - 1:
            msgs = [Message(dst.at[edge[d]], hxs.at[n, d], d) for d in range(2)]
            for m in msgs:
                m.start()

        def body(x, _):
            plane(x, src[x - 1], src[x + 1])
            return 0
        lax.fori_loop(1, nx - 1, body, 0)
        if n < SWEEPS - 1:
            more = [Message(yss.at[n, d], hys.at[n, d], 2 + d) for d in range(2)]
            for m in more:
                m.start()
            solid_msgs[n] = msgs + more

    for m in solid_y:
        m.arrived()

    def body(x, _):
        solid_coef(x, kc[x - 1], kc[x + 1])
        return 0
    lax.fori_loop(1, nx - 1, body, 0)
    for pair in solid_x:
        for m in pair:
            m.arrived()
    solid_coef(0, hxk[0, 0], kc[1])
    solid_coef(nx - 1, kc[nx - 2], hxk[1, 0])
    solid_sweep(0)

    lane8, sub8 = iota((8, 128), 1), iota((8, 128), 0)
    live = jnp.where(lane8 * 8 + sub8 < count_ref[0], 1.0, 0.0)
    owner = jnp.broadcast_to(owner_ref[...], (8, 128))
    self_mask = jnp.where(owner == 0, 1.0, 0.0)
    match = jnp.where((owner == sub8 + 1) & (sub8 < 4), 1.0, 0.0)
    before = jnp.where(iota((128, 128), 0) < iota((128, 128), 1), 1.0, 0.0)
    rank = lax.dot_general(match, before, (((1,), (0,)), ((), ())), precision=HIGHEST, preferred_element_type=jnp.float32)
    place = jnp.sum(match * (rank + (sub8 * 16 + 1).astype(jnp.float32)), axis=0, keepdims=True) - 1.0
    select = jnp.where(iota((128, 128), 0).astype(jnp.float32) == place, 1.0, 0.0)
    row32 = iota((32, 256), 0)
    for n in range(8):
        cell = land_ref[n:n + 1, :]
        hot_x[:, 256 * n:256 * n + 256] = jnp.where((cell >> 5) == row32, 1.0, 0.0)
        hot_y[:, 256 * n:256 * n + 256] = jnp.where(((cell & 31) == row32) & (cell >= 0), 1.0, 0.0)

    lane_f = iota((ny, nz), 1)
    lane_t = iota((ny, 128), 1)
    mirror = 1.0 - 2.0 * live
    source = 2.0 * live * wall_ref[...]

    def columns(v, x):
        return jnp.concatenate([pltpu.roll(v, lax.rem(128 - (x * 4 + j), 128), axis=1) for j in range(4)], axis=0)

    def rows_of(v, x, into):
        for j in range(4):
            into = jnp.where(lane8 == x * 4 + j, jnp.broadcast_to(v[8 * j:8 * j + 8, 0:1], (8, 128)), into)
        return into

    def fluid_coef(x, am, ap, um, up, film):
        a, u = al[x], ux[x]
        p_xm, q_xm = face(u, um, a, am)
        p_xp, q_xp = face(u, up, a, ap)
        ym, yp = shift_rows(a, hyf[0, 0, pl.ds(x, 1), :], hyf[1, 0, pl.ds(x, 1), :])
        u = uy[x]
        vm, vp = shift_rows(u, hyf[0, 1, pl.ds(x, 1), :], hyf[1, 1, pl.ds(x, 1), :])
        p_ym, q_ym = face(u, vm, a, ym)
        p_yp, q_yp = face(u, vp, a, yp)
        zm, zp = roll_lanes(a)
        u = uz[x]
        vm, vp = roll_lanes(u)
        low, high = lane_f == 0, lane_f == nz - 1
        p_zm, q_zm = face(u, jnp.where(low, -u, vm), a, jnp.where(low, a, zm))
        p_zp, q_zp = face(u, jnp.where(high, u, vp), a, jnp.where(high, a, zp))
        away = ((q_xm + p_xp) + (q_ym + p_yp)) + (q_zm + p_zp)
        toward = ((p_xm + q_xp) + (p_ym + q_yp)) + (p_zm + q_zp)
        scale = 1.6 / (away + toward)
        cf[0, x] = p_xm * scale
        cf[1, x] = q_xp * scale
        cf[2, x] = p_ym * scale
        cf[3, x] = q_yp * scale
        below = p_zm * scale
        cf[4, x] = jnp.where(low, 0.0, below)
        cf[5, x] = jnp.where(high, 0.0, q_zp * scale)
        centre = 1.0 - away * scale
        first = lane_t == 0
        wall = jnp.where(first, below[:, 0:128], 0.0)
        sf[x] = wall * columns(source, x)
        cf[6, x] = centre
        cf[6, x, :, 0:128] = centre[:, 0:128] + wall * columns(mirror, x)
        return rows_of(a, x, film)

    def fluid_plane(src, dst, x, tm, tp, low, high):
        t = src[x]
        ym, yp = shift_rows(t, low, high)
        zm, zp = roll_lanes(t)
        new = cf[6, x] * t + cf[0, x] * tm + cf[1, x] * tp + cf[2, x] * ym + cf[3, x] * yp + cf[4, x] * zm + cf[5, x] * zp
        first = new[:, 0:128] + sf[x]
        new = jnp.concatenate([first, new[:, 128:]], axis=1) if nz > 128 else first
        dst[x] = new
        return new

    for name in ("ux", "uz"):
        loads[name].wait()
    for m in fluid_y:
        m.arrived()

    def body(x, film):
        return fluid_coef(x, al[x - 1], al[x + 1], ux[x - 1], ux[x + 1], film)
    film = lax.fori_loop(1, nx - 1, body, jnp.zeros((8, 128), jnp.float32))
    for trio in fluid_x:
        for m in trio:
            m.arrived()
    film = fluid_coef(0, hxf[0, 0], al[1], hxf[0, 1], ux[1], film)
    film = fluid_coef(nx - 1, al[nx - 2], hxf[1, 0], ux[nx - 2], hxf[1, 1], film)
    film = 2.0 * film * live

    def first_plane(x, tm, tp):
        new = fluid_plane(t0, t1, x, tm, tp, hyf[0, 2, pl.ds(x, 1), :], hyf[1, 2, pl.ds(x, 1), :])
        for d, at in ((0, ny - 1), (1, 0)):
            yst[d, pl.ds(x, 1), :] = new[at:at + 1, :]

    first_plane(0, hxf[0, 2], t0[1])
    first_plane(nx - 1, t0[nx - 2], hxf[1, 2])
    t_msgs = [Message(t1.at[edge[d]], hxt.at[d], d) for d in range(2)]
    for m in t_msgs:
        m.start()

    def body(x, _):
        first_plane(x, t0[x - 1], t0[x + 1])
        return 0
    lax.fori_loop(1, nx - 1, body, 0)
    more = [Message(yst.at[d], hyt.at[d], 2 + d) for d in range(2)]
    for m in more:
        m.start()
    t_msgs += more

    solid_sweep(1)

    for m in t_msgs:
        m.arrived()

    def second_plane(x, tm, tp, gas):
        new = fluid_plane(t1, t2, x, tm, tp, hyt[0, pl.ds(x, 1), :], hyt[1, pl.ds(x, 1), :])
        return rows_of(new[:, 0:128], x, gas)

    gas = second_plane(0, hxt[0], t1[1], jnp.zeros((8, 128), jnp.float32))
    gas = second_plane(nx - 1, t1[nx - 2], hxt[1], gas)
    gas = lax.fori_loop(1, nx - 1, lambda x, g: second_plane(x, t1[x - 1], t1[x + 1], g), gas)
    t_store = pltpu.make_async_copy(t2, t_out, load_sem.at[9])
    t_store.start()

    def take(v):
        return lax.dot_general(v, select, (((1,), (1,)), ((), ())), precision=HIGHEST, preferred_element_type=jnp.float32)

    rows_s[...] = take(jnp.concatenate([film, gas], axis=0))
    row_msgs = [Message(rows_s, rows_r.at[d], d) for d in range(4)]
    for m in row_msgs:
        m.start()

    solid_sweep(2)

    for m in near_msgs:
        m.arrived()
    lane_w = iota((nx + 2 * HALO, 128), 1)

    def widen(left, mid, right, f):
        left = pltpu.roll(left, (128 - 32 * f - 24) % 128, axis=1)
        mid = pltpu.roll(mid, (128 + HALO - 32 * f) % 128, axis=1)
        right = pltpu.roll(right, (128 + 40 - 32 * f) % 128, axis=1)
        return jnp.where(lane_w < HALO, left, jnp.where(lane_w < HALO + ny, mid, jnp.where(lane_w < 2 * HALO + ny, right, 0.0)))

    def near_field(z, f):
        return widen(nb[0, z], nb[1, z], nb[2, z], f)

    def body(z, _):
        wk[z] = near_field(z, 1)
        wxa[z] = near_field(z, 0)
        return 0
    lax.fori_loop(0, DEEP, body, 0)

    def shift_all(v):
        n = v.shape[0]
        return [pltpu.roll(v, 1, axis=0), pltpu.roll(v, n - 1, axis=0), pltpu.roll(v, 1, axis=1), pltpu.roll(v, 127, axis=1)]

    def body(z, _):
        k = wk[z]
        under = wk[jnp.maximum(z - 1, 0)] * (z > 0).astype(jnp.float32)
        over = wk[jnp.minimum(z + 1, DEEP - 1)] * (z < DEEP - 1).astype(jnp.float32)
        g = [conductance(k, kn) for kn in shift_all(k) + [under, over]]
        diag = ((g[0] + g[1]) + (g[2] + g[3])) + ((g[4] + g[5]) + near_field(z, 2))
        diag = jnp.where(diag > 0.0, diag, 1.0)
        inverse = 1.0 / diag
        for n in range(6):
            wcf[n, z] = g[n] * inverse
        wcf[6, z] = near_field(z, 3) * inverse

        @pl.when(z == 0)
        def _():
            wd[...] = diag
        return 0
    lax.fori_loop(0, DEEP, body, 0)

    for m in row_msgs:
        m.arrived()

    def bands(refs):
        total = None
        for band, ref in enumerate(refs):
            v = ref[...]
            lane = iota(v.shape, 1)
            v = jnp.where((lane >= 16 * band) & (lane < 16 * band + 16), v, 0.0)
            total = v if total is None else total + v
        return total

    came = bands([rows_r.at[d] for d in range(4)])
    film_in = jnp.concatenate([film * self_mask, came[0:8]], axis=1)
    heat_in = film_in * jnp.concatenate([gas, came[8:16]], axis=1)
    weighed = jnp.concatenate(
        [jnp.concatenate([hot_y[:, 256 * n:256 * n + 256] * v[n:n + 1, :] for n in range(8)], axis=1) for v in (film_in, heat_in)]
        + [jnp.zeros((64, 2048), jnp.float32)], axis=0)
    fb[1, HALO:HALO + nx, :] = lax.dot_general(
        hot_x[...], weighed, (((1,), (1,)), ((), ())), precision=HIGHEST, preferred_element_type=jnp.float32)
    film_msgs = []
    for d in range(8):
        column, out_rows, rows = near_slot(d)
        film_msgs.append(Message(fb.at[1, out_rows, :], fb.at[column, rows, :], d))
        film_msgs[-1].start()

    solid_sweep(3)

    for m in film_msgs:
        m.arrived()
    wide = [widen(fb[0], fb[1], fb[2], f) for f in range(2)]
    diag = wd[...]
    inverse = 1.0 / (diag + wide[0])
    wcf[6, 0] = (wcf[6, 0] * diag + wide[1]) * inverse
    for n in range(6):
        wcf[n, 0] = wcf[n, 0] * diag * inverse

    for n in range(SWEEPS):
        decay, gain = coefficients[n]
        src, dst = (wxa, wxb) if n % 2 == 0 else (wxb, wxa)

        def body(z, _, n=n, decay=decay, gain=gain, src=src, dst=dst):
            v = src[z]
            near_v = shift_all(v) + [src[jnp.maximum(z - 1, 0)], src[z + 1]]
            r = wcf[6, z] - v
            for i in range(6):
                r = r + wcf[i, z] * near_v[i]
            p = gain * r if n == 0 else decay * wp[z] + gain * r
            wp[z] = p
            dst[z] = v + p
            return 0
        lax.fori_loop(0, DEEP - 1 - n, body, 0)

    solved = wxa if SWEEPS % 2 == 0 else wxb
    for z in range(HALO):
        wedge_out[z] = pltpu.roll(solved[z, HALO:HALO + nx, :], 128 - HALO, axis=1)

    surface = wedge_out[0][:, 0:32]
    picked = lax.dot_general(surface, hot_y[...], (((1,), (0,)), ((), ())), precision=HIGHEST, preferred_element_type=jnp.float32)
    picked = jnp.sum(picked * hot_x[...], axis=0, keepdims=True)
    for n in range(8):
        slots[n:n + 1, :] = picked[:, 256 * n:256 * n + 256]
    wall_s[...] = slots[:, 128:256]
    wall_msgs = [Message(wall_s, wall_r.at[d], d) for d in range(4)]
    for m in wall_msgs:
        m.start()

    solid_sweep(4)

    for m in wall_msgs:
        m.arrived()
    back = bands([wall_r.at[d] for d in (1, 0, 3, 2)])
    spread = lax.dot_general(back, select, (((1,), (0,)), ((), ())), precision=HIGHEST, preferred_element_type=jnp.float32)
    wall_out[...] = (self_mask * slots[:, 0:128] + spread) * live

    for n in range(5, SWEEPS):
        solid_sweep(n)
    x_store = pltpu.make_async_copy(xa, x_out, load_sem.at[10])
    x_store.start()
    t_store.wait()
    x_store.wait()
    for m in list(pending):
        m.sent()


N_MESSAGES = 4 + 6 + 2 + 2 + 8 + 4 * (SWEEPS - 1) + 4 + 4 + 8 + 4


def on_device(n_blk, n_sub, fluid_temp, velocity, eddy_diff, wall_prev, row_count, owner_table, landing_cell, solid_temp, conductivity, sink, heat_source):
    nx, ny, nz = fluid_temp.shape
    nsz = solid_temp.shape[2]
    f32 = jnp.float32
    wall_rows = wall_prev.reshape(128, 8).T
    landing = jnp.pad(landing_cell.reshape(192, 8).T, ((0, 0), (0, 64)), constant_values=-1)
    any_space = pl.BlockSpec(memory_space=pl.ANY)
    vmem_space = pl.BlockSpec(memory_space=pltpu.VMEM)

    def vmem(*shape):
        return pltpu.VMEM(shape, f32)

    wide = nx + 2 * HALO
    fluid_new, solid_bulk, wedge, wall_rows_new = pl.pallas_call(
        functools.partial(kernel, n_blk, n_sub),
        out_shape=(
            jax.ShapeDtypeStruct((nx, ny, nz), f32),
            jax.ShapeDtypeStruct((nx, ny, nsz), f32),
            jax.ShapeDtypeStruct((HALO, nx, 128), f32),
            jax.ShapeDtypeStruct((8, 128), f32),
        ),
        in_specs=[pl.BlockSpec(memory_space=pltpu.SMEM)] + [any_space] * 7 + [vmem_space] * 3,
        out_specs=(any_space, any_space, vmem_space, vmem_space),
        scratch_shapes=[
            vmem(nx, ny, nz), vmem(nx, ny, nz), vmem(nx, ny, nz),
            vmem(nx, ny, nz), vmem(nx, ny, nz), vmem(nx, ny, nz), vmem(nx, ny, nz),
            vmem(7, nx, ny, nz), vmem(nx, ny, 128),
            vmem(2, 3, ny, nz), vmem(2, 3, nx, nz), vmem(2, 3, nx, nz),
            vmem(2, ny, nz), vmem(2, nx, nz), vmem(2, nx, nz),
            vmem(nx, ny, nsz), vmem(nx, ny, nsz), vmem(nx, ny, nsz), vmem(nx, ny, nsz), vmem(nx, ny, nsz),
            vmem(7, nx, ny, nsz), vmem(nx, ny, nsz),
            vmem(SWEEPS - 1, 2, ny, nsz), vmem(SWEEPS - 1, 2, nx, nsz), vmem(SWEEPS - 1, 2, nx, nsz),
            vmem(2, 2, ny, nsz), vmem(2, 2, nx, nsz), vmem(2, 2, nx, nsz),
            vmem(3, DEEP, wide, 128), vmem(3, wide, 128),
            vmem(DEEP, wide, 128), vmem(7, DEEP, wide, 128),
            vmem(DEEP, wide, 128), vmem(DEEP, wide, 128), vmem(DEEP, wide, 128), vmem(wide, 128),
            vmem(16, 128), vmem(4, 16, 128), vmem(8, 128), vmem(4, 8, 128),
            vmem(32, 2048), vmem(32, 2048), vmem(8, 256),
            pltpu.SemaphoreType.DMA((11,)),
            pltpu.SemaphoreType.DMA((N_MESSAGES,)),
            pltpu.SemaphoreType.DMA((N_MESSAGES,)),
        ],
        compiler_params=pltpu.CompilerParams(
            collective_id=0, has_side_effects=True, vmem_limit_bytes=60 * 1024 * 1024
        ),
    )(row_count, fluid_temp, velocity, eddy_diff, solid_temp, conductivity, sink, heat_source, wall_rows, owner_table, landing)
    near_wall = jnp.pad(wedge[:, :, 0:ny].transpose(1, 2, 0), ((0, 0), (0, 0), (0, nsz - HALO)))
    depth = lax.broadcasted_iota(jnp.int32, solid_bulk.shape, 2)
    solid_new = jnp.where(depth < HALO, near_wall, solid_bulk)
    return fluid_new, solid_new, wall_rows_new.T.reshape(-1)


def solution(mesh):
    return jax.shard_map(
        functools.partial(on_device, mesh.shape["blk"], mesh.shape["sub"]),
        mesh=mesh,
        in_specs=(
            P("blk", "sub", None),
            P(None, "blk", "sub", None),
            P("blk", "sub", None),
            P(("blk", "sub")),
            P(("blk", "sub")),
            P(("blk", "sub"), None),
            P(("blk", "sub"), None),
            P("blk", "sub", None),
            P("blk", "sub", None),
            P("blk", "sub", None),
            P("blk", "sub", None),
        ),
        out_specs=(P("blk", "sub", None), P("blk", "sub", None), P(("blk", "sub"))),
        check_vma=False,
    )
```

```python
import functools

import jax
import jax.numpy as jnp
from jax import lax
from jax.experimental import pallas as pl
from jax.experimental.pallas import tpu as pltpu
from jax.sharding import PartitionSpec as P

MESH = pl.DeviceIdType.MESH
SWEEPS = 8
HALO = 8
DEEP = 16
TOP = 8
EIG_LOW = 0.02
EIG_HIGH = 2.0
HIGHEST = lax.Precision.HIGHEST
DIRS = ((1, 0), (-1, 0), (0, 1), (0, -1), (1, 1), (1, -1), (-1, 1), (-1, -1))


def cheby_coefficients(count_sweeps):
    center_eig = 0.5 * (EIG_HIGH + EIG_LOW)
    half_width = 0.5 * (EIG_HIGH - EIG_LOW)
    ratio_eig = center_eig / half_width
    damping = 1.0 / ratio_eig
    coefficients = [(0.0, 1.0 / center_eig)]
    for _ in range(1, count_sweeps):
        damping_new = 1.0 / (2.0 * ratio_eig - damping)
        coefficients.append((damping_new * damping, 2.0 * damping_new / half_width))
        damping = damping_new
    return coefficients


def iota(shape, dim):
    return lax.broadcasted_iota(jnp.int32, shape, dim)


def lane_shifts(v):
    lane = iota(v[0].shape, 1)
    low, high = [pltpu.roll(c, 1, axis=1) for c in v], [pltpu.roll(c, 127, axis=1) for c in v]
    below = [low[0]] + [jnp.where(lane == 0, low[c - 1], low[c]) for c in range(1, len(v))]
    above = [jnp.where(lane == 127, high[c + 1], high[c]) for c in range(len(v) - 1)] + [high[-1]]
    return below, above


def face(u, un, a, an):
    total_u, total_a = u + un, a + an
    return total_a + jnp.maximum(total_u, 0.0), total_a - jnp.minimum(total_u, 0.0)


def within(k, kn):
    return 2.0 * k * kn / (k + kn)


def conductance(k, kn):
    total = k + kn
    return 2.0 * k * kn / jnp.where(total > 0.0, total, 1.0)


def kernel(
    n_blk, n_sub,
    count_ref, t_hbm, vel_hbm, a_hbm, x_hbm, k_hbm, e_hbm, q_hbm, wall_ref, owner_ref, land_ref,
    t_out, x_out, wall_out,
    t0, t1, t2, ux, uy, uz, al, cf, sf,
    xa, xb, kc, ec, qc, cs,
    nb, fb, wk, wcf, wxa, wxb, wp, wd, wz,
    rows_s, rows_r, wall_s, wall_r, hot_x, hot_y, slots,
    load_sem, send_sem, recv_sem,
):
    b, s = lax.axis_index("blk"), lax.axis_index("sub")
    nx, ny, _ = t_hbm.shape
    fluid_chunks, solid_chunks = t0.shape[0], xa.shape[0]
    end = TOP + ny
    own_rows, own_planes = slice(TOP, end), slice(1, 1 + nx)
    coefficients = cheby_coefficients(SWEEPS)

    def inside(db, ds):
        ok = None
        for delta, at, count in ((db, b, n_blk), (ds, s, n_sub)):
            if delta:
                this = (at < count - 1) if delta > 0 else (at > 0)
                ok = this if ok is None else ok & this
        return ok

    counter = [0]
    pending = []

    class Message:
        def __init__(self, src, dst, d):
            db, ds = DIRS[d]
            self.n = counter[0]
            counter[0] += 1
            self.make = lambda: pltpu.make_async_remote_copy(
                src_ref=src, dst_ref=dst, send_sem=send_sem.at[self.n], recv_sem=recv_sem.at[self.n],
                device_id=(b + db, s + ds), device_id_type=MESH)
            self.goes, self.comes = inside(db, ds), inside(-db, -ds)

        def start(self):
            @pl.when(self.goes)
            def _():
                self.make().start()
            pending.append(self)
            return self

        def sent(self):
            @pl.when(self.goes)
            def _():
                self.make().wait_send()
            pending.remove(self)

        def arrived(self):
            @pl.when(self.comes)
            def _():
                self.make().wait_recv()

    def send_planes(ref):
        return [Message(ref.at[:, nx if d == 0 else 1, own_rows, :], ref.at[:, 0 if d == 0 else nx + 1, own_rows, :], d).start()
                for d in range(2)]

    def send_rows(ref):
        return [Message(ref.at[:, own_planes, end - 1:end, :], ref.at[:, own_planes, TOP - 1:TOP, :], 2).start(),
                Message(ref.at[:, own_planes, TOP:TOP + 1, :], ref.at[:, own_planes, end:end + 1, :], 3).start()]

    def arrived(messages):
        for m in messages:
            m.arrived()

    loads = {}
    for name, src, dst in (
        ("k", k_hbm, kc), ("x", x_hbm, xa), ("a", a_hbm, al), ("ux", vel_hbm.at[0], ux), ("t", t_hbm, t0), ("uy", vel_hbm.at[1], uy),
        ("e", e_hbm, ec), ("q", q_hbm, qc), ("uz", vel_hbm.at[2], uz),
    ):
        planes = own_planes if dst.shape[1] > nx else slice(0, nx)
        rows = own_rows if dst.shape[2] > ny else slice(0, ny)
        loads[name] = []
        for c in range(dst.shape[0]):
            n = sum(len(v) for v in loads.values())
            copy = pltpu.make_async_copy(src.at[:, :, 128 * c:128 * c + 128], dst.at[c, planes, rows, :], load_sem.at[n])
            copy.start()
            loads[name].append(copy)

    def loaded(*names):
        for name in names:
            for copy in loads[name]:
                copy.wait()

    barrier = pltpu.get_barrier_semaphore()
    for db, ds in DIRS:
        @pl.when(inside(db, ds))
        def _(db=db, ds=ds):
            pl.semaphore_signal(barrier, inc=1, device_id=(b + db, s + ds), device_id_type=MESH)

    def clear(ref, *where):
        ref[where] = jnp.zeros(ref.at[where].shape, jnp.float32)

    for d in range(2):
        @pl.when(jnp.logical_not(inside(-DIRS[d][0], 0)))
        def _(d=d):
            for ref in (t0, t1, al, ux, xa, xb, kc):
                rows = own_rows if ref.shape[2] > ny else slice(0, ny)
                for c in range(ref.shape[0]):
                    clear(ref, c, 0 if d == 0 else nx + 1, rows, slice(None))

        @pl.when(jnp.logical_not(inside(0, -DIRS[2 + d][1])))
        def _(d=d):
            row = TOP - 1 if d == 0 else end

            def body(x, _):
                for ref in (t0, t1, al, uy, xa, xb, kc):
                    for c in range(ref.shape[0]):
                        clear(ref, c, x + (1 if ref.shape[1] > nx else 0), slice(row, row + 1), slice(None))
                return 0
            lax.fori_loop(0, nx, body, 0)
    for d in range(4):
        @pl.when(jnp.logical_not(inside(-DIRS[d][0], -DIRS[d][1])))
        def _(d=d):
            rows_r[d] = jnp.zeros(rows_r.shape[1:], jnp.float32)
            wall_r[d] = jnp.zeros(wall_r.shape[1:], jnp.float32)

    def near_slot(d):
        db, ds = DIRS[d]
        column = {1: 0, 0: 1, -1: 2}[ds]
        if db == 0:
            return column, slice(HALO, HALO + nx), slice(HALO, HALO + nx)
        if db > 0:
            return column, slice(nx, HALO + nx), slice(0, HALO)
        return column, slice(HALO, 2 * HALO), slice(HALO + nx, 2 * HALO + nx)

    for d in range(8):
        @pl.when(jnp.logical_not(inside(-DIRS[d][0], -DIRS[d][1])))
        def _(d=d):
            column, _, rows = near_slot(d)
            height = rows.stop - rows.start
            nb[column, :, rows, :] = jnp.zeros((DEEP, height, 128), jnp.float32)
            fb[column, rows, :] = jnp.zeros((height, 128), jnp.float32)

    near = (b > 0).astype(jnp.int32) + (b < n_blk - 1).astype(jnp.int32)
    side = (s > 0).astype(jnp.int32) + (s < n_sub - 1).astype(jnp.int32)
    pl.semaphore_wait(barrier, near + side + near * side)

    loaded("k", "x")
    k_x, x_x = send_planes(kc), send_planes(xa)
    k_y, x_y = send_rows(kc), send_rows(xa)
    loaded("a", "ux", "t")
    a_x = send_planes(al)
    u_x = [Message(ux.at[:, nx if d == 0 else 1], ux.at[:, 0 if d == 0 else nx + 1], d).start() for d in range(2)]
    t_x = send_planes(t0)
    loaded("uy")
    a_y, t_y = send_rows(al), send_rows(t0)
    u_y = [Message(uy.at[:, :, end - 1:end, :], uy.at[:, :, TOP - 1:TOP, :], 2).start(),
           Message(uy.at[:, :, TOP:TOP + 1, :], uy.at[:, :, end:end + 1, :], 3).start()]

    loaded("e", "q")

    def turn(x, _):
        tile = jnp.concatenate([xa[0, x + 1, own_rows, :], kc[0, x + 1, own_rows, :], ec[0, x], qc[0, x]], axis=0)
        nb[1, :, pl.ds(HALO + x, 1), :] = jnp.transpose(tile)[0:DEEP].reshape(DEEP, 1, 128)
        return 0

    lax.fori_loop(0, nx, turn, 0, unroll=2)
    near_msgs = []
    for d in range(8):
        column, out_rows, rows = near_slot(d)
        near_msgs.append(Message(nb.at[1, :, out_rows, :], nb.at[column, :, rows, :], d).start())

    lane = iota((ny, 128), 1)

    def solid_coef(x, count):
        k = [[kc[c, x + i, own_rows, :] for c in range(solid_chunks)] for i in range(count + 2)]
        out = []
        for i in range(count):
            here, under, over = k[i + 1], k[i], k[i + 2]
            zm, _ = lane_shifts(here)
            gz = [within(here[c], zm[c]) for c in range(solid_chunks)]
            gz[0] = jnp.where(lane == 0, 0.0, gz[0])
            _, gz_up = lane_shifts(gz)
            gz_up[-1] = jnp.where(lane == 127, 0.0, gz_up[-1])
            for c in range(solid_chunks):
                g = [within(here[c], under[c]), within(here[c], over[c]),
                     within(here[c], kc[c, x + i + 1, TOP - 1:end - 1, :]), within(here[c], kc[c, x + i + 1, TOP + 1:end + 1, :]),
                     gz[c], gz_up[c]]
                inverse = 1.0 / (((g[0] + g[1]) + (g[2] + g[3])) + ((g[4] + g[5]) + ec[c, x + i]))
                out.append((c, x + i, [v * inverse for v in g] + [qc[c, x + i] * inverse]))
        for c, at, values in out:
            for n in range(7):
                cs[n, c, at] = values[n]

    def solid_planes(n, src, dst, x, count):
        decay, gain = coefficients[n]
        v = [[src[c, x + i, own_rows, :] for c in range(solid_chunks)] for i in range(count + 2)]
        out = []
        for i in range(count):
            zm, zp = lane_shifts(v[i + 1])
            for c in range(solid_chunks):
                at = x + i
                r = ((cs[0, c, at] * v[i][c] + cs[1, c, at] * v[i + 2][c])
                     + (cs[2, c, at] * src[c, at + 1, TOP - 1:end - 1, :] + cs[3, c, at] * src[c, at + 1, TOP + 1:end + 1, :]))
                r = r + (cs[4, c, at] * zm[c] + cs[5, c, at] * zp[c]) + cs[6, c, at]
                new = (1.0 + decay - gain) * v[i + 1][c] + gain * r
                if n > 0:
                    new = new - decay * dst[c, at + 1, own_rows, :]
                if n == SWEEPS - 1 and c == 0:
                    new = jnp.where(lane < HALO, wz[at], new)
                out.append((c, at, new))
        for c, at, new in out:
            dst[c, at + 1, own_rows, :] = new

    pairs = (nx - 2) // 2

    def solid_sweep(n, waits):
        src, dst = (xa, xb) if n % 2 == 0 else (xb, xa)
        arrived(waits)
        for m in list(solid_sends):
            if m[0] <= n - 2:
                m[1].sent()
                solid_sends.remove(m)
        solid_planes(n, src, dst, 0, 1)
        solid_planes(n, src, dst, nx - 1, 1)
        msgs = send_planes(dst) if n < SWEEPS - 1 else []

        def body(i, _):
            solid_planes(n, src, dst, 1 + 2 * i, 2)
            return 0
        lax.fori_loop(0, pairs, body, 0)
        if n < SWEEPS - 1:
            msgs += send_rows(dst)
        solid_sends.extend((n, m) for m in msgs)
        return msgs

    solid_sends = [(-1, m) for m in x_x + x_y]

    arrived(k_y)

    def body(i, _):
        solid_coef(1 + 2 * i, 2)
        return 0
    lax.fori_loop(0, pairs, body, 0)
    arrived(k_x)
    solid_coef(0, 1)
    solid_coef(nx - 1, 1)
    solid_msgs = solid_sweep(0, x_x + x_y)

    lane8, sub8 = iota((8, 128), 1), iota((8, 128), 0)
    live = jnp.where(lane8 * 8 + sub8 < count_ref[0], 1.0, 0.0)
    owner = jnp.broadcast_to(owner_ref[...], (8, 128))
    self_mask = jnp.where(owner == 0, 1.0, 0.0)
    match = jnp.where((owner == sub8 + 1) & (sub8 < 4), 1.0, 0.0)
    before = jnp.where(iota((128, 128), 0) < iota((128, 128), 1), 1.0, 0.0)
    rank = lax.dot_general(match, before, (((1,), (0,)), ((), ())), precision=HIGHEST, preferred_element_type=jnp.float32)
    place = jnp.sum(match * (rank + (sub8 * 16 + 1).astype(jnp.float32)), axis=0, keepdims=True) - 1.0
    select = jnp.where(iota((128, 128), 0).astype(jnp.float32) == place, 1.0, 0.0)
    row32 = iota((32, 256), 0)
    for n in range(8):
        cell = land_ref[n:n + 1, :]
        hot_x[:, 256 * n:256 * n + 256] = jnp.where((cell >> 5) == row32, 1.0, 0.0)
        hot_y[:, 256 * n:256 * n + 256] = jnp.where(((cell & 31) == row32) & (cell >= 0), 1.0, 0.0)

    mirror = 1.0 - 2.0 * live
    source = 2.0 * live * wall_ref[...]

    def columns(v, x):
        return jnp.concatenate([pltpu.roll(v, lax.rem(128 - (x * 4 + j), 128), axis=1) for j in range(4)], axis=0)

    def rows_of(plane):
        def body(i, parts):
            parts = list(parts)
            for k in range(4):
                v = plane(4 * i + k)
                for j in range(4):
                    parts[j] = jnp.where(lane8 == (4 * i + k) * 4 + j, jnp.broadcast_to(v[8 * j:8 * j + 8, 0:1], (8, 128)), parts[j])
            return tuple(parts)
        parts = lax.fori_loop(0, nx // 4, body, (jnp.zeros((8, 128), jnp.float32),) * 4)
        return (parts[0] + parts[1]) + (parts[2] + parts[3])

    top = fluid_chunks - 1

    def fluid_coef(x):
        a = [al[c, x + 1, own_rows, :] for c in range(fluid_chunks)]
        u = [uz[c, x] for c in range(fluid_chunks)]
        am, _ = lane_shifts(a)
        um, _ = lane_shifts(u)
        am[0] = jnp.where(lane == 0, a[0], am[0])
        um[0] = jnp.where(lane == 0, -u[0], um[0])
        z = [face(u[c], um[c], a[c], am[c]) for c in range(fluid_chunks)]
        _, pz = lane_shifts([v[0] for v in z])
        _, qz = lane_shifts([v[1] for v in z])
        last = face(u[top], u[top], a[top], a[top])
        pz[top] = jnp.where(lane == 127, last[0], pz[top])
        qz[top] = jnp.where(lane == 127, last[1], qz[top])
        for c in range(fluid_chunks):
            v = ux[c, x + 1]
            p_xm, q_xm = face(v, ux[c, x], a[c], al[c, x, own_rows, :])
            p_xp, q_xp = face(v, ux[c, x + 2], a[c], al[c, x + 2, own_rows, :])
            v = uy[c, x, own_rows, :]
            p_ym, q_ym = face(v, uy[c, x, TOP - 1:end - 1, :], a[c], al[c, x + 1, TOP - 1:end - 1, :])
            p_yp, q_yp = face(v, uy[c, x, TOP + 1:end + 1, :], a[c], al[c, x + 1, TOP + 1:end + 1, :])
            p_zm, q_zm = z[c]
            away = ((q_xm + p_xp) + (q_ym + p_yp)) + (q_zm + pz[c])
            toward = ((p_xm + q_xp) + (p_ym + q_yp)) + (p_zm + qz[c])
            scale = 1.6 / (away + toward)
            cf[0, c, x] = p_xm * scale
            cf[1, c, x] = q_xp * scale
            cf[2, c, x] = p_ym * scale
            cf[3, c, x] = q_yp * scale
            below, above, centre = p_zm * scale, qz[c] * scale, 1.0 - away * scale
            if c == 0:
                first = lane == 0
                wall = jnp.where(first, below, 0.0)
                sf[x] = wall * columns(source, x)
                centre = centre + wall * columns(mirror, x)
                below = jnp.where(first, 0.0, below)
            if c == top:
                above = jnp.where(lane == 127, 0.0, above)
            cf[4, c, x] = below
            cf[5, c, x] = above
            cf[6, c, x] = centre

    def fluid_plane(src, x):
        t = [src[c, x + 1, own_rows, :] for c in range(fluid_chunks)]
        zm, zp = lane_shifts(t)
        out = []
        for c in range(fluid_chunks):
            new = ((cf[0, c, x] * src[c, x, own_rows, :] + cf[1, c, x] * src[c, x + 2, own_rows, :])
                   + (cf[2, c, x] * src[c, x + 1, TOP - 1:end - 1, :] + cf[3, c, x] * src[c, x + 1, TOP + 1:end + 1, :]))
            new = new + (cf[4, c, x] * zm[c] + cf[5, c, x] * zp[c]) + cf[6, c, x] * t[c]
            out.append(new + sf[x] if c == 0 else new)
        return out

    loaded("uz")
    film = 2.0 * live * rows_of(lambda x: al[0, x + 1, own_rows, :])
    arrived(a_y + u_y)

    def body(x, _):
        fluid_coef(x)
        return 0
    lax.fori_loop(1, nx - 1, body, 0)
    arrived(a_x + u_x)
    fluid_coef(0)
    fluid_coef(nx - 1)

    def first_plane(x):
        for c, new in enumerate(fluid_plane(t0, x)):
            t1[c, x + 1, own_rows, :] = new

    arrived(t_x + t_y)
    first_plane(0)
    first_plane(nx - 1)
    t_msgs = send_planes(t1)

    def body(x, _):
        first_plane(x)
        return 0
    lax.fori_loop(1, nx - 1, body, 0)
    t_msgs += send_rows(t1)

    solid_msgs = solid_sweep(1, solid_msgs)

    arrived(t_msgs)

    def body(x, _):
        for c, new in enumerate(fluid_plane(t1, x)):
            t2[c, x] = new
        return 0
    lax.fori_loop(0, nx, body, 0)
    gas = rows_of(lambda x: t2[0, x])

    stores = []

    def store(src, dst):
        for c in range(src.shape[0]):
            n = sum(len(v) for v in loads.values()) + len(stores)
            stores.append(pltpu.make_async_copy(src.at[c], dst.at[:, :, 128 * c:128 * c + 128], load_sem.at[n]))
            stores[-1].start()

    store(t2, t_out)

    def take(v):
        return lax.dot_general(v, select, (((1,), (1,)), ((), ())), precision=HIGHEST, preferred_element_type=jnp.float32)

    rows_s[...] = take(jnp.concatenate([film, gas], axis=0))
    row_msgs = [Message(rows_s, rows_r.at[d], d) for d in range(4)]
    for m in row_msgs:
        m.start()

    solid_msgs = solid_sweep(2, solid_msgs)

    for m in near_msgs:
        m.arrived()
    lane_w = iota((nx + 2 * HALO, 128), 1)

    def widen(left, mid, right, f):
        left = pltpu.roll(left, (128 - 32 * f - 24) % 128, axis=1)
        mid = pltpu.roll(mid, (128 + HALO - 32 * f) % 128, axis=1)
        right = pltpu.roll(right, (128 + 40 - 32 * f) % 128, axis=1)
        return jnp.where(lane_w < HALO, left, jnp.where(lane_w < HALO + ny, mid, jnp.where(lane_w < 2 * HALO + ny, right, 0.0)))

    def near_field(z, f):
        return widen(nb[0, z], nb[1, z], nb[2, z], f)

    def body(z, _):
        wk[z] = near_field(z, 1)
        wxa[z] = near_field(z, 0)
        return 0
    lax.fori_loop(0, DEEP, body, 0)

    def shift_all(v):
        n = v.shape[0]
        return [pltpu.roll(v, 1, axis=0), pltpu.roll(v, n - 1, axis=0), pltpu.roll(v, 1, axis=1), pltpu.roll(v, 127, axis=1)]

    def body(z, _):
        k = wk[z]
        under = wk[jnp.maximum(z - 1, 0)] * (z > 0).astype(jnp.float32)
        over = wk[jnp.minimum(z + 1, DEEP - 1)] * (z < DEEP - 1).astype(jnp.float32)
        g = [conductance(k, kn) for kn in shift_all(k) + [under, over]]
        diag = ((g[0] + g[1]) + (g[2] + g[3])) + ((g[4] + g[5]) + near_field(z, 2))
        diag = jnp.where(diag > 0.0, diag, 1.0)
        inverse = 1.0 / diag
        for n in range(6):
            wcf[n, z] = g[n] * inverse
        wcf[6, z] = near_field(z, 3) * inverse

        @pl.when(z == 0)
        def _():
            wd[...] = diag
        return 0
    lax.fori_loop(0, DEEP, body, 0)

    for m in row_msgs:
        m.arrived()

    def bands(refs):
        total = None
        for band, ref in enumerate(refs):
            v = ref[...]
            lane = iota(v.shape, 1)
            v = jnp.where((lane >= 16 * band) & (lane < 16 * band + 16), v, 0.0)
            total = v if total is None else total + v
        return total

    came = bands([rows_r.at[d] for d in range(4)])
    film_in = jnp.concatenate([film * self_mask, came[0:8]], axis=1)
    heat_in = film_in * jnp.concatenate([gas, came[8:16]], axis=1)
    weighed = jnp.concatenate(
        [jnp.concatenate([hot_y[:, 256 * n:256 * n + 256] * v[n:n + 1, :] for n in range(8)], axis=1) for v in (film_in, heat_in)]
        + [jnp.zeros((64, 2048), jnp.float32)], axis=0)
    fb[1, HALO:HALO + nx, :] = lax.dot_general(
        hot_x[...], weighed, (((1,), (1,)), ((), ())), precision=HIGHEST, preferred_element_type=jnp.float32)
    film_msgs = []
    for d in range(8):
        column, out_rows, rows = near_slot(d)
        film_msgs.append(Message(fb.at[1, out_rows, :], fb.at[column, rows, :], d))
        film_msgs[-1].start()

    solid_msgs = solid_sweep(3, solid_msgs)

    for m in film_msgs:
        m.arrived()
    wide = [widen(fb[0], fb[1], fb[2], f) for f in range(2)]
    diag = wd[...]
    inverse = 1.0 / (diag + wide[0])
    wcf[6, 0] = (wcf[6, 0] * diag + wide[1]) * inverse
    for n in range(6):
        wcf[n, 0] = wcf[n, 0] * diag * inverse

    for n in range(SWEEPS):
        decay, gain = coefficients[n]
        src, dst = (wxa, wxb) if n % 2 == 0 else (wxb, wxa)

        def level(z, n=n, decay=decay, gain=gain, src=src):
            v = src[z]
            near_v = shift_all(v) + [src[jnp.maximum(z - 1, 0)], src[z + 1]]
            r = (wcf[0, z] * near_v[0] + wcf[1, z] * near_v[1]) + (wcf[2, z] * near_v[2] + wcf[3, z] * near_v[3])
            r = r + (wcf[4, z] * near_v[4] + wcf[5, z] * near_v[5]) + wcf[6, z]
            new = (1.0 + decay - gain) * v + gain * r
            return new if n == 0 else new - decay * dst[z]

        count = DEEP - 1 - n

        def body(i, _, dst=dst, level=level):
            news = [level(2 * i), level(2 * i + 1)]
            for k in range(2):
                dst[2 * i + k] = news[k]
            return 0
        lax.fori_loop(0, count // 2, body, 0)
        if count % 2:
            dst[count - 1] = level(count - 1)

    solved = wxa if SWEEPS % 2 == 0 else wxb
    surface = pltpu.roll(solved[0, HALO:HALO + nx, :], 128 - HALO, axis=1)[:, 0:32]
    picked = lax.dot_general(surface, hot_y[...], (((1,), (0,)), ((), ())), precision=HIGHEST, preferred_element_type=jnp.float32)
    picked = jnp.sum(picked * hot_x[...], axis=0, keepdims=True)
    for n in range(8):
        slots[n:n + 1, :] = picked[:, 256 * n:256 * n + 256]
    wall_s[...] = slots[:, 128:256]
    wall_msgs = [Message(wall_s, wall_r.at[d], d) for d in range(4)]
    for m in wall_msgs:
        m.start()

    def body(x, _):
        cells = jnp.concatenate([solved[0:HALO, pl.ds(HALO + x, 1), :].reshape(HALO, 128), jnp.zeros((128 - HALO, 128), jnp.float32)], axis=0)
        wz[x] = jnp.transpose(cells)[HALO:HALO + ny]
        return 0
    lax.fori_loop(0, nx, body, 0)

    solid_msgs = solid_sweep(4, solid_msgs)

    for m in wall_msgs:
        m.arrived()
    back = bands([wall_r.at[d] for d in (1, 0, 3, 2)])
    spread = lax.dot_general(back, select, (((1,), (0,)), ((), ())), precision=HIGHEST, preferred_element_type=jnp.float32)
    wall_out[...] = (self_mask * slots[:, 0:128] + spread) * live

    for n in range(5, SWEEPS):
        solid_msgs = solid_sweep(n, solid_msgs)
    store(xa.at[:, own_planes, own_rows, :], x_out)
    for copy in stores:
        copy.wait()
    for m in list(pending):
        m.sent()


N_MESSAGES = 8 + 12 + 8 + 4 * (SWEEPS - 1) + 4 + 4 + 8 + 4


def on_device(n_blk, n_sub, fluid_temp, velocity, eddy_diff, wall_prev, row_count, owner_table, landing_cell, solid_temp, conductivity, sink, heat_source):
    nx, ny, nz = fluid_temp.shape
    nsz = solid_temp.shape[2]
    f32 = jnp.float32
    wall_rows = wall_prev.reshape(128, 8).T
    landing = jnp.pad(landing_cell.reshape(192, 8).T, ((0, 0), (0, 64)), constant_values=-1)
    any_space = pl.BlockSpec(memory_space=pl.ANY)
    vmem_space = pl.BlockSpec(memory_space=pltpu.VMEM)

    def vmem(*shape):
        return pltpu.VMEM(shape, f32)

    def haloed(depth):
        return vmem(depth // 128, nx + 2, ny + 2 * TOP, 128)

    wide = nx + 2 * HALO
    fluid_new, solid_new, wall_rows_new = pl.pallas_call(
        functools.partial(kernel, n_blk, n_sub),
        out_shape=(
            jax.ShapeDtypeStruct((nx, ny, nz), f32),
            jax.ShapeDtypeStruct((nx, ny, nsz), f32),
            jax.ShapeDtypeStruct((8, 128), f32),
        ),
        in_specs=[pl.BlockSpec(memory_space=pltpu.SMEM)] + [any_space] * 7 + [vmem_space] * 3,
        out_specs=(any_space, any_space, vmem_space),
        scratch_shapes=[
            haloed(nz), haloed(nz), vmem(nz // 128, nx, ny, 128),
            vmem(nz // 128, nx + 2, ny, 128), vmem(nz // 128, nx, ny + 2 * TOP, 128), vmem(nz // 128, nx, ny, 128),
            haloed(nz), vmem(7, nz // 128, nx, ny, 128), vmem(nx, ny, 128),
            haloed(nsz), haloed(nsz), haloed(nsz), vmem(nsz // 128, nx, ny, 128), vmem(nsz // 128, nx, ny, 128),
            vmem(7, nsz // 128, nx, ny, 128),
            vmem(3, DEEP, wide, 128), vmem(3, wide, 128),
            vmem(DEEP, wide, 128), vmem(7, DEEP, wide, 128),
            vmem(DEEP, wide, 128), vmem(DEEP, wide, 128), vmem(DEEP, wide, 128), vmem(wide, 128), vmem(nx, ny, 128),
            vmem(16, 128), vmem(4, 16, 128), vmem(8, 128), vmem(4, 8, 128),
            vmem(32, 2048), vmem(32, 2048), vmem(8, 256),
            pltpu.SemaphoreType.DMA((6 * nz // 128 + 5 * nsz // 128,)),
            pltpu.SemaphoreType.DMA((N_MESSAGES,)),
            pltpu.SemaphoreType.DMA((N_MESSAGES,)),
        ],
        compiler_params=pltpu.CompilerParams(
            collective_id=0, has_side_effects=True, vmem_limit_bytes=60 * 1024 * 1024
        ),
    )(row_count, fluid_temp, velocity, eddy_diff, solid_temp, conductivity, sink, heat_source, wall_rows, owner_table, landing)
    return fluid_new, solid_new, wall_rows_new.T.reshape(-1)


def solution(mesh):
    return jax.shard_map(
        functools.partial(on_device, mesh.shape["blk"], mesh.shape["sub"]),
        mesh=mesh,
        in_specs=(
            P("blk", "sub", None),
            P(None, "blk", "sub", None),
            P("blk", "sub", None),
            P(("blk", "sub")),
            P(("blk", "sub")),
            P(("blk", "sub"), None),
            P(("blk", "sub"), None),
            P("blk", "sub", None),
            P("blk", "sub", None),
            P("blk", "sub", None),
            P("blk", "sub", None),
        ),
        out_specs=(P("blk", "sub", None), P("blk", "sub", None), P(("blk", "sub"))),
        check_vma=False,
    )
```

```python
import functools

import jax
import jax.numpy as jnp
from jax import lax
from jax.experimental import pallas as pl
from jax.experimental.pallas import tpu as pltpu
from jax.sharding import PartitionSpec as P

MESH = pl.DeviceIdType.MESH
SWEEPS = 8
HALO = 8
DEEP = 16
TOP = 8
SOLID_STEP = 5
WEDGE_SPLIT = 4
FLUID_STEP = 2
EIG_LOW = 0.02
EIG_HIGH = 2.0
HIGHEST = lax.Precision.HIGHEST
DIRS = ((1, 0), (-1, 0), (0, 1), (0, -1), (1, 1), (1, -1), (-1, 1), (-1, -1))


def cheby_coefficients(count_sweeps):
    center_eig = 0.5 * (EIG_HIGH + EIG_LOW)
    half_width = 0.5 * (EIG_HIGH - EIG_LOW)
    ratio_eig = center_eig / half_width
    damping = 1.0 / ratio_eig
    coefficients = [(0.0, 1.0 / center_eig)]
    for _ in range(1, count_sweeps):
        damping_new = 1.0 / (2.0 * ratio_eig - damping)
        coefficients.append((damping_new * damping, 2.0 * damping_new / half_width))
        damping = damping_new
    return coefficients


def iota(shape, dim):
    return lax.broadcasted_iota(jnp.int32, shape, dim)


def lane_shifts(v):
    lane = iota(v[0].shape, 1)
    low, high = [pltpu.roll(c, 1, axis=1) for c in v], [pltpu.roll(c, 127, axis=1) for c in v]
    below = [low[0]] + [jnp.where(lane == 0, low[c - 1], low[c]) for c in range(1, len(v))]
    above = [jnp.where(lane == 127, high[c + 1], high[c]) for c in range(len(v) - 1)] + [high[-1]]
    return below, above


def face(u, un, a, an):
    total_u, total_a = u + un, a + an
    return total_a + jnp.maximum(total_u, 0.0), total_a - jnp.minimum(total_u, 0.0)


def within(k, kn):
    return 2.0 * k * kn / (k + kn)


def conductance(k, kn):
    total = k + kn
    return 2.0 * k * kn / jnp.where(total > 0.0, total, 1.0)


def kernel(
    n_blk, n_sub,
    count_ref, t_hbm, vel_hbm, a_hbm, x_hbm, k_hbm, e_hbm, q_hbm, wall_ref, owner_ref, land_ref,
    t_out, x_out, wall_out,
    t0, t1, ux, uy, uz, al, cf, sf,
    xa, xb, kc, ec, qc, cs,
    nb, fb, wk, wcf, wxa, wxb, wp, wd, wz,
    rows_s, rows_r, wall_s, wall_r, hot_x, hot_y, slots,
    load_sem, send_sem, recv_sem,
):
    b, s = lax.axis_index("blk"), lax.axis_index("sub")
    nx, ny, _ = t_hbm.shape
    fluid_chunks, solid_chunks = t0.shape[0], xa.shape[0]
    end = TOP + ny
    own_rows, own_planes = slice(TOP, end), slice(1, 1 + nx)
    coefficients = cheby_coefficients(SWEEPS)

    def inside(db, ds):
        ok = None
        for delta, at, count in ((db, b, n_blk), (ds, s, n_sub)):
            if delta:
                this = (at < count - 1) if delta > 0 else (at > 0)
                ok = this if ok is None else ok & this
        return ok

    counter = [0]
    pending = []

    class Message:
        def __init__(self, src, dst, d):
            db, ds = DIRS[d]
            self.n = counter[0]
            counter[0] += 1
            self.make = lambda: pltpu.make_async_remote_copy(
                src_ref=src, dst_ref=dst, send_sem=send_sem.at[self.n], recv_sem=recv_sem.at[self.n],
                device_id=(b + db, s + ds), device_id_type=MESH)
            self.goes, self.comes = inside(db, ds), inside(-db, -ds)

        def start(self):
            @pl.when(self.goes)
            def _():
                self.make().start()
            pending.append(self)
            return self

        def sent(self):
            @pl.when(self.goes)
            def _():
                self.make().wait_send()
            pending.remove(self)

        def arrived(self):
            @pl.when(self.comes)
            def _():
                self.make().wait_recv()

    def send_planes(ref):
        return [Message(ref.at[:, nx if d == 0 else 1, own_rows, :], ref.at[:, 0 if d == 0 else nx + 1, own_rows, :], d).start()
                for d in range(2)]

    def send_rows(ref):
        return [Message(ref.at[:, own_planes, end - 1:end, :], ref.at[:, own_planes, TOP - 1:TOP, :], 2).start(),
                Message(ref.at[:, own_planes, TOP:TOP + 1, :], ref.at[:, own_planes, end:end + 1, :], 3).start()]

    def arrived(messages):
        for m in messages:
            m.arrived()

    loads = {}
    for name, src, dst in (
        ("k", k_hbm, kc), ("x", x_hbm, xa), ("a", a_hbm, al), ("ux", vel_hbm.at[0], ux), ("t", t_hbm, t0), ("uy", vel_hbm.at[1], uy),
        ("e", e_hbm, ec), ("q", q_hbm, qc), ("uz", vel_hbm.at[2], uz),
    ):
        planes = own_planes if dst.shape[1] > nx else slice(0, nx)
        rows = own_rows if dst.shape[2] > ny else slice(0, ny)
        loads[name] = []
        for c in range(dst.shape[0]):
            n = sum(len(v) for v in loads.values())
            copy = pltpu.make_async_copy(src.at[:, :, 128 * c:128 * c + 128], dst.at[c, planes, rows, :], load_sem.at[n])
            copy.start()
            loads[name].append(copy)

    def loaded(*names):
        for name in names:
            for copy in loads[name]:
                copy.wait()

    barrier = pltpu.get_barrier_semaphore()
    for db, ds in DIRS:
        @pl.when(inside(db, ds))
        def _(db=db, ds=ds):
            pl.semaphore_signal(barrier, inc=1, device_id=(b + db, s + ds), device_id_type=MESH)

    def clear(ref, *where):
        ref[where] = jnp.zeros(ref.at[where].shape, jnp.float32)

    for d in range(2):
        @pl.when(jnp.logical_not(inside(-DIRS[d][0], 0)))
        def _(d=d):
            for ref in (t0, t1, al, ux, xa, xb, kc):
                rows = own_rows if ref.shape[2] > ny else slice(0, ny)
                for c in range(ref.shape[0]):
                    clear(ref, c, 0 if d == 0 else nx + 1, rows, slice(None))

        @pl.when(jnp.logical_not(inside(0, -DIRS[2 + d][1])))
        def _(d=d):
            row = TOP - 1 if d == 0 else end

            def body(x, _):
                for ref in (t0, t1, al, uy, xa, xb, kc):
                    for c in range(ref.shape[0]):
                        clear(ref, c, x + (1 if ref.shape[1] > nx else 0), slice(row, row + 1), slice(None))
                return 0
            lax.fori_loop(0, nx, body, 0)
    for d in range(4):
        @pl.when(jnp.logical_not(inside(-DIRS[d][0], -DIRS[d][1])))
        def _(d=d):
            rows_r[d] = jnp.zeros(rows_r.shape[1:], jnp.float32)
            wall_r[d] = jnp.zeros(wall_r.shape[1:], jnp.float32)

    def near_slot(d):
        db, ds = DIRS[d]
        column = {1: 0, 0: 1, -1: 2}[ds]
        if db == 0:
            return column, slice(HALO, HALO + nx), slice(HALO, HALO + nx)
        if db > 0:
            return column, slice(nx, HALO + nx), slice(0, HALO)
        return column, slice(HALO, 2 * HALO), slice(HALO + nx, 2 * HALO + nx)

    for d in range(8):
        @pl.when(jnp.logical_not(inside(-DIRS[d][0], -DIRS[d][1])))
        def _(d=d):
            column, _, rows = near_slot(d)
            height = rows.stop - rows.start
            nb[column, :, rows, :] = jnp.zeros((DEEP, height, 128), jnp.float32)
            fb[column, rows, :] = jnp.zeros((height, 128), jnp.float32)

    def product(x, y, dims):
        return lax.dot_general(x, y, (dims, ((), ())), precision=HIGHEST, preferred_element_type=jnp.float32)

    lane, lane8, sub8 = iota((ny, 128), 1), iota((8, 128), 1), iota((8, 128), 0)
    keep = (lane8 & 7) == sub8
    compress = jnp.where((iota((128, 128), 0) >> 3) == iota((128, 128), 1), 1.0, 0.0)
    flat = [wall_ref[n:n + 1, :] for n in range(8)] + [land_ref[0:1, 128 * n:128 * n + 128].astype(jnp.float32) for n in range(12)]
    packed = product(jnp.concatenate([jnp.where(keep, jnp.broadcast_to(v, (8, 128)), 0.0) for v in flat], axis=0), compress, ((1,), (0,)))

    def gather_rows(first, count):
        total = packed[8 * first:8 * first + 8]
        for n in range(1, count):
            total = total + pltpu.roll(packed[8 * (first + n):8 * (first + n) + 8], 16 * n, axis=1)
        return total

    wall = gather_rows(0, 8)
    land = jnp.concatenate([gather_rows(8, 8), jnp.where(lane8 < 64, gather_rows(16, 4), -1.0)], axis=1).astype(jnp.int32)
    live = jnp.where(lane8 * 8 + sub8 < count_ref[0], 1.0, 0.0)
    owner = jnp.broadcast_to(owner_ref[...], (8, 128))
    self_mask = jnp.where(owner == 0, 1.0, 0.0)
    match = jnp.where((owner == sub8 + 1) & (sub8 < 4), 1.0, 0.0)
    before = jnp.where(iota((128, 128), 0) < iota((128, 128), 1), 1.0, 0.0)
    rank = product(match, before, ((1,), (0,)))
    place = jnp.sum(match * (rank + (sub8 * 16 + 1).astype(jnp.float32)), axis=0, keepdims=True) - 1.0
    row32 = iota((32, 256), 0)
    for n in range(8):
        cell = land[n:n + 1, :]
        hot_x[:, 256 * n:256 * n + 256] = jnp.where((cell >> 5) == row32, 1.0, 0.0)
        hot_y[:, 256 * n:256 * n + 256] = jnp.where(((cell & 31) == row32) & (cell >= 0), 1.0, 0.0)

    def select():
        return jnp.where(iota((128, 128), 0).astype(jnp.float32) == place, 1.0, 0.0)

    near = (b > 0).astype(jnp.int32) + (b < n_blk - 1).astype(jnp.int32)
    side = (s > 0).astype(jnp.int32) + (s < n_sub - 1).astype(jnp.int32)
    pl.semaphore_wait(barrier, near + side + near * side)

    loaded("k", "x")
    k_x, x_x = send_planes(kc), send_planes(xa)
    k_y, x_y = send_rows(kc), send_rows(xa)
    loaded("a", "ux", "t")
    a_x = send_planes(al)
    u_x = [Message(ux.at[:, nx if d == 0 else 1], ux.at[:, 0 if d == 0 else nx + 1], d).start() for d in range(2)]
    t_x = send_planes(t0)
    loaded("uy")
    a_y, t_y = send_rows(al), send_rows(t0)
    u_y = [Message(uy.at[:, :, end - 1:end, :], uy.at[:, :, TOP - 1:TOP, :], 2).start(),
           Message(uy.at[:, :, TOP:TOP + 1, :], uy.at[:, :, end:end + 1, :], 3).start()]

    def turn(x, _):
        tile = jnp.concatenate([xa[0, x + 1, own_rows, :], kc[0, x + 1, own_rows, :], ec[0, x], qc[0, x]], axis=0)
        nb[1, :, pl.ds(HALO + x, 1), :] = jnp.transpose(tile)[0:DEEP].reshape(DEEP, 1, 128)
        return 0

    def send_near(column_ref, part):
        messages = []
        for d in range(8):
            column, out_rows, rows = near_slot(d)
            messages.append(Message(part(column_ref, 1, out_rows), part(column_ref, column, rows), d).start())
        return messages

    def solid_coef(x, count):
        k = [[kc[c, x + i, own_rows, :] for c in range(solid_chunks)] for i in range(count + 2)]
        out = []
        for i in range(count):
            here, under, over = k[i + 1], k[i], k[i + 2]
            zm, _ = lane_shifts(here)
            gz = [within(here[c], zm[c]) for c in range(solid_chunks)]
            gz[0] = jnp.where(lane == 0, 0.0, gz[0])
            _, gz_up = lane_shifts(gz)
            gz_up[-1] = jnp.where(lane == 127, 0.0, gz_up[-1])
            for c in range(solid_chunks):
                g = [within(here[c], under[c]), within(here[c], over[c]),
                     within(here[c], kc[c, x + i + 1, TOP - 1:end - 1, :]), within(here[c], kc[c, x + i + 1, TOP + 1:end + 1, :]),
                     gz[c], gz_up[c]]
                inverse = 1.0 / (((g[0] + g[1]) + (g[2] + g[3])) + ((g[4] + g[5]) + ec[c, x + i]))
                out.append((c, x + i, [v * inverse for v in g] + [qc[c, x + i] * inverse]))
        for c, at, values in out:
            for n in range(7):
                cs[n, c, at] = values[n]

    def solid_planes(n, src, dst, runs):
        decay, gain = coefficients[n]
        out = []
        for x, count in runs:
            v = [[src[c, x + i, own_rows, :] for c in range(solid_chunks)] for i in range(count + 2)]
            for i in range(count):
                zm, zp = lane_shifts(v[i + 1])
                for c in range(solid_chunks):
                    at = x + i
                    r = ((cs[0, c, at] * v[i][c] + cs[1, c, at] * v[i + 2][c])
                         + (cs[2, c, at] * src[c, at + 1, TOP - 1:end - 1, :] + cs[3, c, at] * src[c, at + 1, TOP + 1:end + 1, :]))
                    r = r + (cs[4, c, at] * zm[c] + cs[5, c, at] * zp[c]) + cs[6, c, at]
                    new = (1.0 + decay - gain) * v[i + 1][c] + gain * r
                    if n > 0:
                        new = new - decay * dst[c, at + 1, own_rows, :]
                    if n == SWEEPS - 1 and c == 0:
                        new = jnp.where(lane < HALO, wz[at], new)
                    out.append((c, at, new))
        for c, at, new in out:
            if n == SWEEPS - 1:
                x_out[at, :, 128 * c:128 * c + 128] = new
            else:
                dst[c, at + 1, own_rows, :] = new

    solid_sends = [(-1, m) for m in x_x + x_y]
    solid_waits = [x_x + x_y]
    interior = nx - 2

    def loop(count, step, work):
        def body(i, _):
            work(i * step)
            return 0
        lax.fori_loop(0, count // step, body, 0)

    def solid_sweep(n):
        src, dst = (xa, xb) if n % 2 == 0 else (xb, xa)
        arrived(solid_waits.pop())
        for m in list(solid_sends):
            if m[0] <= n - 2:
                m[1].sent()
                solid_sends.remove(m)
        solid_planes(n, src, dst, [(0, 1), (nx - 1, 1)])
        msgs = send_planes(dst) if n < SWEEPS - 1 else []
        loop(interior, SOLID_STEP, lambda x: solid_planes(n, src, dst, [(1 + x, SOLID_STEP)]))
        if n < SWEEPS - 1:
            msgs += send_rows(dst)
        solid_sends.extend((n, m) for m in msgs)
        solid_waits.append(msgs)

    mirror = 1.0 - 2.0 * live
    source = 2.0 * live * wall

    def columns(v, x):
        return jnp.concatenate([pltpu.roll(v, lax.rem(128 - (x * 4 + j), 128), axis=1) for j in range(4)], axis=0)

    def rows_of(plane):
        def body(i, parts):
            parts = list(parts)
            for k in range(4):
                v = plane(4 * i + k)
                for j in range(4):
                    parts[j] = jnp.where(lane8 == (4 * i + k) * 4 + j, jnp.broadcast_to(v[8 * j:8 * j + 8, 0:1], (8, 128)), parts[j])
            return tuple(parts)
        parts = lax.fori_loop(0, nx // 4, body, (jnp.zeros((8, 128), jnp.float32),) * 4)
        return (parts[0] + parts[1]) + (parts[2] + parts[3])

    top = fluid_chunks - 1

    def fluid_coef(x):
        a = [al[c, x + 1, own_rows, :] for c in range(fluid_chunks)]
        u = [uz[c, x] for c in range(fluid_chunks)]
        am, _ = lane_shifts(a)
        um, _ = lane_shifts(u)
        am[0] = jnp.where(lane == 0, a[0], am[0])
        um[0] = jnp.where(lane == 0, -u[0], um[0])
        z = [face(u[c], um[c], a[c], am[c]) for c in range(fluid_chunks)]
        _, pz = lane_shifts([v[0] for v in z])
        _, qz = lane_shifts([v[1] for v in z])
        last = face(u[top], u[top], a[top], a[top])
        pz[top] = jnp.where(lane == 127, last[0], pz[top])
        qz[top] = jnp.where(lane == 127, last[1], qz[top])
        for c in range(fluid_chunks):
            v = ux[c, x + 1]
            p_xm, q_xm = face(v, ux[c, x], a[c], al[c, x, own_rows, :])
            p_xp, q_xp = face(v, ux[c, x + 2], a[c], al[c, x + 2, own_rows, :])
            v = uy[c, x, own_rows, :]
            p_ym, q_ym = face(v, uy[c, x, TOP - 1:end - 1, :], a[c], al[c, x + 1, TOP - 1:end - 1, :])
            p_yp, q_yp = face(v, uy[c, x, TOP + 1:end + 1, :], a[c], al[c, x + 1, TOP + 1:end + 1, :])
            p_zm, q_zm = z[c]
            away = ((q_xm + p_xp) + (q_ym + p_yp)) + (q_zm + pz[c])
            toward = ((p_xm + q_xp) + (p_ym + q_yp)) + (p_zm + qz[c])
            scale = 1.6 / (away + toward)
            cf[0, c, x] = p_xm * scale
            cf[1, c, x] = q_xp * scale
            cf[2, c, x] = p_ym * scale
            cf[3, c, x] = q_yp * scale
            below, above, centre = p_zm * scale, qz[c] * scale, 1.0 - away * scale
            if c == 0:
                first = lane == 0
                at_wall = jnp.where(first, below, 0.0)
                sf[x] = at_wall * columns(source, x)
                centre = centre + at_wall * columns(mirror, x)
                below = jnp.where(first, 0.0, below)
            if c == top:
                above = jnp.where(lane == 127, 0.0, above)
            cf[4, c, x] = below
            cf[5, c, x] = above
            cf[6, c, x] = centre

    def fluid_planes(src, xs, chunks, put):
        out = []
        for x in xs:
            held = {}

            def rolled(c, shift, held=held, x=x):
                if (c, shift) not in held:
                    held[c, shift] = pltpu.roll(src[c, x + 1, own_rows, :], shift, axis=1)
                return held[c, shift]

            for c in chunks:
                zm = rolled(c, 1) if c == 0 else jnp.where(lane == 0, rolled(c - 1, 1), rolled(c, 1))
                zp = rolled(c, 127) if c == top else jnp.where(lane == 127, rolled(c + 1, 127), rolled(c, 127))
                new = ((cf[0, c, x] * src[c, x, own_rows, :] + cf[1, c, x] * src[c, x + 2, own_rows, :])
                       + (cf[2, c, x] * src[c, x + 1, TOP - 1:end - 1, :] + cf[3, c, x] * src[c, x + 1, TOP + 1:end + 1, :]))
                new = new + (cf[4, c, x] * zm + cf[5, c, x] * zp) + cf[6, c, x] * src[c, x + 1, own_rows, :]
                out.append((c, x, new + sf[x] if c == 0 else new))
        for item in out:
            put(*item)

    def put_first(c, x, new):
        t1[c, x + 1, own_rows, :] = new

    def put_second(c, x, new):
        t_out[x, :, 128 * c:128 * c + 128] = new

    lane_w = iota((nx + 2 * HALO, 128), 1)

    def widen(left, mid, right, f):
        left = pltpu.roll(left, (128 - 32 * f - 24) % 128, axis=1)
        mid = pltpu.roll(mid, (128 + HALO - 32 * f) % 128, axis=1)
        right = pltpu.roll(right, (128 + 40 - 32 * f) % 128, axis=1)
        return jnp.where(lane_w < HALO, left, jnp.where(lane_w < HALO + ny, mid, jnp.where(lane_w < 2 * HALO + ny, right, 0.0)))

    def near_field(z, f):
        return widen(nb[0, z], nb[1, z], nb[2, z], f)

    def shift_all(v):
        n = v.shape[0]
        return [pltpu.roll(v, 1, axis=0), pltpu.roll(v, n - 1, axis=0), pltpu.roll(v, 1, axis=1), pltpu.roll(v, 127, axis=1)]

    def spread_near(z):
        wk[z] = near_field(z, 1)
        wxa[z] = near_field(z, 0)

    def wedge_coef(z):
        k = wk[z]
        under = wk[jnp.maximum(z - 1, 0)] * (z > 0).astype(jnp.float32)
        over = wk[jnp.minimum(z + 1, DEEP - 1)] * (z < DEEP - 1).astype(jnp.float32)
        g = [conductance(k, kn) for kn in shift_all(k) + [under, over]]
        diag = ((g[0] + g[1]) + (g[2] + g[3])) + ((g[4] + g[5]) + near_field(z, 2))
        diag = jnp.where(diag > 0.0, diag, 1.0)
        inverse = 1.0 / diag
        for n in range(6):
            wcf[n, z] = g[n] * inverse
        wcf[6, z] = near_field(z, 3) * inverse

        @pl.when(z == 0)
        def _():
            wd[...] = diag

    def wedge_sweep(n):
        decay, gain = coefficients[n]
        src, dst = (wxa, wxb) if n % 2 == 0 else (wxb, wxa)

        def level(z):
            v = src[z]
            near_v = shift_all(v) + [src[jnp.maximum(z - 1, 0)], src[z + 1]]
            r = (wcf[0, z] * near_v[0] + wcf[1, z] * near_v[1]) + (wcf[2, z] * near_v[2] + wcf[3, z] * near_v[3])
            r = r + (wcf[4, z] * near_v[4] + wcf[5, z] * near_v[5]) + wcf[6, z]
            new = (1.0 + decay - gain) * v + gain * r
            return new if n == 0 else new - decay * dst[z]

        def levels(z, step):
            for k, new in enumerate([level(z + k) for k in range(step)]):
                dst[z + k] = new

        count = DEEP - 1 - n
        step = 3 if count % 3 == 0 else 2
        loop(count - count % step, step, lambda z: levels(z, step))
        if count % step:
            levels(count - count % step, count % step)

    def bands(refs):
        total = None
        for band, ref in enumerate(refs):
            v = ref[...]
            at = iota(v.shape, 1)
            v = jnp.where((at >= 16 * band) & (at < 16 * band + 16), v, 0.0)
            total = v if total is None else total + v
        return total

    all_chunks = range(fluid_chunks)
    loaded("e", "q")
    lax.fori_loop(0, nx, turn, 0, unroll=2)
    film = 2.0 * live * rows_of(lambda x: al[0, x + 1, own_rows, :])
    arrived(k_y)
    loop(interior, 2, lambda x: solid_coef(1 + x, 2))
    arrived(k_x)
    solid_coef(0, 1)
    solid_coef(nx - 1, 1)
    solid_sweep(0)
    near_msgs = send_near(nb, lambda ref, column, rows: ref.at[column, :, rows, :])

    loaded("uz")
    arrived(a_y + u_y)
    half = interior // 2
    loop(half, 1, lambda x: fluid_coef(1 + x))
    solid_sweep(1)
    loop(interior - half, 1, lambda x: fluid_coef(1 + half + x))
    arrived(a_x + u_x)
    fluid_coef(0)
    fluid_coef(nx - 1)

    arrived(t_x + t_y)
    fluid_planes(t0, (0, nx - 1), all_chunks, put_first)
    t_msgs = send_planes(t1)
    loop(interior, FLUID_STEP, lambda x: fluid_planes(t0, [1 + x + i for i in range(FLUID_STEP)], all_chunks, put_first))
    t_msgs += send_rows(t1)
    solid_sweep(2)

    arrived(near_msgs)
    loop(DEEP, 1, spread_near)
    loop(DEEP, 1, wedge_coef)
    solid_sweep(3)

    arrived(t_msgs)
    loop(nx, 4, lambda x: fluid_planes(t1, [x + i for i in range(4)], (0,), put_second))
    gas = rows_of(lambda x: t_out[x, :, 0:128])
    rows_s[...] = product(jnp.concatenate([film, gas], axis=0), select(), ((1,), (1,)))
    row_msgs = [Message(rows_s, rows_r.at[d], d).start() for d in range(4)]

    if fluid_chunks > 1:
        loop(nx, FLUID_STEP, lambda x: fluid_planes(t1, [x + i for i in range(FLUID_STEP)], all_chunks[1:], put_second))
    solid_sweep(4)

    arrived(row_msgs)
    came = bands([rows_r.at[d] for d in range(4)])
    film_in = jnp.concatenate([film * self_mask, came[0:8]], axis=1)
    heat_in = film_in * jnp.concatenate([gas, came[8:16]], axis=1)
    weighed = jnp.concatenate(
        [jnp.concatenate([hot_y[:, 256 * n:256 * n + 256] * v[n:n + 1, :] for n in range(8)], axis=1) for v in (film_in, heat_in)]
        + [jnp.zeros((64, 2048), jnp.float32)], axis=0)
    fb[1, HALO:HALO + nx, :] = product(hot_x[...], weighed, ((1,), (1,)))
    film_msgs = send_near(fb, lambda ref, column, rows: ref.at[column, rows, :])

    solid_sweep(5)

    arrived(film_msgs)
    wide = [widen(fb[0], fb[1], fb[2], f) for f in range(2)]
    diag = wd[...]
    inverse = 1.0 / (diag + wide[0])
    wcf[6, 0] = (wcf[6, 0] * diag + wide[1]) * inverse
    for n in range(6):
        wcf[n, 0] = wcf[n, 0] * diag * inverse
    for n in range(WEDGE_SPLIT):
        wedge_sweep(n)
    solid_sweep(6)
    for n in range(WEDGE_SPLIT, SWEEPS):
        wedge_sweep(n)
    solved = wxa if SWEEPS % 2 == 0 else wxb

    surface = pltpu.roll(solved[0, HALO:HALO + nx, :], 128 - HALO, axis=1)[:, 0:32]
    picked = product(surface, hot_y[...], ((1,), (0,)))
    picked = jnp.sum(picked * hot_x[...], axis=0, keepdims=True)
    for n in range(8):
        slots[n:n + 1, :] = picked[:, 256 * n:256 * n + 256]
    wall_s[...] = slots[:, 128:256]
    wall_msgs = [Message(wall_s, wall_r.at[d], d).start() for d in range(4)]

    def turn_back(x, _):
        cells = jnp.concatenate([solved[0:HALO, pl.ds(HALO + x, 1), :].reshape(HALO, 128), jnp.zeros((128 - HALO, 128), jnp.float32)], axis=0)
        wz[x] = jnp.transpose(cells)[HALO:HALO + ny]
        return 0
    lax.fori_loop(0, nx, turn_back, 0, unroll=2)

    solid_sweep(7)

    arrived(wall_msgs)
    back = bands([wall_r.at[d] for d in (1, 0, 3, 2)])
    rows = (self_mask * slots[:, 0:128] + product(back, select(), ((1,), (0,)))) * live
    rows = jnp.concatenate([jnp.where(lane8 < 16, pltpu.roll(rows, (128 - 16 * n) % 128, axis=1), 0.0) for n in range(8)], axis=0)
    rows = product(rows, compress, ((1,), (1,)))
    for n in range(8):
        wall_out[n:n + 1, :] = jnp.sum(jnp.where(keep, rows[8 * n:8 * n + 8], 0.0), axis=0, keepdims=True)
    for m in list(pending):
        m.sent()


N_MESSAGES = 8 + 12 + 8 + 4 * (SWEEPS - 1) + 4 + 4 + 8 + 4


def on_device(n_blk, n_sub, fluid_temp, velocity, eddy_diff, wall_prev, row_count, owner_table, landing_cell, solid_temp, conductivity, sink, heat_source):
    nx, ny, nz = fluid_temp.shape
    nsz = solid_temp.shape[2]
    f32 = jnp.float32
    any_space = pl.BlockSpec(memory_space=pl.ANY)
    vmem_space = pl.BlockSpec(memory_space=pltpu.VMEM)

    def vmem(*shape):
        return pltpu.VMEM(shape, f32)

    def haloed(depth):
        return vmem(depth // 128, nx + 2, ny + 2 * TOP, 128)

    wide = nx + 2 * HALO
    fluid_new, solid_new, wall_new = pl.pallas_call(
        functools.partial(kernel, n_blk, n_sub),
        out_shape=(
            vmem(nx, ny, nz),
            vmem(nx, ny, nsz),
            jax.ShapeDtypeStruct((8, 128), f32),
        ),
        in_specs=[pl.BlockSpec(memory_space=pltpu.SMEM)] + [any_space] * 7 + [vmem_space] * 3,
        out_specs=(vmem_space,) * 3,
        scratch_shapes=[
            haloed(nz), haloed(nz),
            vmem(nz // 128, nx + 2, ny, 128), vmem(nz // 128, nx, ny + 2 * TOP, 128), vmem(nz // 128, nx, ny, 128),
            haloed(nz), vmem(7, nz // 128, nx, ny, 128), vmem(nx, ny, 128),
            haloed(nsz), haloed(nsz), haloed(nsz), vmem(nsz // 128, nx, ny, 128), vmem(nsz // 128, nx, ny, 128),
            vmem(7, nsz // 128, nx, ny, 128),
            vmem(3, DEEP, wide, 128), vmem(3, wide, 128),
            vmem(DEEP, wide, 128), vmem(7, DEEP, wide, 128),
            vmem(DEEP, wide, 128), vmem(DEEP, wide, 128), vmem(DEEP, wide, 128), vmem(wide, 128), vmem(nx, ny, 128),
            vmem(16, 128), vmem(4, 16, 128), vmem(8, 128), vmem(4, 8, 128),
            vmem(32, 2048), vmem(32, 2048), vmem(8, 256),
            pltpu.SemaphoreType.DMA((6 * nz // 128 + 5 * nsz // 128,)),
            pltpu.SemaphoreType.DMA((N_MESSAGES,)),
            pltpu.SemaphoreType.DMA((N_MESSAGES,)),
        ],
        compiler_params=pltpu.CompilerParams(
            collective_id=0, has_side_effects=True, vmem_limit_bytes=60 * 1024 * 1024
        ),
    )(row_count, fluid_temp, velocity, eddy_diff, solid_temp, conductivity, sink, heat_source, wall_prev.reshape(8, 128), owner_table, landing_cell)
    return fluid_new, solid_new, wall_new.reshape(-1)


def solution(mesh):
    return jax.shard_map(
        functools.partial(on_device, mesh.shape["blk"], mesh.shape["sub"]),
        mesh=mesh,
        in_specs=(
            P("blk", "sub", None),
            P(None, "blk", "sub", None),
            P("blk", "sub", None),
            P(("blk", "sub")),
            P(("blk", "sub")),
            P(("blk", "sub"), None),
            P(("blk", "sub"), None),
            P("blk", "sub", None),
            P("blk", "sub", None),
            P("blk", "sub", None),
            P("blk", "sub", None),
        ),
        out_specs=(P("blk", "sub", None), P("blk", "sub", None), P(("blk", "sub"))),
        check_vma=False,
    )
```

```python
import functools

import jax
import jax.numpy as jnp
from jax import lax
from jax.experimental import pallas as pl
from jax.experimental.pallas import tpu as pltpu
from jax.sharding import PartitionSpec as P

MESH = pl.DeviceIdType.MESH
SWEEPS = 8
HALO = 8
DEEP = 16
TOP = 8
SOLID_STEP = 5
WEDGE_SPLIT = 4
FLUID_STEP = 2
EIG_LOW = 0.02
EIG_HIGH = 2.0
HIGHEST = lax.Precision.HIGHEST
DIRS = ((1, 0), (-1, 0), (0, 1), (0, -1), (1, 1), (1, -1), (-1, 1), (-1, -1))


def cheby_coefficients(count_sweeps):
    center_eig = 0.5 * (EIG_HIGH + EIG_LOW)
    half_width = 0.5 * (EIG_HIGH - EIG_LOW)
    ratio_eig = center_eig / half_width
    damping = 1.0 / ratio_eig
    coefficients = [(0.0, 1.0 / center_eig)]
    for _ in range(1, count_sweeps):
        damping_new = 1.0 / (2.0 * ratio_eig - damping)
        coefficients.append((damping_new * damping, 2.0 * damping_new / half_width))
        damping = damping_new
    return coefficients


def iota(shape, dim):
    return lax.broadcasted_iota(jnp.int32, shape, dim)


def lane_shifts(v):
    lane = iota(v[0].shape, 1)
    low, high = [pltpu.roll(c, 1, axis=1) for c in v], [pltpu.roll(c, 127, axis=1) for c in v]
    below = [low[0]] + [jnp.where(lane == 0, low[c - 1], low[c]) for c in range(1, len(v))]
    above = [jnp.where(lane == 127, high[c + 1], high[c]) for c in range(len(v) - 1)] + [high[-1]]
    return below, above


def face(u, un, a, an):
    total_u, total_a = u + un, a + an
    return total_a + jnp.maximum(total_u, 0.0), total_a - jnp.minimum(total_u, 0.0)


def within(k, kn):
    return 2.0 * k * kn / (k + kn)


def conductance(k, kn):
    total = k + kn
    return 2.0 * k * kn / jnp.where(total > 0.0, total, 1.0)


def kernel(
    n_blk, n_sub,
    count_ref, t_hbm, vel_hbm, a_hbm, x_hbm, k_hbm, e_hbm, q_hbm, wall_ref, owner_ref, land_ref,
    t_out, x_out, wall_out,
    t0, t1, ux, uy, uz, al, cf, sf,
    xa, xb, kc, ec, qc, cs,
    nb, fb, wk, wcf, wxa, wxb, wd, wz,
    rows_s, rows_r, wall_s, wall_r, hot_x, hot_y, hot_x16, hot_y16, slots,
    load_sem, send_sem, recv_sem,
):
    b, s = lax.axis_index("blk"), lax.axis_index("sub")
    nx, ny, _ = t_hbm.shape
    fluid_chunks, solid_chunks = t0.shape[0], xa.shape[0]
    end = TOP + ny
    own_rows, own_planes = slice(TOP, end), slice(1, 1 + nx)
    coefficients = cheby_coefficients(SWEEPS)

    def inside(db, ds):
        ok = None
        for delta, at, count in ((db, b, n_blk), (ds, s, n_sub)):
            if delta:
                this = (at < count - 1) if delta > 0 else (at > 0)
                ok = this if ok is None else ok & this
        return ok

    counter = [0]
    pending = []

    class Message:
        def __init__(self, src, dst, d):
            db, ds = DIRS[d]
            self.n = counter[0]
            counter[0] += 1
            self.make = lambda: pltpu.make_async_remote_copy(
                src_ref=src, dst_ref=dst, send_sem=send_sem.at[self.n], recv_sem=recv_sem.at[self.n],
                device_id=(b + db, s + ds), device_id_type=MESH)
            self.goes, self.comes = inside(db, ds), inside(-db, -ds)

        def start(self):
            @pl.when(self.goes)
            def _():
                self.make().start()
            pending.append(self)
            return self

        def sent(self):
            @pl.when(self.goes)
            def _():
                self.make().wait_send()
            pending.remove(self)

        def arrived(self):
            @pl.when(self.comes)
            def _():
                self.make().wait_recv()

    def send_planes(ref):
        return [Message(ref.at[:, nx if d == 0 else 1, own_rows, :], ref.at[:, 0 if d == 0 else nx + 1, own_rows, :], d).start()
                for d in range(2)]

    def send_rows(ref):
        return [Message(ref.at[:, own_planes, end - 1:end, :], ref.at[:, own_planes, TOP - 1:TOP, :], 2).start(),
                Message(ref.at[:, own_planes, TOP:TOP + 1, :], ref.at[:, own_planes, end:end + 1, :], 3).start()]

    def arrived(messages):
        for m in messages:
            m.arrived()

    loads = {}
    for name, src, dst in (
        ("k", k_hbm, kc), ("x", x_hbm, xa), ("a", a_hbm, al), ("ux", vel_hbm.at[0], ux), ("t", t_hbm, t0), ("uy", vel_hbm.at[1], uy),
        ("e", e_hbm, ec), ("q", q_hbm, qc), ("uz", vel_hbm.at[2], uz),
    ):
        planes = own_planes if dst.shape[1] > nx else slice(0, nx)
        rows = own_rows if dst.shape[2] > ny else slice(0, ny)
        loads[name] = []
        for c in range(dst.shape[0]):
            n = sum(len(v) for v in loads.values())
            copy = pltpu.make_async_copy(src.at[:, :, 128 * c:128 * c + 128], dst.at[c, planes, rows, :], load_sem.at[n])
            copy.start()
            loads[name].append(copy)

    def loaded(*names):
        for name in names:
            for copy in loads[name]:
                copy.wait()

    barrier = pltpu.get_barrier_semaphore()
    for db, ds in DIRS:
        @pl.when(inside(db, ds))
        def _(db=db, ds=ds):
            pl.semaphore_signal(barrier, inc=1, device_id=(b + db, s + ds), device_id_type=MESH)

    def clear(ref, *where):
        ref[where] = jnp.zeros(ref.at[where].shape, jnp.float32)

    for d in range(2):
        @pl.when(jnp.logical_not(inside(-DIRS[d][0], 0)))
        def _(d=d):
            for ref in (t0, t1, al, ux, xa, xb, kc):
                rows = own_rows if ref.shape[2] > ny else slice(0, ny)
                for c in range(ref.shape[0]):
                    clear(ref, c, 0 if d == 0 else nx + 1, rows, slice(None))

        @pl.when(jnp.logical_not(inside(0, -DIRS[2 + d][1])))
        def _(d=d):
            row = TOP - 1 if d == 0 else end

            def body(x, _):
                for ref in (t0, t1, al, uy, xa, xb, kc):
                    for c in range(ref.shape[0]):
                        clear(ref, c, x + (1 if ref.shape[1] > nx else 0), slice(row, row + 1), slice(None))
                return 0
            lax.fori_loop(0, nx, body, 0)
    for d in range(4):
        @pl.when(jnp.logical_not(inside(-DIRS[d][0], -DIRS[d][1])))
        def _(d=d):
            rows_r[d] = jnp.zeros(rows_r.shape[1:], jnp.float32)
            wall_r[d] = jnp.zeros(wall_r.shape[1:], jnp.float32)

    def near_slot(d):
        db, ds = DIRS[d]
        column = {1: 0, 0: 1, -1: 2}[ds]
        if db == 0:
            return column, slice(HALO, HALO + nx), slice(HALO, HALO + nx)
        if db > 0:
            return column, slice(nx, HALO + nx), slice(0, HALO)
        return column, slice(HALO, 2 * HALO), slice(HALO + nx, 2 * HALO + nx)

    for d in range(8):
        @pl.when(jnp.logical_not(inside(-DIRS[d][0], -DIRS[d][1])))
        def _(d=d):
            column, _, rows = near_slot(d)
            height = rows.stop - rows.start
            nb[column, :, rows, :] = jnp.zeros((DEEP, height, 128), jnp.float32)
            fb[column, rows, :] = jnp.zeros((height, 128), jnp.float32)

    def product(x, y, dims):
        return lax.dot_general(x, y, (dims, ((), ())), precision=HIGHEST, preferred_element_type=jnp.float32)

    def pieces(v):
        out = []
        for _ in range(3):
            out.append(v.astype(jnp.bfloat16))
            v = v - out[-1].astype(jnp.float32)
        return out

    def product16(x, y, dims):
        return lax.dot_general(x, y, (dims, ((), ())), preferred_element_type=jnp.float32)

    lane, lane8, sub8 = iota((ny, 128), 1), iota((8, 128), 1), iota((8, 128), 0)
    keep = (lane8 & 7) == sub8
    compress = jnp.where((iota((128, 128), 0) >> 3) == iota((128, 128), 1), 1.0, 0.0)
    flat = [wall_ref[n:n + 1, :] for n in range(8)] + [land_ref[0:1, 128 * n:128 * n + 128].astype(jnp.float32) for n in range(12)]
    packed = product(jnp.concatenate([jnp.where(keep, jnp.broadcast_to(v, (8, 128)), 0.0) for v in flat], axis=0), compress, ((1,), (0,)))

    def gather_rows(first, count):
        total = packed[8 * first:8 * first + 8]
        for n in range(1, count):
            total = total + pltpu.roll(packed[8 * (first + n):8 * (first + n) + 8], 16 * n, axis=1)
        return total

    wall = gather_rows(0, 8)
    land = jnp.concatenate([gather_rows(8, 8), jnp.where(lane8 < 64, gather_rows(16, 4), -1.0)], axis=1).astype(jnp.int32)
    live = jnp.where(lane8 * 8 + sub8 < count_ref[0], 1.0, 0.0)
    owner = jnp.broadcast_to(owner_ref[...], (8, 128))
    self_mask = jnp.where(owner == 0, 1.0, 0.0)
    match = jnp.where((owner == sub8 + 1) & (sub8 < 4), 1.0, 0.0)
    before = jnp.where(iota((128, 128), 0) < iota((128, 128), 1), 1.0, 0.0)
    rank = product(match, before, ((1,), (0,)))
    place = jnp.sum(match * (rank + (sub8 * 16 + 1).astype(jnp.float32)), axis=0, keepdims=True) - 1.0
    row32 = iota((32, 256), 0)
    for n in range(8):
        cell = land[n:n + 1, :]
        at = slice(256 * n, 256 * n + 256)
        hot_x[:, at] = jnp.where((cell >> 5) == row32, 1.0, 0.0)
        hot_y[:, at] = jnp.where(((cell & 31) == row32) & (cell >= 0), 1.0, 0.0)
        hot_x16[:, at] = hot_x[:, at].astype(jnp.bfloat16)
        hot_y16[:, at] = hot_y[:, at].astype(jnp.bfloat16)

    def select():
        return jnp.where(iota((128, 128), 0).astype(jnp.float32) == place, 1.0, 0.0)

    near = (b > 0).astype(jnp.int32) + (b < n_blk - 1).astype(jnp.int32)
    side = (s > 0).astype(jnp.int32) + (s < n_sub - 1).astype(jnp.int32)
    pl.semaphore_wait(barrier, near + side + near * side)

    loaded("k", "x")
    k_x, x_x = send_planes(kc), send_planes(xa)
    k_y, x_y = send_rows(kc), send_rows(xa)
    loaded("a", "ux", "t")
    a_x = send_planes(al)
    loaded("uy")
    a_y, t_y = send_rows(al), send_rows(t0)
    u_y = [Message(uy.at[:, :, end - 1:end, :], uy.at[:, :, TOP - 1:TOP, :], 2).start(),
           Message(uy.at[:, :, TOP:TOP + 1, :], uy.at[:, :, end:end + 1, :], 3).start()]

    def turn(x, _):
        tile = jnp.concatenate([xa[0, x + 1, own_rows, :], kc[0, x + 1, own_rows, :], ec[0, x], qc[0, x]], axis=0)
        nb[1, :, pl.ds(HALO + x, 1), :] = jnp.transpose(tile)[0:DEEP].reshape(DEEP, 1, 128)
        return 0

    def send_near(column_ref, part):
        messages = []
        for d in range(8):
            column, out_rows, rows = near_slot(d)
            messages.append(Message(part(column_ref, 1, out_rows), part(column_ref, column, rows), d).start())
        return messages

    def solid_coef(x, count):
        k = [[kc[c, x + i, own_rows, :] for c in range(solid_chunks)] for i in range(count + 2)]
        out = []
        for i in range(count):
            here, under, over = k[i + 1], k[i], k[i + 2]
            zm, _ = lane_shifts(here)
            gz = [within(here[c], zm[c]) for c in range(solid_chunks)]
            gz[0] = jnp.where(lane == 0, 0.0, gz[0])
            _, gz_up = lane_shifts(gz)
            gz_up[-1] = jnp.where(lane == 127, 0.0, gz_up[-1])
            for c in range(solid_chunks):
                g = [within(here[c], under[c]), within(here[c], over[c]),
                     within(here[c], kc[c, x + i + 1, TOP - 1:end - 1, :]), within(here[c], kc[c, x + i + 1, TOP + 1:end + 1, :]),
                     gz[c], gz_up[c]]
                inverse = 1.0 / (((g[0] + g[1]) + (g[2] + g[3])) + ((g[4] + g[5]) + ec[c, x + i]))
                out.append((c, x + i, [v * inverse for v in g] + [qc[c, x + i] * inverse]))
        for c, at, values in out:
            for n in range(7):
                cs[n, c, at] = values[n]

    def solid_planes(n, src, dst, runs):
        decay, gain = coefficients[n]
        out = []
        for x, count in runs:
            v = [[src[c, x + i, own_rows, :] for c in range(solid_chunks)] for i in range(count + 2)]
            for i in range(count):
                zm, zp = lane_shifts(v[i + 1])
                for c in range(solid_chunks):
                    at = x + i
                    r = ((cs[0, c, at] * v[i][c] + cs[1, c, at] * v[i + 2][c])
                         + (cs[2, c, at] * src[c, at + 1, TOP - 1:end - 1, :] + cs[3, c, at] * src[c, at + 1, TOP + 1:end + 1, :]))
                    r = r + (cs[4, c, at] * zm[c] + cs[5, c, at] * zp[c]) + cs[6, c, at]
                    new = (1.0 + decay - gain) * v[i + 1][c] + gain * r
                    if n > 0:
                        new = new - decay * dst[c, at + 1, own_rows, :]
                    if n == SWEEPS - 1 and c == 0:
                        new = jnp.where(lane < HALO, wz[at], new)
                    out.append((c, at, new))
        for c, at, new in out:
            if n == SWEEPS - 1:
                x_out[at, :, 128 * c:128 * c + 128] = new
            else:
                dst[c, at + 1, own_rows, :] = new

    solid_sends = [(-1, m) for m in x_x + x_y]
    solid_waits = [x_x + x_y]
    interior = nx - 2

    def loop(count, step, work):
        def body(i, _):
            work(i * step)
            return 0
        lax.fori_loop(0, count // step, body, 0)

    def solid_sweep(n):
        src, dst = (xa, xb) if n % 2 == 0 else (xb, xa)
        arrived(solid_waits.pop())
        for m in list(solid_sends):
            if m[0] <= n - 2:
                m[1].sent()
                solid_sends.remove(m)
        solid_planes(n, src, dst, [(0, 1), (nx - 1, 1)])
        msgs = send_planes(dst) if n < SWEEPS - 1 else []
        loop(interior, SOLID_STEP, lambda x: solid_planes(n, src, dst, [(1 + x, SOLID_STEP)]))
        if n < SWEEPS - 1:
            msgs += send_rows(dst)
        solid_sends.extend((n, m) for m in msgs)
        solid_waits.append(msgs)

    mirror = 1.0 - 2.0 * live
    source = 2.0 * live * wall

    def columns(v, x):
        return jnp.concatenate([pltpu.roll(v, lax.rem(128 - (x * 4 + j), 128), axis=1) for j in range(4)], axis=0)

    def rows_of(plane):
        def body(i, parts):
            parts = list(parts)
            for k in range(4):
                v = plane(4 * i + k)
                for j in range(4):
                    parts[j] = jnp.where(lane8 == (4 * i + k) * 4 + j, jnp.broadcast_to(v[8 * j:8 * j + 8, 0:1], (8, 128)), parts[j])
            return tuple(parts)
        parts = lax.fori_loop(0, nx // 4, body, (jnp.zeros((8, 128), jnp.float32),) * 4)
        return (parts[0] + parts[1]) + (parts[2] + parts[3])

    top = fluid_chunks - 1

    def fluid_coef(x):
        a = [al[c, x + 1, own_rows, :] for c in range(fluid_chunks)]
        u = [uz[c, x] for c in range(fluid_chunks)]
        am, _ = lane_shifts(a)
        um, _ = lane_shifts(u)
        am[0] = jnp.where(lane == 0, a[0], am[0])
        um[0] = jnp.where(lane == 0, -u[0], um[0])
        z = [face(u[c], um[c], a[c], am[c]) for c in range(fluid_chunks)]
        _, pz = lane_shifts([v[0] for v in z])
        _, qz = lane_shifts([v[1] for v in z])
        last = face(u[top], u[top], a[top], a[top])
        pz[top] = jnp.where(lane == 127, last[0], pz[top])
        qz[top] = jnp.where(lane == 127, last[1], qz[top])
        for c in range(fluid_chunks):
            v = ux[c, x + 1]
            p_xm, q_xm = face(v, ux[c, x], a[c], al[c, x, own_rows, :])
            p_xp, q_xp = face(v, ux[c, x + 2], a[c], al[c, x + 2, own_rows, :])
            v = uy[c, x, own_rows, :]
            p_ym, q_ym = face(v, uy[c, x, TOP - 1:end - 1, :], a[c], al[c, x + 1, TOP - 1:end - 1, :])
            p_yp, q_yp = face(v, uy[c, x, TOP + 1:end + 1, :], a[c], al[c, x + 1, TOP + 1:end + 1, :])
            p_zm, q_zm = z[c]
            away = ((q_xm + p_xp) + (q_ym + p_yp)) + (q_zm + pz[c])
            toward = ((p_xm + q_xp) + (p_ym + q_yp)) + (p_zm + qz[c])
            scale = 1.6 / (away + toward)
            cf[0, c, x] = p_xm * scale
            cf[1, c, x] = q_xp * scale
            cf[2, c, x] = p_ym * scale
            cf[3, c, x] = q_yp * scale
            below, above, centre = p_zm * scale, qz[c] * scale, 1.0 - away * scale
            if c == 0:
                first = lane == 0
                at_wall = jnp.where(first, below, 0.0)
                sf[x] = at_wall * columns(source, x)
                centre = centre + at_wall * columns(mirror, x)
                below = jnp.where(first, 0.0, below)
            if c == top:
                above = jnp.where(lane == 127, 0.0, above)
            cf[4, c, x] = below
            cf[5, c, x] = above
            cf[6, c, x] = centre

    def fluid_planes(src, xs, chunks, put):
        out = []
        for x in xs:
            held = {}

            def rolled(c, shift, held=held, x=x):
                if (c, shift) not in held:
                    held[c, shift] = pltpu.roll(src[c, x + 1, own_rows, :], shift, axis=1)
                return held[c, shift]

            for c in chunks:
                zm = rolled(c, 1) if c == 0 else jnp.where(lane == 0, rolled(c - 1, 1), rolled(c, 1))
                zp = rolled(c, 127) if c == top else jnp.where(lane == 127, rolled(c + 1, 127), rolled(c, 127))
                new = ((cf[0, c, x] * src[c, x, own_rows, :] + cf[1, c, x] * src[c, x + 2, own_rows, :])
                       + (cf[2, c, x] * src[c, x + 1, TOP - 1:end - 1, :] + cf[3, c, x] * src[c, x + 1, TOP + 1:end + 1, :]))
                new = new + (cf[4, c, x] * zm + cf[5, c, x] * zp) + cf[6, c, x] * src[c, x + 1, own_rows, :]
                out.append((c, x, new + sf[x] if c == 0 else new))
        for item in out:
            put(*item)

    def put_first(c, x, new):
        t1[c, x + 1, own_rows, :] = new

    def put_second(c, x, new):
        t_out[x, :, 128 * c:128 * c + 128] = new

    lane_w = iota((nx + 2 * HALO, 128), 1)

    def widen(left, mid, right, f):
        left = pltpu.roll(left, (128 - 32 * f - 24) % 128, axis=1)
        mid = pltpu.roll(mid, (128 + HALO - 32 * f) % 128, axis=1)
        right = pltpu.roll(right, (128 + 40 - 32 * f) % 128, axis=1)
        return jnp.where(lane_w < HALO, left, jnp.where(lane_w < HALO + ny, mid, jnp.where(lane_w < 2 * HALO + ny, right, 0.0)))

    def near_field(z, f):
        return widen(nb[0, z], nb[1, z], nb[2, z], f)

    def shift_all(v):
        n = v.shape[0]
        return [pltpu.roll(v, 1, axis=0), pltpu.roll(v, n - 1, axis=0), pltpu.roll(v, 1, axis=1), pltpu.roll(v, 127, axis=1)]

    def spread_near(z):
        wk[z] = near_field(z, 1)
        wxa[z] = near_field(z, 0)

    def wedge_coef(z):
        k = wk[z]
        under = wk[jnp.maximum(z - 1, 0)] * (z > 0).astype(jnp.float32)
        over = wk[jnp.minimum(z + 1, DEEP - 1)] * (z < DEEP - 1).astype(jnp.float32)
        g = [conductance(k, kn) for kn in shift_all(k) + [under, over]]
        diag = ((g[0] + g[1]) + (g[2] + g[3])) + ((g[4] + g[5]) + near_field(z, 2))
        diag = jnp.where(diag > 0.0, diag, 1.0)
        inverse = 1.0 / diag
        for n in range(6):
            wcf[n, z] = g[n] * inverse
        wcf[6, z] = near_field(z, 3) * inverse
        wd[z] = diag

    def wedge_sweep(n):
        decay, gain = coefficients[n]
        src, dst = (wxa, wxb) if n % 2 == 0 else (wxb, wxa)

        def level(z):
            v = src[z]
            near_v = shift_all(v) + [src[jnp.maximum(z - 1, 0)], src[z + 1]]
            r = (wcf[0, z] * near_v[0] + wcf[1, z] * near_v[1]) + (wcf[2, z] * near_v[2] + wcf[3, z] * near_v[3])
            r = r + (wcf[4, z] * near_v[4] + wcf[5, z] * near_v[5]) + wcf[6, z]
            new = (1.0 + decay - gain) * v + gain * r
            return new if n == 0 else new - decay * dst[z]

        def levels(z, step):
            for k, new in enumerate([level(z + k) for k in range(step)]):
                dst[z + k] = new

        count = DEEP - 1 - n
        step = 3 if count % 3 == 0 else 2
        loop(count - count % step, step, lambda z: levels(z, step))
        if count % step:
            levels(count - count % step, count % step)

    def bands(refs):
        total = None
        for band, ref in enumerate(refs):
            v = ref[...]
            at = iota(v.shape, 1)
            v = jnp.where((at >= 16 * band) & (at < 16 * band + 16), v, 0.0)
            total = v if total is None else total + v
        return total

    def drain():
        recent = [m for n, m in solid_sends if n >= 0]
        for m in [m for m in pending if m not in recent and m not in held_back]:
            m.sent()

    held_back = []

    all_chunks = range(fluid_chunks)
    loaded("e", "q")
    lax.fori_loop(0, nx, turn, 0, unroll=2)
    film = 2.0 * live * rows_of(lambda x: al[0, x + 1, own_rows, :])
    arrived(k_y)
    loop(interior, 2, lambda x: solid_coef(1 + x, 2))
    arrived(k_x)
    solid_coef(0, 1)
    solid_coef(nx - 1, 1)
    solid_sweep(0)
    u_x = [Message(ux.at[:, nx if d == 0 else 1], ux.at[:, 0 if d == 0 else nx + 1], d).start() for d in range(2)]
    t_x = send_planes(t0)

    loaded("uz")
    arrived(a_y + u_y)
    half = interior // 2
    loop(half, 1, lambda x: fluid_coef(1 + x))
    solid_sweep(1)
    near_msgs = send_near(nb, lambda ref, column, rows: ref.at[column, :, rows, :])
    loop(interior - half, 1, lambda x: fluid_coef(1 + half + x))
    arrived(a_x + u_x)
    fluid_coef(0)
    fluid_coef(nx - 1)

    arrived(t_x + t_y)
    fluid_planes(t0, (0, nx - 1), all_chunks, put_first)
    t_msgs = send_planes(t1)
    loop(interior, FLUID_STEP, lambda x: fluid_planes(t0, [1 + x + i for i in range(FLUID_STEP)], all_chunks, put_first))
    t_msgs += send_rows(t1)
    solid_sweep(2)

    arrived(near_msgs)
    loop(DEEP, 2, lambda z: [spread_near(z), spread_near(z + 1)])
    loop(DEEP, 2, lambda z: [wedge_coef(z), wedge_coef(z + 1)])
    solid_sweep(3)

    arrived(t_msgs)
    loop(nx, 4, lambda x: fluid_planes(t1, [x + i for i in range(4)], (0,), put_second))
    gas = rows_of(lambda x: t_out[x, :, 0:128])
    rows_s[...] = product(jnp.concatenate([film, gas], axis=0), select(), ((1,), (1,)))
    row_msgs = [Message(rows_s, rows_r.at[d], d).start() for d in range(4)]

    if fluid_chunks > 1:
        loop(nx, FLUID_STEP, lambda x: fluid_planes(t1, [x + i for i in range(FLUID_STEP)], all_chunks[1:], put_second))
    solid_sweep(4)

    solid_sends[:] = [item for item in solid_sends if item[0] >= 0]
    held_back.extend(row_msgs)
    drain()
    arrived(row_msgs)
    came = bands([rows_r.at[d] for d in range(4)])
    film_in = jnp.concatenate([film * self_mask, came[0:8]], axis=1)
    heat_in = film_in * jnp.concatenate([gas, came[8:16]], axis=1)
    sums = None
    for film_piece, heat_piece in zip(pieces(film_in), pieces(heat_in)):
        weighed = jnp.concatenate(
            [jnp.concatenate([hot_y[:, 256 * n:256 * n + 256] * v[n:n + 1, :] for n in range(8)], axis=1)
             for v in (film_piece.astype(jnp.float32), heat_piece.astype(jnp.float32))], axis=0).astype(jnp.bfloat16)
        part = product16(hot_x16[...], weighed, ((1,), (1,)))
        sums = part if sums is None else sums + part
    fb[1, HALO:HALO + nx, :] = jnp.concatenate([sums, jnp.zeros((nx, 64), jnp.float32)], axis=1)
    film_msgs = send_near(fb, lambda ref, column, rows: ref.at[column, rows, :])

    solid_sweep(5)

    held_back[:] = film_msgs
    drain()
    arrived(film_msgs)
    wide = [widen(fb[0], fb[1], fb[2], f) for f in range(2)]
    diag = wd[0]
    inverse = 1.0 / (diag + wide[0])
    wcf[6, 0] = (wcf[6, 0] * diag + wide[1]) * inverse
    for n in range(6):
        wcf[n, 0] = wcf[n, 0] * diag * inverse
    for n in range(WEDGE_SPLIT):
        wedge_sweep(n)
    solid_sweep(6)
    for n in range(WEDGE_SPLIT, SWEEPS):
        wedge_sweep(n)
    solved = wxa if SWEEPS % 2 == 0 else wxb

    surface = pltpu.roll(solved[0, HALO:HALO + nx, :], 128 - HALO, axis=1)[:, 0:32]
    picked = product16(jnp.concatenate(pieces(surface), axis=0), hot_y16[...], ((1,), (0,)))
    picked = (picked[0:nx] + picked[nx:2 * nx]) + picked[2 * nx:3 * nx]
    picked = jnp.sum(picked * hot_x[...], axis=0, keepdims=True)
    for n in range(8):
        slots[n:n + 1, :] = picked[:, 256 * n:256 * n + 256]
    wall_s[...] = slots[:, 128:256]
    wall_msgs = [Message(wall_s, wall_r.at[d], d).start() for d in range(4)]

    def turn_back(x, _):
        cells = jnp.concatenate([solved[0:HALO, pl.ds(HALO + x, 1), :].reshape(HALO, 128), jnp.zeros((128 - HALO, 128), jnp.float32)], axis=0)
        wz[x] = jnp.transpose(cells)[HALO:HALO + ny]
        return 0
    lax.fori_loop(0, nx, turn_back, 0, unroll=2)

    solid_sweep(7)

    arrived(wall_msgs)
    back = bands([wall_r.at[d] for d in (1, 0, 3, 2)])
    rows = (self_mask * slots[:, 0:128] + product(back, select(), ((1,), (0,)))) * live
    rows = jnp.concatenate([jnp.where(lane8 < 16, pltpu.roll(rows, (128 - 16 * n) % 128, axis=1), 0.0) for n in range(8)], axis=0)
    rows = product(rows, compress, ((1,), (1,)))
    for n in range(8):
        wall_out[n:n + 1, :] = jnp.sum(jnp.where(keep, rows[8 * n:8 * n + 8], 0.0), axis=0, keepdims=True)
    for m in list(pending):
        m.sent()


N_MESSAGES = 8 + 12 + 8 + 4 * (SWEEPS - 1) + 4 + 4 + 8 + 4


def on_device(n_blk, n_sub, fluid_temp, velocity, eddy_diff, wall_prev, row_count, owner_table, landing_cell, solid_temp, conductivity, sink, heat_source):
    nx, ny, nz = fluid_temp.shape
    nsz = solid_temp.shape[2]
    f32 = jnp.float32
    any_space = pl.BlockSpec(memory_space=pl.ANY)
    vmem_space = pl.BlockSpec(memory_space=pltpu.VMEM)

    def vmem(*shape):
        return pltpu.VMEM(shape, f32)

    def haloed(depth):
        return vmem(depth // 128, nx + 2, ny + 2 * TOP, 128)

    wide = nx + 2 * HALO
    fluid_new, solid_new, wall_new = pl.pallas_call(
        functools.partial(kernel, n_blk, n_sub),
        out_shape=(
            vmem(nx, ny, nz),
            vmem(nx, ny, nsz),
            jax.ShapeDtypeStruct((8, 128), f32),
        ),
        in_specs=[pl.BlockSpec(memory_space=pltpu.SMEM)] + [any_space] * 7 + [vmem_space] * 3,
        out_specs=(vmem_space,) * 3,
        scratch_shapes=[
            haloed(nz), haloed(nz),
            vmem(nz // 128, nx + 2, ny, 128), vmem(nz // 128, nx, ny + 2 * TOP, 128), vmem(nz // 128, nx, ny, 128),
            haloed(nz), vmem(7, nz // 128, nx, ny, 128), vmem(nx, ny, 128),
            haloed(nsz), haloed(nsz), haloed(nsz), vmem(nsz // 128, nx, ny, 128), vmem(nsz // 128, nx, ny, 128),
            vmem(7, nsz // 128, nx, ny, 128),
            vmem(3, DEEP, wide, 128), vmem(3, wide, 128),
            vmem(DEEP, wide, 128), vmem(7, DEEP, wide, 128),
            vmem(DEEP, wide, 128), vmem(DEEP, wide, 128), vmem(DEEP, wide, 128), vmem(nx, ny, 128),
            vmem(16, 128), vmem(4, 16, 128), vmem(8, 128), vmem(4, 8, 128),
            vmem(32, 2048), vmem(32, 2048),
            pltpu.VMEM((32, 2048), jnp.bfloat16), pltpu.VMEM((32, 2048), jnp.bfloat16), vmem(8, 256),
            pltpu.SemaphoreType.DMA((6 * nz // 128 + 5 * nsz // 128,)),
            pltpu.SemaphoreType.DMA((N_MESSAGES,)),
            pltpu.SemaphoreType.DMA((N_MESSAGES,)),
        ],
        compiler_params=pltpu.CompilerParams(
            collective_id=0, has_side_effects=True, vmem_limit_bytes=60 * 1024 * 1024
        ),
    )(row_count, fluid_temp, velocity, eddy_diff, solid_temp, conductivity, sink, heat_source, wall_prev.reshape(8, 128), owner_table, landing_cell)
    return fluid_new, solid_new, wall_new.reshape(-1)


def solution(mesh):
    return jax.shard_map(
        functools.partial(on_device, mesh.shape["blk"], mesh.shape["sub"]),
        mesh=mesh,
        in_specs=(
            P("blk", "sub", None),
            P(None, "blk", "sub", None),
            P("blk", "sub", None),
            P(("blk", "sub")),
            P(("blk", "sub")),
            P(("blk", "sub"), None),
            P(("blk", "sub"), None),
            P("blk", "sub", None),
            P("blk", "sub", None),
            P("blk", "sub", None),
            P("blk", "sub", None),
        ),
        out_specs=(P("blk", "sub", None), P("blk", "sub", None), P(("blk", "sub"))),
        check_vma=False,
    )
```

```python
import functools

import jax
import jax.numpy as jnp
from jax import lax
from jax.experimental import pallas as pl
from jax.experimental.pallas import tpu as pltpu
from jax.sharding import PartitionSpec as P

MESH = pl.DeviceIdType.MESH
SWEEPS = 8
HALO = 8
DEEP = 16
TOP = 8
SOLID_STEP = 10
WEDGE_SPLIT = 5
COEF_CUTS = (0, 14, 26, 30)
FLUID_STEP = 5
COEF_STEP = 2
EIG_LOW = 0.02
EIG_HIGH = 2.0
HIGHEST = lax.Precision.HIGHEST
DIRS = ((1, 0), (-1, 0), (0, 1), (0, -1), (1, 1), (1, -1), (-1, 1), (-1, -1))


def cheby_coefficients(count_sweeps):
    center_eig = 0.5 * (EIG_HIGH + EIG_LOW)
    half_width = 0.5 * (EIG_HIGH - EIG_LOW)
    ratio_eig = center_eig / half_width
    damping = 1.0 / ratio_eig
    coefficients = [(0.0, 1.0 / center_eig)]
    for _ in range(1, count_sweeps):
        damping_new = 1.0 / (2.0 * ratio_eig - damping)
        coefficients.append((damping_new * damping, 2.0 * damping_new / half_width))
        damping = damping_new
    return coefficients


def iota(shape, dim):
    return lax.broadcasted_iota(jnp.int32, shape, dim)


def lane_shifts(v):
    lane = iota(v[0].shape, 1)
    low, high = [pltpu.roll(c, 1, axis=1) for c in v], [pltpu.roll(c, 127, axis=1) for c in v]
    below = [low[0]] + [jnp.where(lane == 0, low[c - 1], low[c]) for c in range(1, len(v))]
    above = [jnp.where(lane == 127, high[c + 1], high[c]) for c in range(len(v) - 1)] + [high[-1]]
    return below, above


def face(u, un, a, an):
    total_u, total_a = u + un, a + an
    return total_a + jnp.maximum(total_u, 0.0), total_a - jnp.minimum(total_u, 0.0)


def within(k, kn):
    return 2.0 * k * kn / (k + kn)


def conductance(k, kn):
    total = k + kn
    return 2.0 * k * kn / jnp.where(total > 0.0, total, 1.0)


def kernel(
    n_blk, n_sub,
    count_ref, t_hbm, vel_hbm, a_hbm, x_hbm, k_hbm, e_hbm, q_hbm, wall_ref, owner_ref, land_ref,
    t_out, x_out, wall_out,
    t0, t1, ux, uy, uz, al, cf, sf,
    xa, xb, kc, ec, qc, cs,
    nb, fb, wk, wcf, wxa, wxb, wd, wz,
    rows_s, rows_r, wall_s, wall_r, hot_x, hot_y, hot_x16, hot_y16, slots,
    load_sem, send_sem, recv_sem,
):
    b, s = lax.axis_index("blk"), lax.axis_index("sub")
    nx, ny, _ = t_hbm.shape
    fluid_chunks, solid_chunks = t0.shape[0], xa.shape[0]
    end = TOP + ny
    own_rows, own_planes = slice(TOP, end), slice(1, 1 + nx)
    coefficients = cheby_coefficients(SWEEPS)

    def inside(db, ds):
        ok = None
        for delta, at, count in ((db, b, n_blk), (ds, s, n_sub)):
            if delta:
                this = (at < count - 1) if delta > 0 else (at > 0)
                ok = this if ok is None else ok & this
        return ok

    counter = [0]
    pending = []

    class Message:
        def __init__(self, src, dst, d):
            db, ds = DIRS[d]
            self.n = counter[0]
            counter[0] += 1
            self.make = lambda: pltpu.make_async_remote_copy(
                src_ref=src, dst_ref=dst, send_sem=send_sem.at[self.n], recv_sem=recv_sem.at[self.n],
                device_id=(b + db, s + ds), device_id_type=MESH)
            self.goes, self.comes = inside(db, ds), inside(-db, -ds)

        def start(self):
            @pl.when(self.goes)
            def _():
                self.make().start()
            pending.append(self)
            return self

        def sent(self):
            @pl.when(self.goes)
            def _():
                self.make().wait_send()
            pending.remove(self)

        def arrived(self):
            @pl.when(self.comes)
            def _():
                self.make().wait_recv()

    def send_planes(ref):
        return [Message(ref.at[:, nx if d == 0 else 1, own_rows, :], ref.at[:, 0 if d == 0 else nx + 1, own_rows, :], d).start()
                for d in range(2)]

    def send_rows(ref):
        return [Message(ref.at[:, own_planes, end - 1:end, :], ref.at[:, own_planes, TOP - 1:TOP, :], 2).start(),
                Message(ref.at[:, own_planes, TOP:TOP + 1, :], ref.at[:, own_planes, end:end + 1, :], 3).start()]

    def arrived(messages):
        for m in messages:
            m.arrived()

    loads = {}
    for name, src, dst in (
        ("k", k_hbm, kc), ("x", x_hbm, xa), ("a", a_hbm, al), ("ux", vel_hbm.at[0], ux), ("t", t_hbm, t0), ("uy", vel_hbm.at[1], uy),
        ("e", e_hbm, ec), ("q", q_hbm, qc), ("uz", vel_hbm.at[2], uz),
    ):
        planes = own_planes if dst.shape[1] > nx else slice(0, nx)
        rows = own_rows if dst.shape[2] > ny else slice(0, ny)
        loads[name] = []
        for c in range(dst.shape[0]):
            n = sum(len(v) for v in loads.values())
            copy = pltpu.make_async_copy(src.at[:, :, 128 * c:128 * c + 128], dst.at[c, planes, rows, :], load_sem.at[n])
            copy.start()
            loads[name].append(copy)

    def loaded(*names):
        for name in names:
            for copy in loads[name]:
                copy.wait()

    barrier = pltpu.get_barrier_semaphore()
    for db, ds in DIRS:
        @pl.when(inside(db, ds))
        def _(db=db, ds=ds):
            pl.semaphore_signal(barrier, inc=1, device_id=(b + db, s + ds), device_id_type=MESH)

    def clear(ref, *where):
        ref[where] = jnp.zeros(ref.at[where].shape, jnp.float32)

    for d in range(2):
        @pl.when(jnp.logical_not(inside(-DIRS[d][0], 0)))
        def _(d=d):
            for ref in (t0, t1, al, ux, xa, xb, kc):
                rows = own_rows if ref.shape[2] > ny else slice(0, ny)
                for c in range(ref.shape[0]):
                    clear(ref, c, 0 if d == 0 else nx + 1, rows, slice(None))

        @pl.when(jnp.logical_not(inside(0, -DIRS[2 + d][1])))
        def _(d=d):
            row = TOP - 1 if d == 0 else end

            def body(x, _):
                for ref in (t0, t1, al, uy, xa, xb, kc):
                    for c in range(ref.shape[0]):
                        clear(ref, c, x + (1 if ref.shape[1] > nx else 0), slice(row, row + 1), slice(None))
                return 0
            lax.fori_loop(0, nx, body, 0)
    for d in range(4):
        @pl.when(jnp.logical_not(inside(-DIRS[d][0], -DIRS[d][1])))
        def _(d=d):
            rows_r[d] = jnp.zeros(rows_r.shape[1:], jnp.float32)
            wall_r[d] = jnp.zeros(wall_r.shape[1:], jnp.float32)

    def near_slot(d):
        db, ds = DIRS[d]
        column = {1: 0, 0: 1, -1: 2}[ds]
        if db == 0:
            return column, slice(HALO, HALO + nx), slice(HALO, HALO + nx)
        if db > 0:
            return column, slice(nx, HALO + nx), slice(0, HALO)
        return column, slice(HALO, 2 * HALO), slice(HALO + nx, 2 * HALO + nx)

    for d in range(8):
        @pl.when(jnp.logical_not(inside(-DIRS[d][0], -DIRS[d][1])))
        def _(d=d):
            column, _, rows = near_slot(d)
            height = rows.stop - rows.start
            nb[column, :, rows, :] = jnp.zeros((DEEP, height, 128), jnp.float32)
            fb[column, rows, :] = jnp.zeros((height, 128), jnp.float32)

    def product(x, y, dims):
        return lax.dot_general(x, y, (dims, ((), ())), precision=HIGHEST, preferred_element_type=jnp.float32)

    def pieces(v):
        out = []
        for _ in range(3):
            out.append(v.astype(jnp.bfloat16))
            v = v - out[-1].astype(jnp.float32)
        return out

    def product16(x, y, dims):
        return lax.dot_general(x, y, (dims, ((), ())), preferred_element_type=jnp.float32)

    lane, lane8, sub8 = iota((ny, 128), 1), iota((8, 128), 1), iota((8, 128), 0)
    keep = (lane8 & 7) == sub8
    compress = jnp.where((iota((128, 128), 0) >> 3) == iota((128, 128), 1), 1.0, 0.0)
    flat = [wall_ref[n:n + 1, :] for n in range(8)] + [land_ref[0:1, 128 * n:128 * n + 128].astype(jnp.float32) for n in range(12)]
    packed = product(jnp.concatenate([jnp.where(keep, jnp.broadcast_to(v, (8, 128)), 0.0) for v in flat], axis=0), compress, ((1,), (0,)))

    def gather_rows(first, count):
        total = packed[8 * first:8 * first + 8]
        for n in range(1, count):
            total = total + pltpu.roll(packed[8 * (first + n):8 * (first + n) + 8], 16 * n, axis=1)
        return total

    wall = gather_rows(0, 8)
    land = jnp.concatenate([gather_rows(8, 8), jnp.where(lane8 < 64, gather_rows(16, 4), -1.0)], axis=1).astype(jnp.int32)
    live = jnp.where(lane8 * 8 + sub8 < count_ref[0], 1.0, 0.0)
    owner = jnp.broadcast_to(owner_ref[...], (8, 128))
    self_mask = jnp.where(owner == 0, 1.0, 0.0)
    match = jnp.where((owner == sub8 + 1) & (sub8 < 4), 1.0, 0.0)
    before = jnp.where(iota((128, 128), 0) < iota((128, 128), 1), 1.0, 0.0)
    rank = product(match, before, ((1,), (0,)))
    place = jnp.sum(match * (rank + (sub8 * 16 + 1).astype(jnp.float32)), axis=0, keepdims=True) - 1.0
    row32 = iota((32, 256), 0)
    for n in range(8):
        cell = land[n:n + 1, :]
        at = slice(256 * n, 256 * n + 256)
        hot_x[:, at] = jnp.where((cell >> 5) == row32, 1.0, 0.0)
        hot_y[:, at] = jnp.where(((cell & 31) == row32) & (cell >= 0), 1.0, 0.0)
        hot_x16[:, at] = hot_x[:, at].astype(jnp.bfloat16)
        hot_y16[:, at] = hot_y[:, at].astype(jnp.bfloat16)

    def select():
        return jnp.where(iota((128, 128), 0).astype(jnp.float32) == place, 1.0, 0.0)

    near = (b > 0).astype(jnp.int32) + (b < n_blk - 1).astype(jnp.int32)
    side = (s > 0).astype(jnp.int32) + (s < n_sub - 1).astype(jnp.int32)
    pl.semaphore_wait(barrier, near + side + near * side)

    loaded("k", "x")
    k_x, x_x = send_planes(kc), send_planes(xa)
    k_y, x_y = send_rows(kc), send_rows(xa)
    loaded("a", "ux", "t")
    a_x = send_planes(al)
    loaded("uy")
    a_y, t_y = send_rows(al), send_rows(t0)
    u_y = [Message(uy.at[:, :, end - 1:end, :], uy.at[:, :, TOP - 1:TOP, :], 2).start(),
           Message(uy.at[:, :, TOP:TOP + 1, :], uy.at[:, :, end:end + 1, :], 3).start()]

    def turn(x, _):
        tile = jnp.concatenate([xa[0, x + 1, own_rows, :], kc[0, x + 1, own_rows, :], ec[0, x], qc[0, x]], axis=0)
        nb[1, :, pl.ds(HALO + x, 1), :] = jnp.transpose(tile)[0:DEEP].reshape(DEEP, 1, 128)
        return 0

    def send_near(column_ref, part):
        messages = []
        for d in range(8):
            column, out_rows, rows = near_slot(d)
            messages.append(Message(part(column_ref, 1, out_rows), part(column_ref, column, rows), d).start())
        return messages

    def solid_coef(x, count):
        k = [[kc[c, x + i, own_rows, :] for c in range(solid_chunks)] for i in range(count + 2)]
        out = []
        for i in range(count):
            here, under, over = k[i + 1], k[i], k[i + 2]
            zm, _ = lane_shifts(here)
            gz = [within(here[c], zm[c]) for c in range(solid_chunks)]
            gz[0] = jnp.where(lane == 0, 0.0, gz[0])
            _, gz_up = lane_shifts(gz)
            gz_up[-1] = jnp.where(lane == 127, 0.0, gz_up[-1])
            for c in range(solid_chunks):
                g = [within(here[c], under[c]), within(here[c], over[c]),
                     within(here[c], kc[c, x + i + 1, TOP - 1:end - 1, :]), within(here[c], kc[c, x + i + 1, TOP + 1:end + 1, :]),
                     gz[c], gz_up[c]]
                inverse = 1.0 / (((g[0] + g[1]) + (g[2] + g[3])) + ((g[4] + g[5]) + ec[c, x + i]))
                out.append((c, x + i, [v * inverse for v in g] + [qc[c, x + i] * inverse]))
        for c, at, values in out:
            for n in range(7):
                cs[n, c, at] = values[n]

    def solid_planes(n, src, dst, runs):
        decay, gain = coefficients[n]
        out = []
        for x, count in runs:
            v = [[src[c, x + i, own_rows, :] for c in range(solid_chunks)] for i in range(count + 2)]
            for i in range(count):
                zm, zp = lane_shifts(v[i + 1])
                for c in range(solid_chunks):
                    at = x + i
                    r = ((cs[0, c, at] * v[i][c] + cs[1, c, at] * v[i + 2][c])
                         + (cs[2, c, at] * src[c, at + 1, TOP - 1:end - 1, :] + cs[3, c, at] * src[c, at + 1, TOP + 1:end + 1, :]))
                    r = r + (cs[4, c, at] * zm[c] + cs[5, c, at] * zp[c]) + cs[6, c, at]
                    new = (1.0 + decay - gain) * v[i + 1][c] + gain * r
                    if n > 0:
                        new = new - decay * dst[c, at + 1, own_rows, :]
                    if n == SWEEPS - 1 and c == 0:
                        new = jnp.where(lane < HALO, wz[at], new)
                    out.append((c, at, new))
        for c, at, new in out:
            if n == SWEEPS - 1:
                x_out[at, :, 128 * c:128 * c + 128] = new
            else:
                dst[c, at + 1, own_rows, :] = new

    solid_sends = [(-1, m) for m in x_x + x_y]
    solid_waits = [x_x + x_y]
    interior = nx - 2

    def loop(count, step, work):
        def body(i, _):
            work(i * step)
            return 0
        lax.fori_loop(0, count // step, body, 0)

    def solid_sweep(n):
        src, dst = (xa, xb) if n % 2 == 0 else (xb, xa)
        arrived(solid_waits.pop())
        for m in list(solid_sends):
            if m[0] <= n - 2:
                m[1].sent()
                solid_sends.remove(m)
        solid_planes(n, src, dst, [(0, 1), (nx - 1, 1)])
        msgs = send_planes(dst) if n < SWEEPS - 1 else []
        loop(interior, SOLID_STEP, lambda x: solid_planes(n, src, dst, [(1 + x, SOLID_STEP)]))
        if n < SWEEPS - 1:
            msgs += send_rows(dst)
        solid_sends.extend((n, m) for m in msgs)
        solid_waits.append(msgs)

    mirror = 1.0 - 2.0 * live
    source = 2.0 * live * wall

    def columns(v, x):
        return jnp.concatenate([pltpu.roll(v, lax.rem(128 - (x * 4 + j), 128), axis=1) for j in range(4)], axis=0)

    def rows_of(plane):
        def body(i, parts):
            parts = list(parts)
            for k in range(4):
                v = plane(4 * i + k)
                for j in range(4):
                    parts[j] = jnp.where(lane8 == (4 * i + k) * 4 + j, jnp.broadcast_to(v[8 * j:8 * j + 8, 0:1], (8, 128)), parts[j])
            return tuple(parts)
        parts = lax.fori_loop(0, nx // 4, body, (jnp.zeros((8, 128), jnp.float32),) * 4)
        return (parts[0] + parts[1]) + (parts[2] + parts[3])

    top = fluid_chunks - 1

    def fluid_coef(x):
        a = [al[c, x + 1, own_rows, :] for c in range(fluid_chunks)]
        u = [uz[c, x] for c in range(fluid_chunks)]
        am, _ = lane_shifts(a)
        um, _ = lane_shifts(u)
        am[0] = jnp.where(lane == 0, a[0], am[0])
        um[0] = jnp.where(lane == 0, -u[0], um[0])
        z = [face(u[c], um[c], a[c], am[c]) for c in range(fluid_chunks)]
        _, pz = lane_shifts([v[0] for v in z])
        _, qz = lane_shifts([v[1] for v in z])
        last = face(u[top], u[top], a[top], a[top])
        pz[top] = jnp.where(lane == 127, last[0], pz[top])
        qz[top] = jnp.where(lane == 127, last[1], qz[top])
        for c in range(fluid_chunks):
            v = ux[c, x + 1]
            p_xm, q_xm = face(v, ux[c, x], a[c], al[c, x, own_rows, :])
            p_xp, q_xp = face(v, ux[c, x + 2], a[c], al[c, x + 2, own_rows, :])
            v = uy[c, x, own_rows, :]
            p_ym, q_ym = face(v, uy[c, x, TOP - 1:end - 1, :], a[c], al[c, x + 1, TOP - 1:end - 1, :])
            p_yp, q_yp = face(v, uy[c, x, TOP + 1:end + 1, :], a[c], al[c, x + 1, TOP + 1:end + 1, :])
            p_zm, q_zm = z[c]
            away = ((q_xm + p_xp) + (q_ym + p_yp)) + (q_zm + pz[c])
            toward = ((p_xm + q_xp) + (p_ym + q_yp)) + (p_zm + qz[c])
            scale = 1.6 / (away + toward)
            cf[0, c, x] = p_xm * scale
            cf[1, c, x] = q_xp * scale
            cf[2, c, x] = p_ym * scale
            cf[3, c, x] = q_yp * scale
            below, above, centre = p_zm * scale, qz[c] * scale, 1.0 - away * scale
            if c == 0:
                first = lane == 0
                at_wall = jnp.where(first, below, 0.0)
                sf[x] = at_wall * columns(source, x)
                centre = centre + at_wall * columns(mirror, x)
                below = jnp.where(first, 0.0, below)
            if c == top:
                above = jnp.where(lane == 127, 0.0, above)
            cf[4, c, x] = below
            cf[5, c, x] = above
            cf[6, c, x] = centre

    def fluid_planes(src, xs, chunks, put):
        out = []
        for x in xs:
            held = {}

            def rolled(c, shift, held=held, x=x):
                if (c, shift) not in held:
                    held[c, shift] = pltpu.roll(src[c, x + 1, own_rows, :], shift, axis=1)
                return held[c, shift]

            for c in chunks:
                zm = rolled(c, 1) if c == 0 else jnp.where(lane == 0, rolled(c - 1, 1), rolled(c, 1))
                zp = rolled(c, 127) if c == top else jnp.where(lane == 127, rolled(c + 1, 127), rolled(c, 127))
                new = ((cf[0, c, x] * src[c, x, own_rows, :] + cf[1, c, x] * src[c, x + 2, own_rows, :])
                       + (cf[2, c, x] * src[c, x + 1, TOP - 1:end - 1, :] + cf[3, c, x] * src[c, x + 1, TOP + 1:end + 1, :]))
                new = new + (cf[4, c, x] * zm + cf[5, c, x] * zp) + cf[6, c, x] * src[c, x + 1, own_rows, :]
                out.append((c, x, new + sf[x] if c == 0 else new))
        for item in out:
            put(*item)

    def put_first(c, x, new):
        t1[c, x + 1, own_rows, :] = new

    def put_second(c, x, new):
        t_out[x, :, 128 * c:128 * c + 128] = new

    lane_w = iota((nx + 2 * HALO, 128), 1)

    def widen(left, mid, right, f):
        left = pltpu.roll(left, (128 - 32 * f - 24) % 128, axis=1)
        mid = pltpu.roll(mid, (128 + HALO - 32 * f) % 128, axis=1)
        right = pltpu.roll(right, (128 + 40 - 32 * f) % 128, axis=1)
        return jnp.where(lane_w < HALO, left, jnp.where(lane_w < HALO + ny, mid, jnp.where(lane_w < 2 * HALO + ny, right, 0.0)))

    def near_field(z, f):
        return widen(nb[0, z], nb[1, z], nb[2, z], f)

    def shift_all(v):
        n = v.shape[0]
        return [pltpu.roll(v, 1, axis=0), pltpu.roll(v, n - 1, axis=0), pltpu.roll(v, 1, axis=1), pltpu.roll(v, 127, axis=1)]

    def spread_near(z):
        wk[z] = near_field(z, 1)
        wxa[z] = near_field(z, 0)

    def wedge_coef(z):
        k = wk[z]
        under = wk[jnp.maximum(z - 1, 0)] * (z > 0).astype(jnp.float32)
        over = wk[jnp.minimum(z + 1, DEEP - 1)] * (z < DEEP - 1).astype(jnp.float32)
        g = [conductance(k, kn) for kn in shift_all(k) + [under, over]]
        diag = ((g[0] + g[1]) + (g[2] + g[3])) + ((g[4] + g[5]) + near_field(z, 2))
        diag = jnp.where(diag > 0.0, diag, 1.0)
        inverse = 1.0 / diag
        for n in range(6):
            wcf[n, z] = g[n] * inverse
        wcf[6, z] = near_field(z, 3) * inverse
        wd[z] = diag

    def wedge_sweep(n, first=0, last=None):
        decay, gain = coefficients[n]
        src, dst = (wxa, wxb) if n % 2 == 0 else (wxb, wxa)

        def level(z):
            v = src[z]
            near_v = shift_all(v) + [src[jnp.maximum(z - 1, 0) if not isinstance(z, int) else max(z - 1, 0)], src[z + 1]]
            r = (wcf[0, z] * near_v[0] + wcf[1, z] * near_v[1]) + (wcf[2, z] * near_v[2] + wcf[3, z] * near_v[3])
            r = r + (wcf[4, z] * near_v[4] + wcf[5, z] * near_v[5]) + wcf[6, z]
            new = (1.0 + decay - gain) * v + gain * r
            return new if n == 0 else new - decay * dst[z]

        def levels(z, step):
            for k, new in enumerate([level(z + k) for k in range(step)]):
                dst[z + k] = new

        if last is None:
            last = DEEP - 1 - n
        count = last - first
        step = 3 if count % 3 == 0 else 2
        if count > step:
            loop(count - count % step, step, lambda z: levels(first + z, step))
            if count % step:
                levels(last - count % step, count % step)
        else:
            levels(first, count)

    def bands(refs):
        total = None
        for band, ref in enumerate(refs):
            v = ref[...]
            at = iota(v.shape, 1)
            v = jnp.where((at >= 16 * band) & (at < 16 * band + 16), v, 0.0)
            total = v if total is None else total + v
        return total

    def drain():
        recent = [m for n, m in solid_sends if n >= 0]
        for m in [m for m in pending if m not in recent and m not in held_back]:
            m.sent()

    held_back = []

    all_chunks = range(fluid_chunks)
    loaded("e", "q")
    lax.fori_loop(0, nx, turn, 0, unroll=2)
    film = 2.0 * live * rows_of(lambda x: al[0, x + 1, own_rows, :])
    arrived(k_y)
    loop(interior, 2, lambda x: solid_coef(1 + x, 2))
    arrived(k_x)
    solid_coef(0, 1)
    solid_coef(nx - 1, 1)
    solid_sweep(0)
    u_x = [Message(ux.at[:, nx if d == 0 else 1], ux.at[:, 0 if d == 0 else nx + 1], d).start() for d in range(2)]
    t_x = send_planes(t0)

    loaded("uz")
    arrived(a_y + u_y)
    cuts = [interior * n // (30 * COEF_STEP) * COEF_STEP for n in COEF_CUTS]

    def coef_part(n):
        first = 1 + cuts[n]
        loop(cuts[n + 1] - cuts[n], COEF_STEP, lambda x: [fluid_coef(first + x + i) for i in range(COEF_STEP)])

    coef_part(0)
    solid_sweep(1)
    near_msgs = send_near(nb, lambda ref, column, rows: ref.at[column, :, rows, :])
    coef_part(1)
    solid_sweep(2)
    coef_part(2)
    arrived(a_x + u_x)
    fluid_coef(0)
    fluid_coef(nx - 1)

    arrived(t_x + t_y)
    fluid_planes(t0, (0, nx - 1), all_chunks, put_first)
    t_msgs = send_planes(t1)
    loop(interior, FLUID_STEP, lambda x: fluid_planes(t0, [1 + x + i for i in range(FLUID_STEP)], all_chunks, put_first))
    t_msgs += send_rows(t1)
    solid_sweep(3)

    arrived(near_msgs)
    loop(DEEP, 2, lambda z: [spread_near(z), spread_near(z + 1)])

    arrived(t_msgs)
    loop(nx, 4, lambda x: fluid_planes(t1, [x + i for i in range(4)], (0,), put_second))
    gas = rows_of(lambda x: t_out[x, :, 0:128])
    rows_s[...] = product(jnp.concatenate([film, gas], axis=0), select(), ((1,), (1,)))
    row_msgs = [Message(rows_s, rows_r.at[d], d).start() for d in range(4)]

    if fluid_chunks > 1:
        loop(nx, 4, lambda x: fluid_planes(t1, [x + i for i in range(4)], all_chunks[1:], put_second))
    solid_sweep(4)

    solid_sends[:] = [item for item in solid_sends if item[0] >= 0]
    held_back.extend(row_msgs)
    drain()
    arrived(row_msgs)
    came = bands([rows_r.at[d] for d in range(4)])
    film_in = jnp.concatenate([film * self_mask, came[0:8]], axis=1)
    heat_in = film_in * jnp.concatenate([gas, came[8:16]], axis=1)
    sums = None
    for film_piece, heat_piece in zip(pieces(film_in), pieces(heat_in)):
        weighed = jnp.concatenate(
            [jnp.concatenate([hot_y[:, 256 * n:256 * n + 256] * v[n:n + 1, :] for n in range(8)], axis=1)
             for v in (film_piece.astype(jnp.float32), heat_piece.astype(jnp.float32))], axis=0).astype(jnp.bfloat16)
        part = product16(hot_x16[...], weighed, ((1,), (1,)))
        sums = part if sums is None else sums + part
    fb[1, HALO:HALO + nx, :] = jnp.concatenate([sums, jnp.zeros((nx, 64), jnp.float32)], axis=1)
    film_msgs = send_near(fb, lambda ref, column, rows: ref.at[column, rows, :])

    loop(DEEP, 2, lambda z: [wedge_coef(z), wedge_coef(z + 1)])
    solid_sweep(5)

    held_back[:] = film_msgs
    drain()
    arrived(film_msgs)
    wide = [widen(fb[0], fb[1], fb[2], f) for f in range(2)]
    diag = wd[0]
    inverse = 1.0 / (diag + wide[0])
    wcf[6, 0] = (wcf[6, 0] * diag + wide[1]) * inverse
    for n in range(6):
        wcf[n, 0] = wcf[n, 0] * diag * inverse
    for n in range(WEDGE_SPLIT):
        wedge_sweep(n)
    solid_sweep(6)
    for n in range(WEDGE_SPLIT, SWEEPS):
        wedge_sweep(n, 0, SWEEPS - n)
    solved = wxa if SWEEPS % 2 == 0 else wxb

    surface = pltpu.roll(solved[0, HALO:HALO + nx, :], 128 - HALO, axis=1)[:, 0:32]
    picked = product16(jnp.concatenate(pieces(surface), axis=0), hot_y16[...], ((1,), (0,)))
    picked = (picked[0:nx] + picked[nx:2 * nx]) + picked[2 * nx:3 * nx]
    picked = jnp.sum(picked * hot_x[...], axis=0, keepdims=True)
    for n in range(8):
        slots[n:n + 1, :] = picked[:, 256 * n:256 * n + 256]
    wall_s[...] = slots[:, 128:256]
    wall_msgs = [Message(wall_s, wall_r.at[d], d).start() for d in range(4)]

    for n in range(WEDGE_SPLIT, SWEEPS):
        wedge_sweep(n, SWEEPS - n)

    def turn_back(x, _):
        cells = jnp.concatenate([solved[0:HALO, pl.ds(HALO + x, 1), :].reshape(HALO, 128), jnp.zeros((128 - HALO, 128), jnp.float32)], axis=0)
        wz[x] = jnp.transpose(cells)[HALO:HALO + ny]
        return 0
    lax.fori_loop(0, nx, turn_back, 0, unroll=2)

    held_back[:] = wall_msgs
    drain()
    solid_sweep(7)

    arrived(wall_msgs)
    back = bands([wall_r.at[d] for d in (1, 0, 3, 2)])
    rows = (self_mask * slots[:, 0:128] + product(back, select(), ((1,), (0,)))) * live
    rows = jnp.concatenate([jnp.where(lane8 < 16, pltpu.roll(rows, (128 - 16 * n) % 128, axis=1), 0.0) for n in range(8)], axis=0)
    rows = product(rows, compress, ((1,), (1,)))
    for n in range(8):
        wall_out[n:n + 1, :] = jnp.sum(jnp.where(keep, rows[8 * n:8 * n + 8], 0.0), axis=0, keepdims=True)
    for m in list(pending):
        m.sent()


N_MESSAGES = 8 + 12 + 8 + 4 * (SWEEPS - 1) + 4 + 4 + 8 + 4


def on_device(n_blk, n_sub, fluid_temp, velocity, eddy_diff, wall_prev, row_count, owner_table, landing_cell, solid_temp, conductivity, sink, heat_source):
    nx, ny, nz = fluid_temp.shape
    nsz = solid_temp.shape[2]
    f32 = jnp.float32
    any_space = pl.BlockSpec(memory_space=pl.ANY)
    vmem_space = pl.BlockSpec(memory_space=pltpu.VMEM)

    def vmem(*shape):
        return pltpu.VMEM(shape, f32)

    def haloed(depth):
        return vmem(depth // 128, nx + 2, ny + 2 * TOP, 128)

    wide = nx + 2 * HALO
    fluid_new, solid_new, wall_new = pl.pallas_call(
        functools.partial(kernel, n_blk, n_sub),
        out_shape=(
            vmem(nx, ny, nz),
            vmem(nx, ny, nsz),
            jax.ShapeDtypeStruct((8, 128), f32),
        ),
        in_specs=[pl.BlockSpec(memory_space=pltpu.SMEM)] + [any_space] * 7 + [vmem_space] * 3,
        out_specs=(vmem_space,) * 3,
        scratch_shapes=[
            haloed(nz), haloed(nz),
            vmem(nz // 128, nx + 2, ny, 128), vmem(nz // 128, nx, ny + 2 * TOP, 128), vmem(nz // 128, nx, ny, 128),
            haloed(nz), vmem(7, nz // 128, nx, ny, 128), vmem(nx, ny, 128),
            haloed(nsz), haloed(nsz), haloed(nsz), vmem(nsz // 128, nx, ny, 128), vmem(nsz // 128, nx, ny, 128),
            vmem(7, nsz // 128, nx, ny, 128),
            vmem(3, DEEP, wide, 128), vmem(3, wide, 128),
            vmem(DEEP, wide, 128), vmem(7, DEEP, wide, 128),
            vmem(DEEP, wide, 128), vmem(DEEP, wide, 128), vmem(DEEP, wide, 128), vmem(nx, ny, 128),
            vmem(16, 128), vmem(4, 16, 128), vmem(8, 128), vmem(4, 8, 128),
            vmem(32, 2048), vmem(32, 2048),
            pltpu.VMEM((32, 2048), jnp.bfloat16), pltpu.VMEM((32, 2048), jnp.bfloat16), vmem(8, 256),
            pltpu.SemaphoreType.DMA((6 * nz // 128 + 5 * nsz // 128,)),
            pltpu.SemaphoreType.DMA((N_MESSAGES,)),
            pltpu.SemaphoreType.DMA((N_MESSAGES,)),
        ],
        compiler_params=pltpu.CompilerParams(
            collective_id=0, has_side_effects=True, vmem_limit_bytes=60 * 1024 * 1024
        ),
    )(row_count, fluid_temp, velocity, eddy_diff, solid_temp, conductivity, sink, heat_source, wall_prev.reshape(8, 128), owner_table, landing_cell)
    return fluid_new, solid_new, wall_new.reshape(-1)


def solution(mesh):
    return jax.shard_map(
        functools.partial(on_device, mesh.shape["blk"], mesh.shape["sub"]),
        mesh=mesh,
        in_specs=(
            P("blk", "sub", None),
            P(None, "blk", "sub", None),
            P("blk", "sub", None),
            P(("blk", "sub")),
            P(("blk", "sub")),
            P(("blk", "sub"), None),
            P(("blk", "sub"), None),
            P("blk", "sub", None),
            P("blk", "sub", None),
            P("blk", "sub", None),
            P("blk", "sub", None),
        ),
        out_specs=(P("blk", "sub", None), P("blk", "sub", None), P(("blk", "sub"))),
        check_vma=False,
    )
```

```python
import functools

import jax
import jax.numpy as jnp
from jax import lax
from jax.experimental import pallas as pl
from jax.experimental.pallas import tpu as pltpu
from jax.sharding import PartitionSpec as P

MESH = pl.DeviceIdType.MESH
SWEEPS = 8
HALO = 8
DEEP = 16
TOP = 8
SOLID_STEP = 10
WEDGE_SPLIT = 5
COEF_CUTS = (0, 14, 26, 30)
FLUID_STEP = 5
COEF_STEP = 2
EIG_LOW = 0.02
EIG_HIGH = 2.0
HIGHEST = lax.Precision.HIGHEST
DIRS = ((1, 0), (-1, 0), (0, 1), (0, -1), (1, 1), (1, -1), (-1, 1), (-1, -1))


def cheby_coefficients(count_sweeps):
    center_eig = 0.5 * (EIG_HIGH + EIG_LOW)
    half_width = 0.5 * (EIG_HIGH - EIG_LOW)
    ratio_eig = center_eig / half_width
    damping = 1.0 / ratio_eig
    coefficients = [(0.0, 1.0 / center_eig)]
    for _ in range(1, count_sweeps):
        damping_new = 1.0 / (2.0 * ratio_eig - damping)
        coefficients.append((damping_new * damping, 2.0 * damping_new / half_width))
        damping = damping_new
    return coefficients


def iota(shape, dim):
    return lax.broadcasted_iota(jnp.int32, shape, dim)


def lane_shifts(v):
    lane = iota(v[0].shape, 1)
    low, high = [pltpu.roll(c, 1, axis=1) for c in v], [pltpu.roll(c, 127, axis=1) for c in v]
    below = [low[0]] + [jnp.where(lane == 0, low[c - 1], low[c]) for c in range(1, len(v))]
    above = [jnp.where(lane == 127, high[c + 1], high[c]) for c in range(len(v) - 1)] + [high[-1]]
    return below, above


def face(u, un, a, an):
    total_u, total_a = u + un, a + an
    return total_a + jnp.maximum(total_u, 0.0), total_a - jnp.minimum(total_u, 0.0)


def within(k, kn):
    return 2.0 * k * kn / (k + kn)


def conductance(k, kn):
    total = k + kn
    return 2.0 * k * kn / jnp.where(total > 0.0, total, 1.0)


def kernel(
    n_blk, n_sub,
    count_ref, t_hbm, vel_hbm, a_hbm, x_hbm, k_hbm, e_hbm, q_hbm, wall_ref, owner_ref, land_ref,
    t_out, x_out, wall_out,
    t0, t1, ux, uy, uz, al, cf, sf,
    xa, xb, kc, ec, qc, cs,
    nb, fb, wk, wcf, wxa, wxb, wd, wz,
    rows_s, rows_r, wall_s, wall_r, hot_x, hot_y, hot_x16, hot_y16, slots,
    load_sem, send_sem, recv_sem,
):
    b, s = lax.axis_index("blk"), lax.axis_index("sub")
    nx, ny, _ = t_hbm.shape
    fluid_chunks, solid_chunks = t0.shape[0], xa.shape[0]
    end = TOP + ny
    own_rows, own_planes = slice(TOP, end), slice(1, 1 + nx)
    coefficients = cheby_coefficients(SWEEPS)

    def inside(db, ds):
        ok = None
        for delta, at, count in ((db, b, n_blk), (ds, s, n_sub)):
            if delta:
                this = (at < count - 1) if delta > 0 else (at > 0)
                ok = this if ok is None else ok & this
        return ok

    counter = [0]
    pending = []

    class Message:
        def __init__(self, src, dst, d):
            db, ds = DIRS[d]
            self.n = counter[0]
            counter[0] += 1
            self.make = lambda: pltpu.make_async_remote_copy(
                src_ref=src, dst_ref=dst, send_sem=send_sem.at[self.n], recv_sem=recv_sem.at[self.n],
                device_id=(b + db, s + ds), device_id_type=MESH)
            self.goes, self.comes = inside(db, ds), inside(-db, -ds)

        def start(self):
            @pl.when(self.goes)
            def _():
                self.make().start()
            pending.append(self)
            return self

        def sent(self):
            @pl.when(self.goes)
            def _():
                self.make().wait_send()
            pending.remove(self)

        def arrived(self):
            @pl.when(self.comes)
            def _():
                self.make().wait_recv()

    def send_planes(ref):
        return [Message(ref.at[:, nx if d == 0 else 1, own_rows, :], ref.at[:, 0 if d == 0 else nx + 1, own_rows, :], d).start()
                for d in range(2)]

    def send_rows(ref):
        return [Message(ref.at[:, own_planes, end - 1:end, :], ref.at[:, own_planes, TOP - 1:TOP, :], 2).start(),
                Message(ref.at[:, own_planes, TOP:TOP + 1, :], ref.at[:, own_planes, end:end + 1, :], 3).start()]

    def arrived(messages):
        for m in messages:
            m.arrived()

    loads = {}
    for name, src, dst in (
        ("k", k_hbm, kc), ("x", x_hbm, xa), ("a", a_hbm, al), ("ux", vel_hbm.at[0], ux), ("t", t_hbm, t0), ("uy", vel_hbm.at[1], uy),
        ("e", e_hbm, ec), ("q", q_hbm, qc), ("uz", vel_hbm.at[2], uz),
    ):
        planes = own_planes if dst.shape[1] > nx else slice(0, nx)
        rows = own_rows if dst.shape[2] > ny else slice(0, ny)
        n = len(loads)
        for c in range(dst.shape[0]):
            pltpu.make_async_copy(src.at[:, :, 128 * c:128 * c + 128], dst.at[c, planes, rows, :], load_sem.at[n]).start()
        whole = dst.at[:, planes, rows, :]
        loads[name] = pltpu.make_async_copy(whole, whole, load_sem.at[n])

    def loaded(*names):
        for name in names:
            loads[name].wait()

    barrier = pltpu.get_barrier_semaphore()
    for db, ds in DIRS:
        @pl.when(inside(db, ds))
        def _(db=db, ds=ds):
            pl.semaphore_signal(barrier, inc=1, device_id=(b + db, s + ds), device_id_type=MESH)

    def clear(ref, *where):
        ref[where] = jnp.zeros(ref.at[where].shape, jnp.float32)

    for d in range(2):
        @pl.when(jnp.logical_not(inside(-DIRS[d][0], 0)))
        def _(d=d):
            for ref in (t0, t1, al, ux, xa, xb, kc):
                rows = own_rows if ref.shape[2] > ny else slice(0, ny)
                for c in range(ref.shape[0]):
                    clear(ref, c, 0 if d == 0 else nx + 1, rows, slice(None))

        @pl.when(jnp.logical_not(inside(0, -DIRS[2 + d][1])))
        def _(d=d):
            row = TOP - 1 if d == 0 else end

            def body(x, _):
                for ref in (t0, t1, al, uy, xa, xb, kc):
                    for c in range(ref.shape[0]):
                        clear(ref, c, x + (1 if ref.shape[1] > nx else 0), slice(row, row + 1), slice(None))
                return 0
            lax.fori_loop(0, nx, body, 0)
    for d in range(4):
        @pl.when(jnp.logical_not(inside(-DIRS[d][0], -DIRS[d][1])))
        def _(d=d):
            rows_r[d] = jnp.zeros(rows_r.shape[1:], jnp.float32)
            wall_r[d] = jnp.zeros(wall_r.shape[1:], jnp.float32)

    def near_slot(d):
        db, ds = DIRS[d]
        column = {1: 0, 0: 1, -1: 2}[ds]
        if db == 0:
            return column, slice(HALO, HALO + nx), slice(HALO, HALO + nx)
        if db > 0:
            return column, slice(nx, HALO + nx), slice(0, HALO)
        return column, slice(HALO, 2 * HALO), slice(HALO + nx, 2 * HALO + nx)

    for d in range(8):
        @pl.when(jnp.logical_not(inside(-DIRS[d][0], -DIRS[d][1])))
        def _(d=d):
            column, _, rows = near_slot(d)
            height = rows.stop - rows.start
            nb[column, :, rows, :] = jnp.zeros((DEEP, height, 128), jnp.float32)
            fb[column, rows, :] = jnp.zeros((height, 128), jnp.float32)

    def product(x, y, dims):
        return lax.dot_general(x, y, (dims, ((), ())), precision=HIGHEST, preferred_element_type=jnp.float32)

    def pieces(v):
        out = []
        for _ in range(3):
            out.append(v.astype(jnp.bfloat16))
            v = v - out[-1].astype(jnp.float32)
        return out

    def product16(x, y, dims):
        return lax.dot_general(x, y, (dims, ((), ())), preferred_element_type=jnp.float32)

    lane, lane8, sub8 = iota((ny, 128), 1), iota((8, 128), 1), iota((8, 128), 0)
    keep = (lane8 & 7) == sub8
    compress = jnp.where((iota((128, 128), 0) >> 3) == iota((128, 128), 1), 1.0, 0.0)
    flat = [wall_ref[n:n + 1, :] for n in range(8)] + [land_ref[0:1, 128 * n:128 * n + 128].astype(jnp.float32) for n in range(12)]
    packed = product(jnp.concatenate([jnp.where(keep, jnp.broadcast_to(v, (8, 128)), 0.0) for v in flat], axis=0), compress, ((1,), (0,)))

    def gather_rows(first, count):
        total = packed[8 * first:8 * first + 8]
        for n in range(1, count):
            total = total + pltpu.roll(packed[8 * (first + n):8 * (first + n) + 8], 16 * n, axis=1)
        return total

    wall = gather_rows(0, 8)
    land = jnp.concatenate([gather_rows(8, 8), jnp.where(lane8 < 64, gather_rows(16, 4), -1.0)], axis=1).astype(jnp.int32)
    live = jnp.where(lane8 * 8 + sub8 < count_ref[0], 1.0, 0.0)
    owner = jnp.broadcast_to(owner_ref[...], (8, 128))
    self_mask = jnp.where(owner == 0, 1.0, 0.0)
    match = jnp.where((owner == sub8 + 1) & (sub8 < 4), 1.0, 0.0)
    before = jnp.where(iota((128, 128), 0) < iota((128, 128), 1), 1.0, 0.0)
    rank = product(match, before, ((1,), (0,)))
    place = jnp.sum(match * (rank + (sub8 * 16 + 1).astype(jnp.float32)), axis=0, keepdims=True) - 1.0
    row32 = iota((32, 256), 0)
    for n in range(8):
        cell = land[n:n + 1, :]
        at = slice(256 * n, 256 * n + 256)
        hot_x[:, at] = jnp.where((cell >> 5) == row32, 1.0, 0.0)
        hot_y[:, at] = jnp.where(((cell & 31) == row32) & (cell >= 0), 1.0, 0.0)
        hot_x16[:, at] = hot_x[:, at].astype(jnp.bfloat16)
        hot_y16[:, at] = hot_y[:, at].astype(jnp.bfloat16)

    def select():
        return jnp.where(iota((128, 128), 0).astype(jnp.float32) == place, 1.0, 0.0)

    near = (b > 0).astype(jnp.int32) + (b < n_blk - 1).astype(jnp.int32)
    side = (s > 0).astype(jnp.int32) + (s < n_sub - 1).astype(jnp.int32)
    pl.semaphore_wait(barrier, near + side + near * side)

    loaded("k", "x")
    k_x, x_x = send_planes(kc), send_planes(xa)
    k_y, x_y = send_rows(kc), send_rows(xa)
    loaded("a", "ux", "t")
    a_x = send_planes(al)
    loaded("uy")
    a_y, t_y = send_rows(al), send_rows(t0)
    u_y = [Message(uy.at[:, :, end - 1:end, :], uy.at[:, :, TOP - 1:TOP, :], 2).start(),
           Message(uy.at[:, :, TOP:TOP + 1, :], uy.at[:, :, end:end + 1, :], 3).start()]

    def turn(x, _):
        tile = jnp.concatenate([xa[0, x + 1, own_rows, :], kc[0, x + 1, own_rows, :], ec[0, x], qc[0, x]], axis=0)
        nb[1, :, pl.ds(HALO + x, 1), :] = jnp.transpose(tile)[0:DEEP].reshape(DEEP, 1, 128)
        return 0

    def send_near(column_ref, part):
        messages = []
        for d in range(8):
            column, out_rows, rows = near_slot(d)
            messages.append(Message(part(column_ref, 1, out_rows), part(column_ref, column, rows), d).start())
        return messages

    def solid_coef(x, count):
        k = [[kc[c, x + i, own_rows, :] for c in range(solid_chunks)] for i in range(count + 2)]
        out = []
        for i in range(count):
            here, under, over = k[i + 1], k[i], k[i + 2]
            zm, _ = lane_shifts(here)
            gz = [within(here[c], zm[c]) for c in range(solid_chunks)]
            gz[0] = jnp.where(lane == 0, 0.0, gz[0])
            _, gz_up = lane_shifts(gz)
            gz_up[-1] = jnp.where(lane == 127, 0.0, gz_up[-1])
            for c in range(solid_chunks):
                g = [within(here[c], under[c]), within(here[c], over[c]),
                     within(here[c], kc[c, x + i + 1, TOP - 1:end - 1, :]), within(here[c], kc[c, x + i + 1, TOP + 1:end + 1, :]),
                     gz[c], gz_up[c]]
                inverse = 1.0 / (((g[0] + g[1]) + (g[2] + g[3])) + ((g[4] + g[5]) + ec[c, x + i]))
                out.append((c, x + i, [v * inverse for v in g] + [qc[c, x + i] * inverse]))
        for c, at, values in out:
            for n in range(7):
                cs[n, c, at] = values[n]

    def solid_planes(n, src, dst, runs):
        decay, gain = coefficients[n]
        out = []
        for x, count in runs:
            v = [[src[c, x + i, own_rows, :] for c in range(solid_chunks)] for i in range(count + 2)]
            for i in range(count):
                zm, zp = lane_shifts(v[i + 1])
                for c in range(solid_chunks):
                    at = x + i
                    r = ((cs[0, c, at] * v[i][c] + cs[1, c, at] * v[i + 2][c])
                         + (cs[2, c, at] * src[c, at + 1, TOP - 1:end - 1, :] + cs[3, c, at] * src[c, at + 1, TOP + 1:end + 1, :]))
                    r = r + (cs[4, c, at] * zm[c] + cs[5, c, at] * zp[c]) + cs[6, c, at]
                    new = (1.0 + decay - gain) * v[i + 1][c] + gain * r
                    if n > 0:
                        new = new - decay * dst[c, at + 1, own_rows, :]
                    if n == SWEEPS - 1 and c == 0:
                        new = jnp.where(lane < HALO, wz[at], new)
                    out.append((c, at, new))
        for c, at, new in out:
            if n == SWEEPS - 1:
                x_out[at, :, 128 * c:128 * c + 128] = new
            else:
                dst[c, at + 1, own_rows, :] = new

    solid_sends = [(-1, m) for m in x_x + x_y]
    solid_waits = [x_x + x_y]
    interior = nx - 2

    def loop(count, step, work):
        def body(i, _):
            work(i * step)
            return 0
        lax.fori_loop(0, count // step, body, 0)

    def solid_sweep(n):
        src, dst = (xa, xb) if n % 2 == 0 else (xb, xa)
        arrived(solid_waits.pop())
        for m in list(solid_sends):
            if m[0] <= n - 2:
                m[1].sent()
                solid_sends.remove(m)
        solid_planes(n, src, dst, [(0, 1), (nx - 1, 1)])
        msgs = send_planes(dst) if n < SWEEPS - 1 else []
        loop(interior, SOLID_STEP, lambda x: solid_planes(n, src, dst, [(1 + x, SOLID_STEP)]))
        if n < SWEEPS - 1:
            msgs += send_rows(dst)
        solid_sends.extend((n, m) for m in msgs)
        solid_waits.append(msgs)

    mirror = 1.0 - 2.0 * live
    source = 2.0 * live * wall

    def columns(v, x):
        return jnp.concatenate([pltpu.roll(v, lax.rem(128 - (x * 4 + j), 128), axis=1) for j in range(4)], axis=0)

    def rows_of(plane):
        def body(i, parts):
            parts = list(parts)
            for k in range(4):
                v = plane(4 * i + k)
                for j in range(4):
                    parts[j] = jnp.where(lane8 == (4 * i + k) * 4 + j, jnp.broadcast_to(v[8 * j:8 * j + 8, 0:1], (8, 128)), parts[j])
            return tuple(parts)
        parts = lax.fori_loop(0, nx // 4, body, (jnp.zeros((8, 128), jnp.float32),) * 4)
        return (parts[0] + parts[1]) + (parts[2] + parts[3])

    top = fluid_chunks - 1

    def fluid_coef(x):
        a = [al[c, x + 1, own_rows, :] for c in range(fluid_chunks)]
        u = [uz[c, x] for c in range(fluid_chunks)]
        am, _ = lane_shifts(a)
        um, _ = lane_shifts(u)
        am[0] = jnp.where(lane == 0, a[0], am[0])
        um[0] = jnp.where(lane == 0, -u[0], um[0])
        z = [face(u[c], um[c], a[c], am[c]) for c in range(fluid_chunks)]
        _, pz = lane_shifts([v[0] for v in z])
        _, qz = lane_shifts([v[1] for v in z])
        last = face(u[top], u[top], a[top], a[top])
        pz[top] = jnp.where(lane == 127, last[0], pz[top])
        qz[top] = jnp.where(lane == 127, last[1], qz[top])
        for c in range(fluid_chunks):
            v = ux[c, x + 1]
            p_xm, q_xm = face(v, ux[c, x], a[c], al[c, x, own_rows, :])
            p_xp, q_xp = face(v, ux[c, x + 2], a[c], al[c, x + 2, own_rows, :])
            v = uy[c, x, own_rows, :]
            p_ym, q_ym = face(v, uy[c, x, TOP - 1:end - 1, :], a[c], al[c, x + 1, TOP - 1:end - 1, :])
            p_yp, q_yp = face(v, uy[c, x, TOP + 1:end + 1, :], a[c], al[c, x + 1, TOP + 1:end + 1, :])
            p_zm, q_zm = z[c]
            away = ((q_xm + p_xp) + (q_ym + p_yp)) + (q_zm + pz[c])
            toward = ((p_xm + q_xp) + (p_ym + q_yp)) + (p_zm + qz[c])
            scale = 1.6 / (away + toward)
            cf[0, c, x] = p_xm * scale
            cf[1, c, x] = q_xp * scale
            cf[2, c, x] = p_ym * scale
            cf[3, c, x] = q_yp * scale
            below, above, centre = p_zm * scale, qz[c] * scale, 1.0 - away * scale
            if c == 0:
                first = lane == 0
                at_wall = jnp.where(first, below, 0.0)
                sf[x] = at_wall * columns(source, x)
                centre = centre + at_wall * columns(mirror, x)
                below = jnp.where(first, 0.0, below)
            if c == top:
                above = jnp.where(lane == 127, 0.0, above)
            cf[4, c, x] = below
            cf[5, c, x] = above
            cf[6, c, x] = centre

    def fluid_planes(src, xs, chunks, put):
        out = []
        for x in xs:
            held = {}

            def rolled(c, shift, held=held, x=x):
                if (c, shift) not in held:
                    held[c, shift] = pltpu.roll(src[c, x + 1, own_rows, :], shift, axis=1)
                return held[c, shift]

            for c in chunks:
                zm = rolled(c, 1) if c == 0 else jnp.where(lane == 0, rolled(c - 1, 1), rolled(c, 1))
                zp = rolled(c, 127) if c == top else jnp.where(lane == 127, rolled(c + 1, 127), rolled(c, 127))
                new = ((cf[0, c, x] * src[c, x, own_rows, :] + cf[1, c, x] * src[c, x + 2, own_rows, :])
                       + (cf[2, c, x] * src[c, x + 1, TOP - 1:end - 1, :] + cf[3, c, x] * src[c, x + 1, TOP + 1:end + 1, :]))
                new = new + (cf[4, c, x] * zm + cf[5, c, x] * zp) + cf[6, c, x] * src[c, x + 1, own_rows, :]
                out.append((c, x, new + sf[x] if c == 0 else new))
        for item in out:
            put(*item)

    def put_first(c, x, new):
        t1[c, x + 1, own_rows, :] = new

    def put_second(c, x, new):
        t_out[x, :, 128 * c:128 * c + 128] = new

    lane_w = iota((nx + 2 * HALO, 128), 1)

    def widen(left, mid, right, f):
        left = pltpu.roll(left, (128 - 32 * f - 24) % 128, axis=1)
        mid = pltpu.roll(mid, (128 + HALO - 32 * f) % 128, axis=1)
        right = pltpu.roll(right, (128 + 40 - 32 * f) % 128, axis=1)
        return jnp.where(lane_w < HALO, left, jnp.where(lane_w < HALO + ny, mid, jnp.where(lane_w < 2 * HALO + ny, right, 0.0)))

    def near_field(z, f):
        return widen(nb[0, z], nb[1, z], nb[2, z], f)

    def shift_all(v):
        n = v.shape[0]
        return [pltpu.roll(v, 1, axis=0), pltpu.roll(v, n - 1, axis=0), pltpu.roll(v, 1, axis=1), pltpu.roll(v, 127, axis=1)]

    def spread_near(z):
        wk[z] = near_field(z, 1)
        wxa[z] = near_field(z, 0)

    def wedge_coef(z):
        k = wk[z]
        under = wk[jnp.maximum(z - 1, 0)] * (z > 0).astype(jnp.float32)
        over = wk[jnp.minimum(z + 1, DEEP - 1)] * (z < DEEP - 1).astype(jnp.float32)
        g = [conductance(k, kn) for kn in shift_all(k) + [under, over]]
        diag = ((g[0] + g[1]) + (g[2] + g[3])) + ((g[4] + g[5]) + near_field(z, 2))
        diag = jnp.where(diag > 0.0, diag, 1.0)
        inverse = 1.0 / diag
        for n in range(6):
            wcf[n, z] = g[n] * inverse
        wcf[6, z] = near_field(z, 3) * inverse
        wd[z] = diag

    def wedge_sweep(n, first=0, last=None):
        decay, gain = coefficients[n]
        src, dst = (wxa, wxb) if n % 2 == 0 else (wxb, wxa)

        def level(z):
            v = src[z]
            near_v = shift_all(v) + [src[jnp.maximum(z - 1, 0) if not isinstance(z, int) else max(z - 1, 0)], src[z + 1]]
            r = (wcf[0, z] * near_v[0] + wcf[1, z] * near_v[1]) + (wcf[2, z] * near_v[2] + wcf[3, z] * near_v[3])
            r = r + (wcf[4, z] * near_v[4] + wcf[5, z] * near_v[5]) + wcf[6, z]
            new = (1.0 + decay - gain) * v + gain * r
            return new if n == 0 else new - decay * dst[z]

        def levels(z, step):
            for k, new in enumerate([level(z + k) for k in range(step)]):
                dst[z + k] = new

        if last is None:
            last = DEEP - 1 - n
        count = last - first
        step = 3 if count % 3 == 0 else 2
        if count > step:
            loop(count - count % step, step, lambda z: levels(first + z, step))
            if count % step:
                levels(last - count % step, count % step)
        else:
            levels(first, count)

    def bands(refs):
        total = None
        for band, ref in enumerate(refs):
            v = ref[...]
            at = iota(v.shape, 1)
            v = jnp.where((at >= 16 * band) & (at < 16 * band + 16), v, 0.0)
            total = v if total is None else total + v
        return total

    def drain():
        recent = [m for n, m in solid_sends if n >= 0]
        for m in [m for m in pending if m not in recent and m not in held_back]:
            m.sent()

    held_back = []

    all_chunks = range(fluid_chunks)
    loaded("e", "q")
    lax.fori_loop(0, nx, turn, 0, unroll=2)
    film = 2.0 * live * rows_of(lambda x: al[0, x + 1, own_rows, :])
    arrived(k_y)
    loop(interior, 2, lambda x: solid_coef(1 + x, 2))
    arrived(k_x)
    solid_coef(0, 1)
    solid_coef(nx - 1, 1)
    solid_sweep(0)
    u_x = [Message(ux.at[:, nx if d == 0 else 1], ux.at[:, 0 if d == 0 else nx + 1], d).start() for d in range(2)]
    t_x = send_planes(t0)

    loaded("uz")
    arrived(a_y + u_y)
    cuts = [interior * n // (30 * COEF_STEP) * COEF_STEP for n in COEF_CUTS]

    def coef_part(n):
        first = 1 + cuts[n]
        loop(cuts[n + 1] - cuts[n], COEF_STEP, lambda x: [fluid_coef(first + x + i) for i in range(COEF_STEP)])

    coef_part(0)
    solid_sweep(1)
    near_msgs = send_near(nb, lambda ref, column, rows: ref.at[column, :, rows, :])
    coef_part(1)
    solid_sweep(2)
    coef_part(2)
    arrived(a_x + u_x)
    fluid_coef(0)
    fluid_coef(nx - 1)

    arrived(t_x + t_y)
    fluid_planes(t0, (0, nx - 1), all_chunks, put_first)
    t_msgs = send_planes(t1)
    loop(interior, FLUID_STEP, lambda x: fluid_planes(t0, [1 + x + i for i in range(FLUID_STEP)], all_chunks, put_first))
    t_msgs += send_rows(t1)
    solid_sweep(3)

    arrived(near_msgs)
    loop(DEEP, 2, lambda z: [spread_near(z), spread_near(z + 1)])

    arrived(t_msgs)
    loop(nx, 4, lambda x: fluid_planes(t1, [x + i for i in range(4)], (0,), put_second))
    gas = rows_of(lambda x: t_out[x, :, 0:128])
    rows_s[...] = product(jnp.concatenate([film, gas], axis=0), select(), ((1,), (1,)))
    row_msgs = [Message(rows_s, rows_r.at[d], d).start() for d in range(4)]

    if fluid_chunks > 1:
        loop(nx, 4, lambda x: fluid_planes(t1, [x + i for i in range(4)], all_chunks[1:], put_second))
    solid_sweep(4)

    solid_sends[:] = [item for item in solid_sends if item[0] >= 0]
    held_back.extend(row_msgs)
    drain()
    arrived(row_msgs)
    came = bands([rows_r.at[d] for d in range(4)])
    film_in = jnp.concatenate([film * self_mask, came[0:8]], axis=1)
    heat_in = film_in * jnp.concatenate([gas, came[8:16]], axis=1)
    sums = None
    for film_piece, heat_piece in zip(pieces(film_in), pieces(heat_in)):
        weighed = jnp.concatenate(
            [jnp.concatenate([hot_y[:, 256 * n:256 * n + 256] * v[n:n + 1, :] for n in range(8)], axis=1)
             for v in (film_piece.astype(jnp.float32), heat_piece.astype(jnp.float32))], axis=0).astype(jnp.bfloat16)
        part = product16(hot_x16[...], weighed, ((1,), (1,)))
        sums = part if sums is None else sums + part
    fb[1, HALO:HALO + nx, :] = jnp.concatenate([sums, jnp.zeros((nx, 64), jnp.float32)], axis=1)
    film_msgs = send_near(fb, lambda ref, column, rows: ref.at[column, rows, :])

    loop(DEEP, 2, lambda z: [wedge_coef(z), wedge_coef(z + 1)])
    solid_sweep(5)

    held_back[:] = film_msgs
    drain()
    arrived(film_msgs)
    wide = [widen(fb[0], fb[1], fb[2], f) for f in range(2)]
    diag = wd[0]
    inverse = 1.0 / (diag + wide[0])
    wcf[6, 0] = (wcf[6, 0] * diag + wide[1]) * inverse
    for n in range(6):
        wcf[n, 0] = wcf[n, 0] * diag * inverse
    for n in range(WEDGE_SPLIT):
        wedge_sweep(n)
    solid_sweep(6)
    for n in range(WEDGE_SPLIT, SWEEPS):
        wedge_sweep(n, 0, SWEEPS - n)
    solved = wxa if SWEEPS % 2 == 0 else wxb

    surface = pltpu.roll(solved[0, HALO:HALO + nx, :], 128 - HALO, axis=1)[:, 0:32]
    picked = product16(jnp.concatenate(pieces(surface), axis=0), hot_y16[...], ((1,), (0,)))
    picked = (picked[0:nx] + picked[nx:2 * nx]) + picked[2 * nx:3 * nx]
    picked = jnp.sum(picked * hot_x[...], axis=0, keepdims=True)
    for n in range(8):
        slots[n:n + 1, :] = picked[:, 256 * n:256 * n + 256]
    wall_s[...] = slots[:, 128:256]
    wall_msgs = [Message(wall_s, wall_r.at[d], d).start() for d in range(4)]

    for n in range(WEDGE_SPLIT, SWEEPS):
        wedge_sweep(n, SWEEPS - n)

    def turn_back(x, _):
        cells = jnp.concatenate([solved[0:HALO, pl.ds(HALO + x, 1), :].reshape(HALO, 128), jnp.zeros((128 - HALO, 128), jnp.float32)], axis=0)
        wz[x] = jnp.transpose(cells)[HALO:HALO + ny]
        return 0
    lax.fori_loop(0, nx, turn_back, 0, unroll=2)

    held_back[:] = wall_msgs
    drain()
    solid_sweep(7)

    arrived(wall_msgs)
    back = bands([wall_r.at[d] for d in (1, 0, 3, 2)])
    rows = (self_mask * slots[:, 0:128] + product(back, select(), ((1,), (0,)))) * live
    rows = jnp.concatenate([jnp.where(lane8 < 16, pltpu.roll(rows, (128 - 16 * n) % 128, axis=1), 0.0) for n in range(8)], axis=0)
    rows = product(rows, compress, ((1,), (1,)))
    for n in range(8):
        wall_out[n:n + 1, :] = jnp.sum(jnp.where(keep, rows[8 * n:8 * n + 8], 0.0), axis=0, keepdims=True)
    for m in list(pending):
        m.sent()


N_MESSAGES = 8 + 12 + 8 + 4 * (SWEEPS - 1) + 4 + 4 + 8 + 4


def store_kernel(t_in, x_in, wall_in, t_out, x_out, wall_out, sems):
    copies = [pltpu.make_async_copy(src, dst, sems.at[n]) for n, (src, dst) in enumerate(
        ((t_in, t_out), (x_in, x_out), (wall_in, wall_out)))]
    for copy in copies:
        copy.start()
    for copy in copies:
        copy.wait()


def on_device(n_blk, n_sub, fluid_temp, velocity, eddy_diff, wall_prev, row_count, owner_table, landing_cell, solid_temp, conductivity, sink, heat_source):
    nx, ny, nz = fluid_temp.shape
    nsz = solid_temp.shape[2]
    f32 = jnp.float32
    any_space = pl.BlockSpec(memory_space=pl.ANY)
    vmem_space = pl.BlockSpec(memory_space=pltpu.VMEM)

    def vmem(*shape):
        return pltpu.VMEM(shape, f32)

    def haloed(depth):
        return vmem(depth // 128, nx + 2, ny + 2 * TOP, 128)

    wide = nx + 2 * HALO
    fluid_new, solid_new, wall_new = pl.pallas_call(
        functools.partial(kernel, n_blk, n_sub),
        out_shape=(
            vmem(nx, ny, nz),
            vmem(nx, ny, nsz),
            vmem(8, 128),
        ),
        in_specs=[pl.BlockSpec(memory_space=pltpu.SMEM)] + [any_space] * 7 + [vmem_space] * 3,
        out_specs=(vmem_space,) * 3,
        scratch_shapes=[
            haloed(nz), haloed(nz),
            vmem(nz // 128, nx + 2, ny, 128), vmem(nz // 128, nx, ny + 2 * TOP, 128), vmem(nz // 128, nx, ny, 128),
            haloed(nz), vmem(7, nz // 128, nx, ny, 128), vmem(nx, ny, 128),
            haloed(nsz), haloed(nsz), haloed(nsz), vmem(nsz // 128, nx, ny, 128), vmem(nsz // 128, nx, ny, 128),
            vmem(7, nsz // 128, nx, ny, 128),
            vmem(3, DEEP, wide, 128), vmem(3, wide, 128),
            vmem(DEEP, wide, 128), vmem(7, DEEP, wide, 128),
            vmem(DEEP, wide, 128), vmem(DEEP, wide, 128), vmem(DEEP, wide, 128), vmem(nx, ny, 128),
            vmem(16, 128), vmem(4, 16, 128), vmem(8, 128), vmem(4, 8, 128),
            vmem(32, 2048), vmem(32, 2048),
            pltpu.VMEM((32, 2048), jnp.bfloat16), pltpu.VMEM((32, 2048), jnp.bfloat16), vmem(8, 256),
            pltpu.SemaphoreType.DMA((9,)),
            pltpu.SemaphoreType.DMA((N_MESSAGES,)),
            pltpu.SemaphoreType.DMA((N_MESSAGES,)),
        ],
        compiler_params=pltpu.CompilerParams(
            collective_id=0, has_side_effects=True, vmem_limit_bytes=60 * 1024 * 1024
        ),
    )(row_count, fluid_temp, velocity, eddy_diff, solid_temp, conductivity, sink, heat_source, wall_prev.reshape(8, 128), owner_table, landing_cell)
    fluid_new, solid_new, wall_new = pl.pallas_call(
        store_kernel,
        out_shape=(
            jax.ShapeDtypeStruct((nx, ny, nz), f32),
            jax.ShapeDtypeStruct((nx, ny, nsz), f32),
            jax.ShapeDtypeStruct((8, 128), f32),
        ),
        in_specs=[vmem_space] * 3,
        out_specs=(any_space,) * 3,
        scratch_shapes=[pltpu.SemaphoreType.DMA((3,))],
    )(*[pltpu.with_memory_space_constraint(v, pltpu.VMEM) for v in (fluid_new, solid_new, wall_new)])
    return fluid_new, solid_new, wall_new.reshape(-1)


def solution(mesh):
    return jax.shard_map(
        functools.partial(on_device, mesh.shape["blk"], mesh.shape["sub"]),
        mesh=mesh,
        in_specs=(
            P("blk", "sub", None),
            P(None, "blk", "sub", None),
            P("blk", "sub", None),
            P(("blk", "sub")),
            P(("blk", "sub")),
            P(("blk", "sub"), None),
            P(("blk", "sub"), None),
            P("blk", "sub", None),
            P("blk", "sub", None),
            P("blk", "sub", None),
            P("blk", "sub", None),
        ),
        out_specs=(P("blk", "sub", None), P("blk", "sub", None), P(("blk", "sub"))),
        check_vma=False,
    )
```

```python
import functools

import jax
import jax.numpy as jnp
from jax import lax
from jax.experimental import pallas as pl
from jax.experimental.pallas import tpu as pltpu
from jax.sharding import PartitionSpec as P

MESH = pl.DeviceIdType.MESH
SWEEPS = 8
HALO = 8
DEEP = 16
TOP = 8
SOLID_STEP = 10
WEDGE_SPLIT = 5
COEF_CUTS = (0, 14, 26, 30)
FLUID_STEP = 5
COEF_STEP = 2
EIG_LOW = 0.02
EIG_HIGH = 2.0
HIGHEST = lax.Precision.HIGHEST
DIRS = ((1, 0), (-1, 0), (0, 1), (0, -1), (1, 1), (1, -1), (-1, 1), (-1, -1))


def cheby_coefficients(count_sweeps):
    center_eig = 0.5 * (EIG_HIGH + EIG_LOW)
    half_width = 0.5 * (EIG_HIGH - EIG_LOW)
    ratio_eig = center_eig / half_width
    damping = 1.0 / ratio_eig
    coefficients = [(0.0, 1.0 / center_eig)]
    for _ in range(1, count_sweeps):
        damping_new = 1.0 / (2.0 * ratio_eig - damping)
        coefficients.append((damping_new * damping, 2.0 * damping_new / half_width))
        damping = damping_new
    return coefficients


def iota(shape, dim):
    return lax.broadcasted_iota(jnp.int32, shape, dim)


def lane_shifts(v):
    lane = iota(v[0].shape, 1)
    low, high = [pltpu.roll(c, 1, axis=1) for c in v], [pltpu.roll(c, 127, axis=1) for c in v]
    below = [low[0]] + [jnp.where(lane == 0, low[c - 1], low[c]) for c in range(1, len(v))]
    above = [jnp.where(lane == 127, high[c + 1], high[c]) for c in range(len(v) - 1)] + [high[-1]]
    return below, above


def face(u, un, a, an):
    total_u, total_a = u + un, a + an
    return total_a + jnp.maximum(total_u, 0.0), total_a - jnp.minimum(total_u, 0.0)


def within(k, kn):
    return 2.0 * k * kn / (k + kn)


def conductance(k, kn):
    total = k + kn
    return 2.0 * k * kn / jnp.where(total > 0.0, total, 1.0)


def kernel(
    n_blk, n_sub,
    count_ref, t_hbm, vel_hbm, a_hbm, x_hbm, k_hbm, e_hbm, q_hbm, wall_ref, owner_ref, land_ref,
    t_out, x_out, wall_out,
    t0, t1, ux, uy, uz, al, cf, sf,
    xa, xb, kc, ec, qc, cs,
    nb, fb, wk, wcf, wxa, wxb, wd, wz,
    rows_s, rows_r, wall_s, wall_r, hot_x, hot_y, hot_x16, hot_y16, slots,
    load_sem, send_sem, recv_sem,
):
    b, s = lax.axis_index("blk"), lax.axis_index("sub")
    nx, ny, _ = t_hbm.shape
    fluid_chunks, solid_chunks = t0.shape[0], xa.shape[0]
    end = TOP + ny
    own_rows, own_planes = slice(TOP, end), slice(1, 1 + nx)
    coefficients = cheby_coefficients(SWEEPS)

    def inside(db, ds):
        ok = None
        for delta, at, count in ((db, b, n_blk), (ds, s, n_sub)):
            if delta:
                this = (at < count - 1) if delta > 0 else (at > 0)
                ok = this if ok is None else ok & this
        return ok

    counter = [0]
    pending = []

    class Message:
        def __init__(self, src, dst, d):
            db, ds = DIRS[d]
            self.n = counter[0]
            counter[0] += 1
            self.make = lambda: pltpu.make_async_remote_copy(
                src_ref=src, dst_ref=dst, send_sem=send_sem.at[self.n], recv_sem=recv_sem.at[self.n],
                device_id=(b + db, s + ds), device_id_type=MESH)
            self.goes, self.comes = inside(db, ds), inside(-db, -ds)

        def start(self):
            @pl.when(self.goes)
            def _():
                self.make().start()
            pending.append(self)
            return self

        def sent(self):
            @pl.when(self.goes)
            def _():
                self.make().wait_send()
            pending.remove(self)

        def arrived(self):
            @pl.when(self.comes)
            def _():
                self.make().wait_recv()

    def send_planes(ref):
        return [Message(ref.at[:, nx if d == 0 else 1, own_rows, :], ref.at[:, 0 if d == 0 else nx + 1, own_rows, :], d).start()
                for d in range(2)]

    def send_rows(ref):
        return [Message(ref.at[:, own_planes, end - 1:end, :], ref.at[:, own_planes, TOP - 1:TOP, :], 2).start(),
                Message(ref.at[:, own_planes, TOP:TOP + 1, :], ref.at[:, own_planes, end:end + 1, :], 3).start()]

    def arrived(messages):
        for m in messages:
            m.arrived()

    loads = {}
    for name, src, dst in (
        ("k", k_hbm, kc), ("x", x_hbm, xa), ("a", a_hbm, al), ("ux", vel_hbm.at[0], ux), ("t", t_hbm, t0), ("uy", vel_hbm.at[1], uy),
        ("e", e_hbm, ec), ("q", q_hbm, qc), ("uz", vel_hbm.at[2], uz),
    ):
        planes = own_planes if dst.shape[1] > nx else slice(0, nx)
        rows = own_rows if dst.shape[2] > ny else slice(0, ny)
        n = len(loads)
        for c in range(dst.shape[0]):
            pltpu.make_async_copy(src.at[:, :, 128 * c:128 * c + 128], dst.at[c, planes, rows, :], load_sem.at[n]).start()
        whole = dst.at[:, planes, rows, :]
        loads[name] = pltpu.make_async_copy(whole, whole, load_sem.at[n])

    def loaded(*names):
        for name in names:
            loads[name].wait()

    barrier = pltpu.get_barrier_semaphore()
    for db, ds in DIRS:
        @pl.when(inside(db, ds))
        def _(db=db, ds=ds):
            pl.semaphore_signal(barrier, inc=1, device_id=(b + db, s + ds), device_id_type=MESH)

    def clear(ref, *where):
        ref[where] = jnp.zeros(ref.at[where].shape, jnp.float32)

    for d in range(2):
        @pl.when(jnp.logical_not(inside(-DIRS[d][0], 0)))
        def _(d=d):
            for ref in (t0, t1, al, ux, xa, xb, kc):
                rows = own_rows if ref.shape[2] > ny else slice(0, ny)
                for c in range(ref.shape[0]):
                    clear(ref, c, 0 if d == 0 else nx + 1, rows, slice(None))

        @pl.when(jnp.logical_not(inside(0, -DIRS[2 + d][1])))
        def _(d=d):
            row = TOP - 1 if d == 0 else end

            def body(x, _):
                for ref in (t0, t1, al, uy, xa, xb, kc):
                    for c in range(ref.shape[0]):
                        clear(ref, c, x + (1 if ref.shape[1] > nx else 0), slice(row, row + 1), slice(None))
                return 0
            lax.fori_loop(0, nx, body, 0)
    for d in range(4):
        @pl.when(jnp.logical_not(inside(-DIRS[d][0], -DIRS[d][1])))
        def _(d=d):
            rows_r[d] = jnp.zeros(rows_r.shape[1:], jnp.float32)
            wall_r[d] = jnp.zeros(wall_r.shape[1:], jnp.float32)

    def near_slot(d):
        db, ds = DIRS[d]
        column = {1: 0, 0: 1, -1: 2}[ds]
        if db == 0:
            return column, slice(HALO, HALO + nx), slice(HALO, HALO + nx)
        if db > 0:
            return column, slice(nx, HALO + nx), slice(0, HALO)
        return column, slice(HALO, 2 * HALO), slice(HALO + nx, 2 * HALO + nx)

    for d in range(8):
        @pl.when(jnp.logical_not(inside(-DIRS[d][0], -DIRS[d][1])))
        def _(d=d):
            column, _, rows = near_slot(d)
            height = rows.stop - rows.start
            nb[column, :, rows, :] = jnp.zeros((DEEP, height, 128), jnp.float32)
            fb[column, rows, :] = jnp.zeros((height, 128), jnp.float32)

    def product(x, y, dims):
        return lax.dot_general(x, y, (dims, ((), ())), precision=HIGHEST, preferred_element_type=jnp.float32)

    def pieces(v):
        out = []
        for _ in range(3):
            out.append(v.astype(jnp.bfloat16))
            v = v - out[-1].astype(jnp.float32)
        return out

    def product16(x, y, dims):
        return lax.dot_general(x, y, (dims, ((), ())), preferred_element_type=jnp.float32)

    def picked_by(v, hot, dims):
        n = v.shape[0]
        out = product16(jnp.concatenate(pieces(v), axis=0), hot.astype(jnp.bfloat16), dims)
        return (out[0:n] + out[n:2 * n]) + out[2 * n:3 * n]

    lane, lane8, sub8 = iota((ny, 128), 1), iota((8, 128), 1), iota((8, 128), 0)
    keep = (lane8 & 7) == sub8
    compress = jnp.where((iota((128, 128), 0) >> 3) == iota((128, 128), 1), 1.0, 0.0)
    flat = [wall_ref[n:n + 1, :] for n in range(8)] + [land_ref[0:1, 128 * n:128 * n + 128].astype(jnp.float32) for n in range(12)]
    packed = product(jnp.concatenate([jnp.where(keep, jnp.broadcast_to(v, (8, 128)), 0.0) for v in flat], axis=0), compress, ((1,), (0,)))

    def gather_rows(first, count):
        total = packed[8 * first:8 * first + 8]
        for n in range(1, count):
            total = total + pltpu.roll(packed[8 * (first + n):8 * (first + n) + 8], 16 * n, axis=1)
        return total

    wall = gather_rows(0, 8)
    land = jnp.concatenate([gather_rows(8, 8), jnp.where(lane8 < 64, gather_rows(16, 4), -1.0)], axis=1).astype(jnp.int32)
    live = jnp.where(lane8 * 8 + sub8 < count_ref[0], 1.0, 0.0)
    owner = jnp.broadcast_to(owner_ref[...], (8, 128))
    self_mask = jnp.where(owner == 0, 1.0, 0.0)
    match = jnp.where((owner == sub8 + 1) & (sub8 < 4), 1.0, 0.0)
    before = jnp.where(iota((128, 128), 0) < iota((128, 128), 1), 1.0, 0.0)
    rank = product(match, before, ((1,), (0,)))
    place = jnp.sum(match * (rank + (sub8 * 16 + 1).astype(jnp.float32)), axis=0, keepdims=True) - 1.0
    row32 = iota((32, 256), 0)
    for n in range(8):
        cell = land[n:n + 1, :]
        at = slice(256 * n, 256 * n + 256)
        hot_x[:, at] = jnp.where((cell >> 5) == row32, 1.0, 0.0)
        hot_y[:, at] = jnp.where(((cell & 31) == row32) & (cell >= 0), 1.0, 0.0)
        hot_x16[:, at] = hot_x[:, at].astype(jnp.bfloat16)
        hot_y16[:, at] = hot_y[:, at].astype(jnp.bfloat16)

    def select():
        return jnp.where(iota((128, 128), 0).astype(jnp.float32) == place, 1.0, 0.0)

    near = (b > 0).astype(jnp.int32) + (b < n_blk - 1).astype(jnp.int32)
    side = (s > 0).astype(jnp.int32) + (s < n_sub - 1).astype(jnp.int32)
    pl.semaphore_wait(barrier, near + side + near * side)

    loaded("k", "x")
    k_x, x_x = send_planes(kc), send_planes(xa)
    k_y, x_y = send_rows(kc), send_rows(xa)
    loaded("a", "ux", "t")
    a_x = send_planes(al)
    loaded("uy")
    a_y, t_y = send_rows(al), send_rows(t0)
    u_y = [Message(uy.at[:, :, end - 1:end, :], uy.at[:, :, TOP - 1:TOP, :], 2).start(),
           Message(uy.at[:, :, TOP:TOP + 1, :], uy.at[:, :, end:end + 1, :], 3).start()]

    def turn(x, _):
        tile = jnp.concatenate([xa[0, x + 1, own_rows, :], kc[0, x + 1, own_rows, :], ec[0, x], qc[0, x]], axis=0)
        nb[1, :, pl.ds(HALO + x, 1), :] = jnp.transpose(tile)[0:DEEP].reshape(DEEP, 1, 128)
        return 0

    def send_near(column_ref, part):
        messages = []
        for d in range(8):
            column, out_rows, rows = near_slot(d)
            messages.append(Message(part(column_ref, 1, out_rows), part(column_ref, column, rows), d).start())
        return messages

    def solid_coef(x, count):
        k = [[kc[c, x + i, own_rows, :] for c in range(solid_chunks)] for i in range(count + 2)]
        out = []
        for i in range(count):
            here, under, over = k[i + 1], k[i], k[i + 2]
            zm, _ = lane_shifts(here)
            gz = [within(here[c], zm[c]) for c in range(solid_chunks)]
            gz[0] = jnp.where(lane == 0, 0.0, gz[0])
            _, gz_up = lane_shifts(gz)
            gz_up[-1] = jnp.where(lane == 127, 0.0, gz_up[-1])
            for c in range(solid_chunks):
                g = [within(here[c], under[c]), within(here[c], over[c]),
                     within(here[c], kc[c, x + i + 1, TOP - 1:end - 1, :]), within(here[c], kc[c, x + i + 1, TOP + 1:end + 1, :]),
                     gz[c], gz_up[c]]
                inverse = 1.0 / (((g[0] + g[1]) + (g[2] + g[3])) + ((g[4] + g[5]) + ec[c, x + i]))
                out.append((c, x + i, [v * inverse for v in g] + [qc[c, x + i] * inverse]))
        for c, at, values in out:
            for n in range(7):
                cs[n, c, at] = values[n]

    def solid_planes(n, src, dst, runs):
        decay, gain = coefficients[n]
        out = []
        for x, count in runs:
            v = [[src[c, x + i, own_rows, :] for c in range(solid_chunks)] for i in range(count + 2)]
            for i in range(count):
                zm, zp = lane_shifts(v[i + 1])
                for c in range(solid_chunks):
                    at = x + i
                    r = ((cs[0, c, at] * v[i][c] + cs[1, c, at] * v[i + 2][c])
                         + (cs[2, c, at] * src[c, at + 1, TOP - 1:end - 1, :] + cs[3, c, at] * src[c, at + 1, TOP + 1:end + 1, :]))
                    r = r + (cs[4, c, at] * zm[c] + cs[5, c, at] * zp[c]) + cs[6, c, at]
                    new = (1.0 + decay - gain) * v[i + 1][c] + gain * r
                    if n > 0:
                        new = new - decay * dst[c, at + 1, own_rows, :]
                    if n == SWEEPS - 1 and c == 0:
                        new = jnp.where(lane < HALO, wz[at], new)
                    out.append((c, at, new))
        for c, at, new in out:
            if n == SWEEPS - 1:
                x_out[at, :, 128 * c:128 * c + 128] = new
            else:
                dst[c, at + 1, own_rows, :] = new

    solid_sends = [(-1, m) for m in x_x + x_y]
    solid_waits = [x_x + x_y]
    interior = nx - 2

    def loop(count, step, work):
        def body(i, _):
            work(i * step)
            return 0
        lax.fori_loop(0, count // step, body, 0)

    def solid_sweep(n):
        src, dst = (xa, xb) if n % 2 == 0 else (xb, xa)
        arrived(solid_waits.pop())
        for m in list(solid_sends):
            if m[0] <= n - 2:
                m[1].sent()
                solid_sends.remove(m)
        solid_planes(n, src, dst, [(0, 1), (nx - 1, 1)])
        msgs = send_planes(dst) if n < SWEEPS - 1 else []
        loop(interior, SOLID_STEP, lambda x: solid_planes(n, src, dst, [(1 + x, SOLID_STEP)]))
        if n < SWEEPS - 1:
            msgs += send_rows(dst)
        solid_sends.extend((n, m) for m in msgs)
        solid_waits.append(msgs)

    mirror = 1.0 - 2.0 * live
    source = 2.0 * live * wall

    def columns(v, x):
        return jnp.concatenate([pltpu.roll(v, lax.rem(128 - (x * 4 + j), 128), axis=1) for j in range(4)], axis=0)

    def rows_of(plane):
        def body(i, parts):
            parts = list(parts)
            for k in range(4):
                v = plane(4 * i + k)
                for j in range(4):
                    parts[j] = jnp.where(lane8 == (4 * i + k) * 4 + j, jnp.broadcast_to(v[8 * j:8 * j + 8, 0:1], (8, 128)), parts[j])
            return tuple(parts)
        parts = lax.fori_loop(0, nx // 4, body, (jnp.zeros((8, 128), jnp.float32),) * 4)
        return (parts[0] + parts[1]) + (parts[2] + parts[3])

    top = fluid_chunks - 1

    def fluid_coef(x):
        a = [al[c, x + 1, own_rows, :] for c in range(fluid_chunks)]
        u = [uz[c, x] for c in range(fluid_chunks)]
        am, _ = lane_shifts(a)
        um, _ = lane_shifts(u)
        am[0] = jnp.where(lane == 0, a[0], am[0])
        um[0] = jnp.where(lane == 0, -u[0], um[0])
        z = [face(u[c], um[c], a[c], am[c]) for c in range(fluid_chunks)]
        _, pz = lane_shifts([v[0] for v in z])
        _, qz = lane_shifts([v[1] for v in z])
        last = face(u[top], u[top], a[top], a[top])
        pz[top] = jnp.where(lane == 127, last[0], pz[top])
        qz[top] = jnp.where(lane == 127, last[1], qz[top])
        for c in range(fluid_chunks):
            v = ux[c, x + 1]
            p_xm, q_xm = face(v, ux[c, x], a[c], al[c, x, own_rows, :])
            p_xp, q_xp = face(v, ux[c, x + 2], a[c], al[c, x + 2, own_rows, :])
            v = uy[c, x, own_rows, :]
            p_ym, q_ym = face(v, uy[c, x, TOP - 1:end - 1, :], a[c], al[c, x + 1, TOP - 1:end - 1, :])
            p_yp, q_yp = face(v, uy[c, x, TOP + 1:end + 1, :], a[c], al[c, x + 1, TOP + 1:end + 1, :])
            p_zm, q_zm = z[c]
            away = ((q_xm + p_xp) + (q_ym + p_yp)) + (q_zm + pz[c])
            toward = ((p_xm + q_xp) + (p_ym + q_yp)) + (p_zm + qz[c])
            scale = 1.6 / (away + toward)
            cf[0, c, x] = p_xm * scale
            cf[1, c, x] = q_xp * scale
            cf[2, c, x] = p_ym * scale
            cf[3, c, x] = q_yp * scale
            below, above, centre = p_zm * scale, qz[c] * scale, 1.0 - away * scale
            if c == 0:
                first = lane == 0
                at_wall = jnp.where(first, below, 0.0)
                sf[x] = at_wall * columns(source, x)
                centre = centre + at_wall * columns(mirror, x)
                below = jnp.where(first, 0.0, below)
            if c == top:
                above = jnp.where(lane == 127, 0.0, above)
            cf[4, c, x] = below
            cf[5, c, x] = above
            cf[6, c, x] = centre

    def fluid_planes(src, xs, chunks, put):
        out = []
        for x in xs:
            held = {}

            def rolled(c, shift, held=held, x=x):
                if (c, shift) not in held:
                    held[c, shift] = pltpu.roll(src[c, x + 1, own_rows, :], shift, axis=1)
                return held[c, shift]

            for c in chunks:
                zm = rolled(c, 1) if c == 0 else jnp.where(lane == 0, rolled(c - 1, 1), rolled(c, 1))
                zp = rolled(c, 127) if c == top else jnp.where(lane == 127, rolled(c + 1, 127), rolled(c, 127))
                new = ((cf[0, c, x] * src[c, x, own_rows, :] + cf[1, c, x] * src[c, x + 2, own_rows, :])
                       + (cf[2, c, x] * src[c, x + 1, TOP - 1:end - 1, :] + cf[3, c, x] * src[c, x + 1, TOP + 1:end + 1, :]))
                new = new + (cf[4, c, x] * zm + cf[5, c, x] * zp) + cf[6, c, x] * src[c, x + 1, own_rows, :]
                out.append((c, x, new + sf[x] if c == 0 else new))
        for item in out:
            put(*item)

    def put_first(c, x, new):
        t1[c, x + 1, own_rows, :] = new

    def put_second(c, x, new):
        t_out[x, :, 128 * c:128 * c + 128] = new

    lane_w = iota((nx + 2 * HALO, 128), 1)

    def widen(left, mid, right, f):
        left = pltpu.roll(left, (128 - 32 * f - 24) % 128, axis=1)
        mid = pltpu.roll(mid, (128 + HALO - 32 * f) % 128, axis=1)
        right = pltpu.roll(right, (128 + 40 - 32 * f) % 128, axis=1)
        return jnp.where(lane_w < HALO, left, jnp.where(lane_w < HALO + ny, mid, jnp.where(lane_w < 2 * HALO + ny, right, 0.0)))

    def near_field(z, f):
        return widen(nb[0, z], nb[1, z], nb[2, z], f)

    def shift_all(v):
        n = v.shape[0]
        return [pltpu.roll(v, 1, axis=0), pltpu.roll(v, n - 1, axis=0), pltpu.roll(v, 1, axis=1), pltpu.roll(v, 127, axis=1)]

    def spread_near(z):
        wk[z] = near_field(z, 1)
        wxa[z] = near_field(z, 0)

    def wedge_coef(z):
        k = wk[z]
        under = wk[jnp.maximum(z - 1, 0)] * (z > 0).astype(jnp.float32)
        over = wk[jnp.minimum(z + 1, DEEP - 1)] * (z < DEEP - 1).astype(jnp.float32)
        g = [conductance(k, kn) for kn in shift_all(k) + [under, over]]
        diag = ((g[0] + g[1]) + (g[2] + g[3])) + ((g[4] + g[5]) + near_field(z, 2))
        diag = jnp.where(diag > 0.0, diag, 1.0)
        inverse = 1.0 / diag
        for n in range(6):
            wcf[n, z] = g[n] * inverse
        wcf[6, z] = near_field(z, 3) * inverse
        wd[z] = diag

    def wedge_sweep(n, first=0, last=None):
        decay, gain = coefficients[n]
        src, dst = (wxa, wxb) if n % 2 == 0 else (wxb, wxa)

        def level(z):
            v = src[z]
            near_v = shift_all(v) + [src[jnp.maximum(z - 1, 0) if not isinstance(z, int) else max(z - 1, 0)], src[z + 1]]
            r = (wcf[0, z] * near_v[0] + wcf[1, z] * near_v[1]) + (wcf[2, z] * near_v[2] + wcf[3, z] * near_v[3])
            r = r + (wcf[4, z] * near_v[4] + wcf[5, z] * near_v[5]) + wcf[6, z]
            new = (1.0 + decay - gain) * v + gain * r
            return new if n == 0 else new - decay * dst[z]

        def levels(z, step):
            for k, new in enumerate([level(z + k) for k in range(step)]):
                dst[z + k] = new

        if last is None:
            last = DEEP - 1 - n
        count = last - first
        step = 3 if count % 3 == 0 else 2
        if count > step:
            loop(count - count % step, step, lambda z: levels(first + z, step))
            if count % step:
                levels(last - count % step, count % step)
        else:
            levels(first, count)

    def bands(refs):
        total = None
        for band, ref in enumerate(refs):
            v = ref[...]
            at = iota(v.shape, 1)
            v = jnp.where((at >= 16 * band) & (at < 16 * band + 16), v, 0.0)
            total = v if total is None else total + v
        return total

    def drain():
        recent = [m for n, m in solid_sends if n >= 0]
        for m in [m for m in pending if m not in recent and m not in held_back]:
            m.sent()

    held_back = []

    all_chunks = range(fluid_chunks)
    loaded("e", "q")
    lax.fori_loop(0, nx, turn, 0, unroll=2)
    film = 2.0 * live * rows_of(lambda x: al[0, x + 1, own_rows, :])
    arrived(k_y)
    loop(interior, 2, lambda x: solid_coef(1 + x, 2))
    arrived(k_x)
    solid_coef(0, 1)
    solid_coef(nx - 1, 1)
    solid_sweep(0)
    u_x = [Message(ux.at[:, nx if d == 0 else 1], ux.at[:, 0 if d == 0 else nx + 1], d).start() for d in range(2)]
    t_x = send_planes(t0)

    loaded("uz")
    arrived(a_y + u_y)
    cuts = [interior * n // (30 * COEF_STEP) * COEF_STEP for n in COEF_CUTS]

    def coef_part(n):
        first = 1 + cuts[n]
        loop(cuts[n + 1] - cuts[n], COEF_STEP, lambda x: [fluid_coef(first + x + i) for i in range(COEF_STEP)])

    coef_part(0)
    solid_sweep(1)
    near_msgs = send_near(nb, lambda ref, column, rows: ref.at[column, :, rows, :])
    coef_part(1)
    solid_sweep(2)
    coef_part(2)
    arrived(a_x + u_x)
    fluid_coef(0)
    fluid_coef(nx - 1)

    arrived(t_x + t_y)
    fluid_planes(t0, (0, nx - 1), all_chunks, put_first)
    t_msgs = send_planes(t1)
    loop(interior, FLUID_STEP, lambda x: fluid_planes(t0, [1 + x + i for i in range(FLUID_STEP)], all_chunks, put_first))
    t_msgs += send_rows(t1)
    solid_sweep(3)

    arrived(near_msgs)
    loop(DEEP, 2, lambda z: [spread_near(z), spread_near(z + 1)])

    arrived(t_msgs)
    loop(nx, 4, lambda x: fluid_planes(t1, [x + i for i in range(4)], (0,), put_second))
    gas = rows_of(lambda x: t_out[x, :, 0:128])
    rows_s[...] = picked_by(jnp.concatenate([film, gas], axis=0), select(), ((1,), (1,)))
    row_msgs = [Message(rows_s, rows_r.at[d], d).start() for d in range(4)]

    if fluid_chunks > 1:
        loop(nx, 4, lambda x: fluid_planes(t1, [x + i for i in range(4)], all_chunks[1:], put_second))
    solid_sweep(4)

    solid_sends[:] = [item for item in solid_sends if item[0] >= 0]
    held_back.extend(row_msgs)
    drain()
    arrived(row_msgs)
    came = bands([rows_r.at[d] for d in range(4)])
    film_in = jnp.concatenate([film * self_mask, came[0:8]], axis=1)
    heat_in = film_in * jnp.concatenate([gas, came[8:16]], axis=1)
    sums = None
    for film_piece, heat_piece in zip(pieces(film_in), pieces(heat_in)):
        weighed = jnp.concatenate(
            [jnp.concatenate([hot_y[:, 256 * n:256 * n + 256] * v[n:n + 1, :] for n in range(8)], axis=1)
             for v in (film_piece.astype(jnp.float32), heat_piece.astype(jnp.float32))], axis=0).astype(jnp.bfloat16)
        part = product16(hot_x16[...], weighed, ((1,), (1,)))
        sums = part if sums is None else sums + part
    fb[1, HALO:HALO + nx, :] = jnp.concatenate([sums, jnp.zeros((nx, 64), jnp.float32)], axis=1)
    film_msgs = send_near(fb, lambda ref, column, rows: ref.at[column, rows, :])

    loop(DEEP, 2, lambda z: [wedge_coef(z), wedge_coef(z + 1)])
    solid_sweep(5)

    held_back[:] = film_msgs
    drain()
    arrived(film_msgs)
    wide = [widen(fb[0], fb[1], fb[2], f) for f in range(2)]
    diag = wd[0]
    inverse = 1.0 / (diag + wide[0])
    wcf[6, 0] = (wcf[6, 0] * diag + wide[1]) * inverse
    for n in range(6):
        wcf[n, 0] = wcf[n, 0] * diag * inverse
    for n in range(WEDGE_SPLIT):
        wedge_sweep(n)
    solid_sweep(6)
    for n in range(WEDGE_SPLIT, SWEEPS):
        wedge_sweep(n, 0, SWEEPS - n)
    solved = wxa if SWEEPS % 2 == 0 else wxb

    surface = pltpu.roll(solved[0, HALO:HALO + nx, :], 128 - HALO, axis=1)[:, 0:32]
    picked = product16(jnp.concatenate(pieces(surface), axis=0), hot_y16[...], ((1,), (0,)))
    picked = (picked[0:nx] + picked[nx:2 * nx]) + picked[2 * nx:3 * nx]
    picked = jnp.sum(picked * hot_x[...], axis=0, keepdims=True)
    for n in range(8):
        slots[n:n + 1, :] = picked[:, 256 * n:256 * n + 256]
    wall_s[...] = slots[:, 128:256]
    wall_msgs = [Message(wall_s, wall_r.at[d], d).start() for d in range(4)]

    for n in range(WEDGE_SPLIT, SWEEPS):
        wedge_sweep(n, SWEEPS - n)

    def turn_back(x, _):
        cells = jnp.concatenate([solved[0:HALO, pl.ds(HALO + x, 1), :].reshape(HALO, 128), jnp.zeros((128 - HALO, 128), jnp.float32)], axis=0)
        wz[x] = jnp.transpose(cells)[HALO:HALO + ny]
        return 0
    lax.fori_loop(0, nx, turn_back, 0, unroll=2)

    held_back[:] = wall_msgs
    drain()
    solid_sweep(7)

    arrived(wall_msgs)
    back = bands([wall_r.at[d] for d in (1, 0, 3, 2)])
    rows = (self_mask * slots[:, 0:128] + picked_by(back, select(), ((1,), (0,)))) * live
    rows = jnp.concatenate([jnp.where(lane8 < 16, pltpu.roll(rows, (128 - 16 * n) % 128, axis=1), 0.0) for n in range(8)], axis=0)
    rows = picked_by(rows, compress, ((1,), (1,)))
    for n in range(8):
        wall_out[n:n + 1, :] = jnp.sum(jnp.where(keep, rows[8 * n:8 * n + 8], 0.0), axis=0, keepdims=True)
    for m in list(pending):
        m.sent()


N_MESSAGES = 8 + 12 + 8 + 4 * (SWEEPS - 1) + 4 + 4 + 8 + 4


def store_kernel(t_in, x_in, wall_in, t_out, x_out, wall_out, sems):
    copies = [pltpu.make_async_copy(src, dst, sems.at[n]) for n, (src, dst) in enumerate(
        ((t_in, t_out), (x_in, x_out), (wall_in, wall_out)))]
    for copy in copies:
        copy.start()
    for copy in copies:
        copy.wait()


def on_device(n_blk, n_sub, fluid_temp, velocity, eddy_diff, wall_prev, row_count, owner_table, landing_cell, solid_temp, conductivity, sink, heat_source):
    nx, ny, nz = fluid_temp.shape
    nsz = solid_temp.shape[2]
    f32 = jnp.float32
    any_space = pl.BlockSpec(memory_space=pl.ANY)
    vmem_space = pl.BlockSpec(memory_space=pltpu.VMEM)

    def vmem(*shape):
        return pltpu.VMEM(shape, f32)

    def haloed(depth):
        return vmem(depth // 128, nx + 2, ny + 2 * TOP, 128)

    wide = nx + 2 * HALO
    fluid_new, solid_new, wall_new = pl.pallas_call(
        functools.partial(kernel, n_blk, n_sub),
        out_shape=(
            vmem(nx, ny, nz),
            vmem(nx, ny, nsz),
            vmem(8, 128),
        ),
        in_specs=[pl.BlockSpec(memory_space=pltpu.SMEM)] + [any_space] * 7 + [vmem_space] * 3,
        out_specs=(vmem_space,) * 3,
        scratch_shapes=[
            haloed(nz), haloed(nz),
            vmem(nz // 128, nx + 2, ny, 128), vmem(nz // 128, nx, ny + 2 * TOP, 128), vmem(nz // 128, nx, ny, 128),
            haloed(nz), vmem(7, nz // 128, nx, ny, 128), vmem(nx, ny, 128),
            haloed(nsz), haloed(nsz), haloed(nsz), vmem(nsz // 128, nx, ny, 128), vmem(nsz // 128, nx, ny, 128),
            vmem(7, nsz // 128, nx, ny, 128),
            vmem(3, DEEP, wide, 128), vmem(3, wide, 128),
            vmem(DEEP, wide, 128), vmem(7, DEEP, wide, 128),
            vmem(DEEP, wide, 128), vmem(DEEP, wide, 128), vmem(DEEP, wide, 128), vmem(nx, ny, 128),
            vmem(16, 128), vmem(4, 16, 128), vmem(8, 128), vmem(4, 8, 128),
            vmem(32, 2048), vmem(32, 2048),
            pltpu.VMEM((32, 2048), jnp.bfloat16), pltpu.VMEM((32, 2048), jnp.bfloat16), vmem(8, 256),
            pltpu.SemaphoreType.DMA((9,)),
            pltpu.SemaphoreType.DMA((N_MESSAGES,)),
            pltpu.SemaphoreType.DMA((N_MESSAGES,)),
        ],
        compiler_params=pltpu.CompilerParams(
            collective_id=0, has_side_effects=True, vmem_limit_bytes=60 * 1024 * 1024
        ),
    )(row_count, fluid_temp, velocity, eddy_diff, solid_temp, conductivity, sink, heat_source, wall_prev.reshape(8, 128), owner_table, landing_cell)
    fluid_new, solid_new, wall_new = pl.pallas_call(
        store_kernel,
        out_shape=(
            jax.ShapeDtypeStruct((nx, ny, nz), f32),
            jax.ShapeDtypeStruct((nx, ny, nsz), f32),
            jax.ShapeDtypeStruct((8, 128), f32),
        ),
        in_specs=[vmem_space] * 3,
        out_specs=(any_space,) * 3,
        scratch_shapes=[pltpu.SemaphoreType.DMA((3,))],
    )(*[pltpu.with_memory_space_constraint(v, pltpu.VMEM) for v in (fluid_new, solid_new, wall_new)])
    return fluid_new, solid_new, wall_new.reshape(-1)


def solution(mesh):
    return jax.shard_map(
        functools.partial(on_device, mesh.shape["blk"], mesh.shape["sub"]),
        mesh=mesh,
        in_specs=(
            P("blk", "sub", None),
            P(None, "blk", "sub", None),
            P("blk", "sub", None),
            P(("blk", "sub")),
            P(("blk", "sub")),
            P(("blk", "sub"), None),
            P(("blk", "sub"), None),
            P("blk", "sub", None),
            P("blk", "sub", None),
            P("blk", "sub", None),
            P("blk", "sub", None),
        ),
        out_specs=(P("blk", "sub", None), P("blk", "sub", None), P(("blk", "sub"))),
        check_vma=False,
    )
```
